128 devices in a mesh: dp: 8 (over z, core), expert: 16 (over y, x).
Axes of the slice: x: 4, y: 4, z: 4, core: 2. Of those that a mesh axis runs over, the one named last changes fastest.
Arguments:
- tokens: bfloat16 [16384, 4096], P(('dp', 'expert')), may hold values from -24 to 24
- cotangent: bfloat16 [16384, 4096], P(('dp', 'expert')), may hold values from -6 to 6
- expert_ids: int32 [16384, 8], P(('dp', 'expert')), may hold values from 0 to 15, all different within a row; in each aligned block of 128 rows (0 to 127, 128 to 255, ...) at most 72 rows name the same one
- route_weight: float32 [16384, 8], P(('dp', 'expert')), may hold values from 0.02 to 0.5
- up_weight: bfloat16 [16, 4096, 768], P('expert'), may hold values from -0.09375 to 0.09375
- down_weight: bfloat16 [16, 768, 4096], P('expert'), may hold values from -0.21875 to 0.21875
Outputs:
- token_grad: bfloat16 [16384, 4096], P(('dp', 'expert'))
- up_grad: float32 [16, 4096, 768], P('expert', 'dp')
- down_grad: float32 [16, 768, 4096], P('expert', 'dp')
The draws below stay inside these ranges and needn't reach their ends.
Inputs may be any that keep to these rules, and one draw needn't show every extreme that they name: `expert_ids`: each row names 8 different experts. Among the 128 tokens of one device (aligned blocks) no expert is named more than 72 times, a bound that some block reaches.
All inputs are finite; a program needn't handle non-finite values.
Results may differ from the reference program's by a relative error of at most 0.017.
Values may be sent and summed in bfloat16 or wider, within the bound.
No kernel may reach another device: no remote copies, remote signals or barrier semaphores. Data moves between devices by JAX's collectives and lax.ppermute only.
A program may use at most 192 MiB of HBM per device.

```python
import math
import jax
import jax.numpy as jnp
import numpy as np
from jax import lax

D = 4096
H = 768
TOP = 8
TOK_DEV = 128
EXPERTS = 16
CAP = 72
TOKENS = 16384
N_DP = 8
N_EXPERT = 16


def strengthened(values, own_key, source, target, blocks, factor):
    def block_of(dim):
        return (jnp.arange(values.shape[dim]) // (values.shape[dim] // blocks)).reshape((-1,) + (1,) * (values.ndim - 1 - dim))

    near = jax.random.permutation(own_key, blocks)[block_of(target)]
    other_side = (block_of(target) + blocks // 2) % blocks
    return jnp.where((block_of(source) == near) | (block_of(source) == other_side), factor * values, values)


def block_scale(rng, dims, split, least, largest):
    def one(position, blocks):
        steps = jax.random.uniform(jax.random.fold_in(jax.random.fold_in(rng, 6), position), (blocks,), jnp.float32, least / len(split), largest / len(split))
        return jnp.repeat(jnp.exp(steps), dims[position] // blocks).reshape((-1,) + (1,) * (len(dims) - position - 1))

    level = one(*split[0])
    for cut in split[1:]:
        level = level * one(*cut)
    return level


def shared_out(stream_key, own, number, rows, count, top, bound, skew):
    order = jax.random.permutation(stream_key, count)
    heavy_load, common = shares(count, rows * top, bound, skew, True), shares(count, rows * top, bound, skew, False)
    places = jnp.arange(count)

    def named(lengths, turn):
        used = int((lengths > 0).sum())
        fixed = max(1, used // 4)
        shifted = fixed + (places - fixed + turn * (used - fixed)) % max(1, count - fixed)
        return jnp.zeros((count,), jnp.int32).at[order[jnp.where(places < fixed, places, shifted)]].set(jnp.asarray(lengths, jnp.int32))

    lengths = jnp.where(number % 4 == 0, named(heavy_load, number // 4), named(common, number - number // 4 - 1))
    mixed = jax.random.permutation(jax.random.fold_in(own, 3), count)
    giver, taker = mixed[0:count // 2 * 2:2], mixed[1:count // 2 * 2:2]
    slack = jnp.minimum(lengths[giver] - 1, bound - lengths[taker]) // 2
    slack = jnp.where((giver == order[0]) | (taker == order[0]) | (lengths[taker] == 0), 0, jnp.maximum(slack, 0))
    shifted = jax.random.randint(jax.random.fold_in(own, 4), (count // 2,), 0, 1 << 20) % (slack + 1)
    lengths = lengths.at[giver].add(-shifted).at[taker].add(shifted)
    labels = jnp.searchsorted(jnp.cumsum(lengths), jnp.arange(rows * top), side="right").astype(jnp.int32)
    table = labels.reshape(top, rows).T
    table = table[jax.random.permutation(jax.random.fold_in(own, 1), rows)]
    turn = jax.random.randint(jax.random.fold_in(own, 2), (rows, 1), 0, top)
    return jnp.take_along_axis(table, (jnp.arange(top)[None, :] + turn) % top, axis=1)


def shares(count, total, bound, skew, full):
    loads = [(1 << 20) // math.isqrt(grade ** skew) + 1 for grade in range(1, count + 1)]
    largest = bound if full else min(bound, max(-(-total // count), total * loads[0] // sum(loads)))
    least = 1 if total - largest >= count - 1 else 0
    given, surplus = [largest] + [least] * (count - 1), total - largest - least * (count - 1)
    while surplus > 0:
        free = [i for i in range(1, count) if given[i] < largest] or [i for i in range(1, count) if given[i] < bound]
        whole, left = sum([loads[i] for i in free]), surplus
        for i in free:
            addition = min(bound - given[i], max(1, left * loads[i] // whole), surplus)
            given[i] = given[i] + addition
            surplus = surplus - addition
    return np.array(given)


def normal_values(key, shape, deviation, bound, shards=(), held_as=jnp.bfloat16):
    level = block_scale(key, shape, shards, -0.22, 0.18) if shards else 1.0
    entries = jax.random.normal(key, shape, jnp.float32) * deviation * level
    return jnp.minimum(jnp.maximum(entries, -bound), bound).astype(held_as)


def bell_draw_with(stream_key, shape, scale, bound, pieces, heavy, kind=jnp.bfloat16):
    entries = scale * jax.random.normal(stream_key, shape, jnp.float32)
    if pieces:
        entries = entries * block_scale(stream_key, shape, pieces, -0.22, 0.18)
    return jnp.clip(strengthened(entries, jax.random.fold_in(stream_key, 3), *heavy), -bound, bound).astype(kind)


def setup_inputs(seed: int = 0) -> dict:
    key_list = jax.random.split(jax.random.key(seed), 7)
    tokens = bell_draw_with(key_list[0], (TOKENS, D), 1.0, 24.0, ((0, 128),), (0, 1, 128, 5.5))
    cotangent = normal_values(key_list[1], (TOKENS, D), 1.0, 6.0, ((0, 128),))
    expert_ids_keys = jax.random.split(jax.random.fold_in(key_list[2], 1), TOKENS // TOK_DEV)
    expert_ids_turns = jax.random.permutation(jax.random.fold_in(key_list[2], 3), TOKENS // TOK_DEV)
    expert_ids = jax.vmap(lambda own, number: shared_out(jax.random.fold_in(key_list[2], 2), own, number, TOK_DEV, EXPERTS, TOP, CAP, 1))(expert_ids_keys, expert_ids_turns).reshape((TOKENS, TOP))
    route_weight = jnp.clip(jnp.exp(math.log(0.5) - 3.218876 * jax.random.uniform(key_list[3], (TOKENS, TOP), jnp.float32) ** block_scale(key_list[3], (TOKENS, TOP), ((0, 128),), -0.2, 0.2)), 0.02, 0.5)
    up_weight = normal_values(key_list[4], (EXPERTS, D, H), D ** -0.5, 0.09375, ((0, 16),))
    down_weight = normal_values(key_list[5], (EXPERTS, H, D), H ** -0.5, 0.21875, ((0, 16),))
    return dict(tokens=tokens, cotangent=cotangent, expert_ids=expert_ids, route_weight=route_weight, up_weight=up_weight, down_weight=down_weight)


def reference(tokens, cotangent, expert_ids, route_weight, up_weight, down_weight):
    group_rows = N_EXPERT * TOK_DEV
    slots = N_EXPERT * CAP

    def one_expert(grad_total, expert):
        w_up = up_weight[expert]
        w_down = down_weight[expert]

        def one_group(carry, group):
            grad_acc, up_acc, down_acc = carry
            start = (group * group_rows).astype(jnp.int32)
            ids_group = lax.dynamic_slice_in_dim(expert_ids, start, group_rows, 0)
            present = jnp.any(ids_group == expert, axis=1)
            order = jnp.argsort(jnp.where(present, 0, 1).astype(jnp.int32), stable=True)[:slots].astype(jnp.int32)
            valid = present[order]
            index = (order + start).astype(jnp.int32)
            rows_x = jnp.where(valid[:, None], tokens[index], jnp.zeros((), tokens.dtype)).astype(jnp.bfloat16)
            weight_e = jnp.sum(jnp.where(expert_ids[index] == expert, route_weight[index], jnp.float32(0.0)), axis=1)
            rows_g = (weight_e[:, None] * cotangent[index].astype(jnp.float32)).astype(jnp.bfloat16)
            pre = jnp.dot(rows_x, w_up, preferred_element_type=jnp.float32)
            sigma = jax.nn.sigmoid(pre)
            active = (pre * sigma).astype(jnp.bfloat16)
            back = jnp.dot(rows_g, w_down.T, preferred_element_type=jnp.float32)
            pre_grad = (back * sigma * (1.0 + pre * (1.0 - sigma))).astype(jnp.bfloat16)
            row_grad = jnp.dot(pre_grad, w_up.T, preferred_element_type=jnp.float32).astype(jnp.bfloat16)
            row_grad = lax.optimization_barrier(row_grad).astype(jnp.float32)
            grad_acc = grad_acc.at[index].add(jnp.where(valid[:, None], row_grad, jnp.float32(0.0)))
            up_part = jnp.dot(rows_x.T, pre_grad, preferred_element_type=jnp.float32).astype(jnp.bfloat16)
            down_part = jnp.dot(active.T, rows_g, preferred_element_type=jnp.float32).astype(jnp.bfloat16)
            up_part, down_part = lax.optimization_barrier((up_part, down_part))
            return (grad_acc, up_acc + up_part.astype(jnp.float32), down_acc + down_part.astype(jnp.float32)), None

        start_carry = (grad_total, jnp.zeros((D, H), jnp.float32), jnp.zeros((H, D), jnp.float32))
        (grad_total, up_sum, down_sum), _ = lax.scan(one_group, start_carry, jnp.arange(N_DP, dtype=jnp.int32))
        return grad_total, (up_sum, down_sum)

    grad_start = jnp.zeros((TOKENS, D), jnp.float32)
    grad_total, (up_grad, down_grad) = lax.scan(one_expert, grad_start, jnp.arange(EXPERTS, dtype=jnp.int32))
    return grad_total.astype(jnp.bfloat16), up_grad, down_grad
```

```python
import functools

import jax
import jax.numpy as jnp
from jax import lax
from jax.experimental import pallas as pl
from jax.experimental.pallas import tpu as pltpu
from jax.sharding import PartitionSpec as P

SIDE = 4
OFFSETS = (0, 1, 3, 2)
SLOTS = 72
BOTH = ("dp", "expert")
VMEM_LIMIT = 48 * 1024 * 1024


def ring(first, shift):
    pairs = []
    for dp in range(8):
        along_x = first == (dp % 2 == 0)
        for y in range(SIDE):
            for x in range(SIDE):
                to = y * SIDE + (x + shift) % SIDE if along_x else ((y + shift) % SIDE) * SIDE + x
                pairs.append((dp * 16 + y * SIDE + x, dp * 16 + to))
    return pairs


def send(value, first, shift):
    shift = shift % SIDE
    return value if shift == 0 else lax.ppermute(value, BOTH, ring(first, shift))


def route_kernel(dest_ref, m0, m1, m2, m3, pick_ref, put_ref, weight_ref):
    rows = lax.broadcasted_iota(jnp.int32, (16, 128), 0)
    masks = jnp.zeros((16, 128), jnp.float32)
    weights = []
    for i, meta in enumerate((m0, m1, m2, m3)):
        ids, route = meta[0:8, :], meta[8:16, :]
        for j in range(SIDE):
            hit = ids == dest_ref[j].astype(jnp.float32)
            mask = jnp.sum(jnp.where(hit, 1.0, 0.0), axis=0, keepdims=True)
            weights.append(jnp.sum(jnp.where(hit, route, 0.0), axis=0, keepdims=True))
            masks = jnp.where(rows == i * SIDE + j, mask, masks)
    before = lax.broadcasted_iota(jnp.int32, (128, 128), 0) < lax.broadcasted_iota(
        jnp.int32, (128, 128), 1
    )
    rank = jnp.dot(
        masks.astype(jnp.bfloat16),
        before.astype(jnp.float32).astype(jnp.bfloat16),
        preferred_element_type=jnp.float32,
    )
    rank = jnp.where(masks > 0.5, rank, -1.0)
    slot = lax.broadcasted_iota(jnp.int32, (SLOTS, 128), 0).astype(jnp.float32)
    for i in range(SIDE):
        for j in range(SIDE):
            n = i * SIDE + j
            pick = jnp.where(slot == rank[n : n + 1, :], 1.0, 0.0)
            pick_ref[i, j * SLOTS : (j + 1) * SLOTS, :] = pick.astype(jnp.bfloat16)
            put_ref[i, j, :, :] = pick.T.astype(jnp.bfloat16)
            column = jnp.sum(pick * weights[n], axis=1, keepdims=True)
            weight_ref[i, j * SLOTS : (j + 1) * SLOTS, :] = jnp.broadcast_to(column, (SLOTS, 128))


def route(dest, metas):
    return pl.pallas_call(
        route_kernel,
        out_shape=(
            jax.ShapeDtypeStruct((SIDE, SIDE * SLOTS, 128), jnp.bfloat16),
            jax.ShapeDtypeStruct((SIDE, SIDE, 128, SLOTS), jnp.bfloat16),
            jax.ShapeDtypeStruct((SIDE, SIDE * SLOTS, 128), jnp.float32),
        ),
        in_specs=[pl.BlockSpec(memory_space=pltpu.SMEM)]
        + [pl.BlockSpec(memory_space=pltpu.VMEM)] * 4,
        out_specs=(pl.BlockSpec(memory_space=pltpu.VMEM),) * 3,
        name="route",
    )(dest, *metas)


def select_kernel(scaled, pick_ref, weight_ref, b0, b1, b2, b3, o0, o1, o2, o3):
    outs = (o0, o1, o2, o3)
    for i, block in enumerate((b0, b1, b2, b3)):
        rows = jnp.dot(pick_ref[i], block[...], preferred_element_type=jnp.float32)
        if scaled:
            rows = rows * weight_ref[i][:, 0:1]
        rows = rows.astype(jnp.bfloat16)
        for j in range(SIDE):
            outs[j][i, :, :] = rows[j * SLOTS : (j + 1) * SLOTS, :]


def select(pick, weight, blocks, scaled):
    width = blocks[0].shape[1]
    tile = 512
    return pl.pallas_call(
        functools.partial(select_kernel, scaled),
        out_shape=(jax.ShapeDtypeStruct((SIDE, SLOTS, width), jnp.bfloat16),) * SIDE,
        grid=(width // tile,),
        in_specs=[
            pl.BlockSpec((SIDE, SIDE * SLOTS, 128), lambda c: (0, 0, 0)),
            pl.BlockSpec((SIDE, SIDE * SLOTS, 128), lambda c: (0, 0, 0)),
        ]
        + [pl.BlockSpec((128, tile), lambda c: (0, c))] * SIDE,
        out_specs=(pl.BlockSpec((SIDE, SLOTS, tile), lambda c: (0, 0, c)),) * SIDE,
        compiler_params=pltpu.CompilerParams(vmem_limit_bytes=VMEM_LIMIT),
        cost_estimate=pl.CostEstimate(
            flops=2 * 1152 * 128 * width, bytes_accessed=1664 * width * 2, transcendentals=0
        ),
        name="select_scaled" if scaled else "select",
    )(pick, weight, *blocks)


def combine_kernel(put_ref, r0, r1, r2, r3, o0, o1, o2, o3):
    returned = (r0, r1, r2, r3)
    for i, out in enumerate((o0, o1, o2, o3)):
        total = jnp.dot(put_ref[i, 0], r0[i], preferred_element_type=jnp.float32)
        for j in range(1, SIDE):
            total += jnp.dot(put_ref[i, j], returned[j][i], preferred_element_type=jnp.float32)
        out[...] = total.astype(jnp.bfloat16)


def combine(put, returned):
    width = returned[0].shape[2]
    tile = 512
    return pl.pallas_call(
        combine_kernel,
        out_shape=(jax.ShapeDtypeStruct((128, width), jnp.bfloat16),) * SIDE,
        grid=(width // tile,),
        in_specs=[pl.BlockSpec((SIDE, SIDE, 128, SLOTS), lambda c: (0, 0, 0, 0))]
        + [pl.BlockSpec((SIDE, SLOTS, tile), lambda c: (0, 0, c))] * SIDE,
        out_specs=(pl.BlockSpec((128, tile), lambda c: (0, c)),) * SIDE,
        compiler_params=pltpu.CompilerParams(vmem_limit_bytes=VMEM_LIMIT),
        cost_estimate=pl.CostEstimate(
            flops=2 * 1152 * 128 * width, bytes_accessed=1664 * width * 2, transcendentals=0
        ),
        name="combine",
    )(put, *returned)


ROWS_FIRST = (((0,), (0,)), ((), ()))


def up_kernel(x0, x1, x2, x3, p0, p1, p2, p3, out):
    total = None
    for x, p in ((x0, p0), (x1, p1), (x2, p2), (x3, p3)):
        part = lax.dot_general(x[...], p[...], ROWS_FIRST, preferred_element_type=jnp.float32)
        total = part if total is None else total + part
    out[...] = total.astype(jnp.bfloat16)


def down_kernel(a0, a1, a2, a3, g0, g1, g2, g3, out):
    total = None
    for a, g in ((a0, g0), (a1, g1), (a2, g2), (a3, g3)):
        part = lax.dot_general(a[...], g[...], ROWS_FIRST, preferred_element_type=jnp.float32)
        total = part if total is None else total + part
    out[...] = total.astype(jnp.bfloat16)


def weight_grad(kernel, wide, narrow, wide_first):
    rows, width = wide[0].shape
    hidden = narrow[0].shape[1]
    tile = 512
    wide_specs = [pl.BlockSpec((rows, tile), lambda c: (0, c))] * SIDE
    narrow_specs = [pl.BlockSpec((rows, hidden), lambda c: (0, 0))] * SIDE
    cost = pl.CostEstimate(
        flops=2 * SIDE * rows * width * hidden,
        bytes_accessed=2 * (SIDE * rows * (width + hidden) + width * hidden),
        transcendentals=0,
    )
    params = pltpu.CompilerParams(vmem_limit_bytes=VMEM_LIMIT)
    if wide_first:
        return pl.pallas_call(
            kernel,
            out_shape=jax.ShapeDtypeStruct((width, hidden), jnp.bfloat16),
            grid=(width // tile,),
            in_specs=wide_specs + narrow_specs,
            out_specs=pl.BlockSpec((tile, hidden), lambda c: (c, 0)),
            compiler_params=params,
            cost_estimate=cost,
            name="up_grad",
        )(*wide, *narrow)
    return pl.pallas_call(
        kernel,
        out_shape=jax.ShapeDtypeStruct((hidden, width), jnp.bfloat16),
        grid=(width // tile,),
        in_specs=narrow_specs + wide_specs,
        out_specs=pl.BlockSpec((hidden, tile), lambda c: (0, c)),
        compiler_params=params,
        cost_estimate=cost,
        name="down_grad",
    )(*narrow, *wide)


def body(tokens, cotangent, expert_ids, route_weight, up_weight, down_weight):
    width = tokens.shape[1]
    up_matrix = up_weight[0]
    down_matrix = down_weight[0]
    odd = lax.axis_index("dp") % 2 == 1
    place = lax.axis_index("expert")
    y, x = place // SIDE, place % SIDE
    shifts = jnp.array(OFFSETS, jnp.int32)
    dest = jnp.where(odd, y * SIDE + (x + shifts) % SIDE, ((y + shifts) % SIDE) * SIDE + x)
    meta = jnp.concatenate([expert_ids.astype(jnp.float32).T, route_weight.T], axis=0)

    metas = [send(meta, True, o) for o in OFFSETS]
    token_blocks = [send(tokens, True, o) for o in OFFSETS]
    cot_blocks = [send(cotangent, True, o) for o in OFFSETS]
    pick, put, weight = route(dest, metas)

    rows_x = select(pick, weight, token_blocks, False)
    rows_x = [send(r, False, o).reshape(SIDE * SLOTS, width) for r, o in zip(rows_x, OFFSETS)]
    rows_g = select(pick, weight, cot_blocks, True)
    rows_g = [send(r, False, o).reshape(SIDE * SLOTS, width) for r, o in zip(rows_g, OFFSETS)]

    actives, grads, returned = [], [], []
    for rx, rg, o in zip(rows_x, rows_g, OFFSETS):
        pre = jnp.dot(rx, up_matrix, preferred_element_type=jnp.float32)
        sigma = jax.nn.sigmoid(pre)
        actives.append((pre * sigma).astype(jnp.bfloat16))
        back = lax.dot_general(
            rg, down_matrix, (((1,), (1,)), ((), ())), preferred_element_type=jnp.float32
        )
        grad = (back * sigma * (1.0 + pre * (1.0 - sigma))).astype(jnp.bfloat16)
        grads.append(grad)
        row_grad = lax.dot_general(
            grad, up_matrix, (((1,), (1,)), ((), ())), preferred_element_type=jnp.float32
        ).astype(jnp.bfloat16)
        returned.append(send(row_grad.reshape(SIDE, SLOTS, width), False, -o))

    up_part = weight_grad(up_kernel, rows_x, grads, True)
    up_grad = lax.psum_scatter(up_part, "dp", scatter_dimension=0, tiled=True)
    down_part = weight_grad(down_kernel, rows_g, actives, False)
    down_grad = lax.psum_scatter(down_part, "dp", scatter_dimension=0, tiled=True)

    parts = combine(put, returned)
    parts = [send(p, True, -o) for p, o in zip(parts, OFFSETS)]
    token_grad = sum(p.astype(jnp.float32) for p in parts).astype(jnp.bfloat16)
    return (
        token_grad,
        up_grad.astype(jnp.float32)[None],
        down_grad.astype(jnp.float32)[None],
    )


def solution(mesh):
    rows = P(("dp", "expert"), None)
    weights = P("expert", None, None)
    return jax.shard_map(
        body,
        mesh=mesh,
        in_specs=(rows, rows, rows, rows, weights, weights),
        out_specs=(rows, P("expert", "dp", None), P("expert", "dp", None)),
        check_vma=False,
    )
```

```python
import functools

import jax
import jax.numpy as jnp
from jax import lax
from jax.experimental import pallas as pl
from jax.experimental.pallas import tpu as pltpu
from jax.sharding import PartitionSpec as P

SIDE = 4
OFFSETS = (0, 1, 3, 2)
SLOTS = 72
BOTH = ("dp", "expert")
VMEM_LIMIT = 40 * 1024 * 1024
FREE = pl.CostEstimate(flops=1, bytes_accessed=1, transcendentals=0)
PARAMS = pltpu.CompilerParams(vmem_limit_bytes=VMEM_LIMIT)


def ring(first, shift):
    pairs = []
    for dp in range(8):
        along_x = first == (dp % 2 == 0)
        for y in range(SIDE):
            for x in range(SIDE):
                to = y * SIDE + (x + shift) % SIDE if along_x else ((y + shift) % SIDE) * SIDE + x
                pairs.append((dp * 16 + y * SIDE + x, dp * 16 + to))
    return pairs


def send(value, first, shift):
    shift = shift % SIDE
    return value if shift == 0 else lax.ppermute(value, BOTH, ring(first, shift))


def route_kernel(dest_ref, m0, m1, m2, m3, pick_ref, put_ref, weight_ref):
    rows = lax.broadcasted_iota(jnp.int32, (16, 128), 0)
    masks = jnp.zeros((16, 128), jnp.float32)
    weights = []
    for i, meta in enumerate((m0, m1, m2, m3)):
        ids, route = meta[0:8, :], meta[8:16, :]
        for j in range(SIDE):
            hit = ids == dest_ref[j].astype(jnp.float32)
            mask = jnp.sum(jnp.where(hit, 1.0, 0.0), axis=0, keepdims=True)
            weights.append(jnp.sum(jnp.where(hit, route, 0.0), axis=0, keepdims=True))
            masks = jnp.where(rows == i * SIDE + j, mask, masks)
    before = lax.broadcasted_iota(jnp.int32, (128, 128), 0) < lax.broadcasted_iota(
        jnp.int32, (128, 128), 1
    )
    rank = jnp.dot(
        masks.astype(jnp.bfloat16),
        before.astype(jnp.float32).astype(jnp.bfloat16),
        preferred_element_type=jnp.float32,
    )
    rank = jnp.where(masks > 0.5, rank, -1.0)
    slot = lax.broadcasted_iota(jnp.int32, (SLOTS, 128), 0).astype(jnp.float32)
    for i in range(SIDE):
        for j in range(SIDE):
            n = i * SIDE + j
            pick = jnp.where(slot == rank[n : n + 1, :], 1.0, 0.0)
            pick_ref[i, j * SLOTS : (j + 1) * SLOTS, :] = pick.astype(jnp.bfloat16)
            put_ref[i, j, :, :] = pick.T.astype(jnp.bfloat16)
            column = jnp.sum(pick * weights[n], axis=1, keepdims=True)
            weight_ref[i, j * SLOTS : (j + 1) * SLOTS, :] = jnp.broadcast_to(column, (SLOTS, 128))


def route(dest, metas):
    return pl.pallas_call(
        route_kernel,
        out_shape=(
            jax.ShapeDtypeStruct((SIDE, SIDE * SLOTS, 128), jnp.bfloat16),
            jax.ShapeDtypeStruct((SIDE, SIDE, 128, SLOTS), jnp.bfloat16),
            jax.ShapeDtypeStruct((SIDE, SIDE * SLOTS, 128), jnp.float32),
        ),
        in_specs=[pl.BlockSpec(memory_space=pltpu.SMEM)]
        + [pl.BlockSpec(memory_space=pltpu.VMEM)] * 4,
        out_specs=(pl.BlockSpec(memory_space=pltpu.VMEM),) * 3,
        cost_estimate=FREE,
        name="route",
    )(dest, *metas)


def select_kernel(scaled, pick_ref, weight_ref, b0, b1, b2, b3, o0, o1, o2, o3):
    outs = (o0, o1, o2, o3)
    for i, block in enumerate((b0, b1, b2, b3)):
        rows = jnp.dot(pick_ref[i], block[...], preferred_element_type=jnp.float32)
        if scaled:
            rows = rows * weight_ref[i][:, 0:1]
        rows = rows.astype(jnp.bfloat16)
        for j in range(SIDE):
            outs[j][i, :, :] = rows[j * SLOTS : (j + 1) * SLOTS, :]


def select(pick, weight, blocks, scaled):
    width = blocks[0].shape[1]
    tile = 512
    return pl.pallas_call(
        functools.partial(select_kernel, scaled),
        out_shape=(jax.ShapeDtypeStruct((SIDE, SLOTS, width), jnp.bfloat16),) * SIDE,
        grid=(width // tile,),
        in_specs=[
            pl.BlockSpec((SIDE, SIDE * SLOTS, 128), lambda c: (0, 0, 0)),
            pl.BlockSpec((SIDE, SIDE * SLOTS, 128), lambda c: (0, 0, 0)),
        ]
        + [pl.BlockSpec((128, tile), lambda c: (0, c))] * SIDE,
        out_specs=(pl.BlockSpec((SIDE, SLOTS, tile), lambda c: (0, 0, c)),) * SIDE,
        compiler_params=PARAMS,
        cost_estimate=FREE,
        name="select_scaled" if scaled else "select",
    )(pick, weight, *blocks)


def combine_kernel(put_ref, r0, r1, r2, r3, o0, o1, o2, o3):
    returned = (r0, r1, r2, r3)
    for i, out in enumerate((o0, o1, o2, o3)):
        total = jnp.dot(put_ref[i, 0], r0[i], preferred_element_type=jnp.float32)
        for j in range(1, SIDE):
            total += jnp.dot(put_ref[i, j], returned[j][i], preferred_element_type=jnp.float32)
        out[...] = total.astype(jnp.bfloat16)


def combine(put, returned):
    width = returned[0].shape[2]
    tile = 512
    return pl.pallas_call(
        combine_kernel,
        out_shape=(jax.ShapeDtypeStruct((128, width), jnp.bfloat16),) * SIDE,
        grid=(width // tile,),
        in_specs=[pl.BlockSpec((SIDE, SIDE, 128, SLOTS), lambda c: (0, 0, 0, 0))]
        + [pl.BlockSpec((SIDE, SLOTS, tile), lambda c: (0, 0, c))] * SIDE,
        out_specs=(pl.BlockSpec((128, tile), lambda c: (0, c)),) * SIDE,
        compiler_params=PARAMS,
        cost_estimate=FREE,
        name="combine",
    )(put, *returned)


TILE = 512
ROWS = SIDE * SLOTS
ROWS_FIRST = (((0,), (0,)), ((), ()))
COLS_LAST = (((1,), (1,)), ((), ()))


def dot(a, b, dims=(((1,), (0,)), ((), ()))):
    return lax.dot_general(a, b, dims, preferred_element_type=jnp.float32)


def pre_kernel(n, *refs):
    xs, up, pres, acts = refs[:n], refs[n], refs[n + 1 : 2 * n + 1], refs[2 * n + 1 :]
    step = pl.program_id(0)
    for x, pre, act in zip(xs, pres, acts):
        part = dot(x[...], up[...])

        @pl.when(step == 0)
        def _():
            pre[...] = part

        @pl.when(step > 0)
        def _():
            pre[...] += part

        @pl.when(step == pl.num_programs(0) - 1)
        def _():
            value = pre[...]
            active = value * jax.nn.sigmoid(value)
            act[...] = active.T.astype(jnp.bfloat16).reshape(act.shape)


def expert_pre(xs, up):
    n, (width, hidden) = len(xs), up.shape
    out = pl.pallas_call(
        functools.partial(pre_kernel, n),
        out_shape=(jax.ShapeDtypeStruct((ROWS, hidden), jnp.float32),) * n
        + (jax.ShapeDtypeStruct((8, hidden // 8, ROWS), jnp.bfloat16),) * n,
        grid=(width // TILE,),
        in_specs=[pl.BlockSpec((ROWS, TILE), lambda c: (0, c))] * n
        + [pl.BlockSpec((TILE, hidden), lambda c: (c, 0))],
        out_specs=(pl.BlockSpec((ROWS, hidden), lambda c: (0, 0)),) * n
        + (pl.BlockSpec((8, hidden // 8, ROWS), lambda c: (0, 0, 0)),) * n,
        compiler_params=PARAMS,
        cost_estimate=FREE,
        name="expert_pre",
    )(*xs, up)
    return list(zip(out[:n], out[n:]))


def back_kernel(n, *refs):
    gs, pres, down, up = refs[:n], refs[n : 2 * n], refs[2 * n], refs[2 * n + 1]
    grads, rows, back = refs[2 * n + 2 : 3 * n + 2], refs[3 * n + 2 : 4 * n + 2], refs[-1]
    step = pl.program_id(0)
    half = pl.num_programs(0) // 2

    @pl.when(step == 0)
    def _():
        for i in range(n):
            back[i] = dot(gs[i][...], down[...], COLS_LAST)

    @pl.when(jnp.logical_and(step > 0, step < half))
    def _():
        for i in range(n):
            back[i] += dot(gs[i][...], down[...], COLS_LAST)

    @pl.when(step == half - 1)
    def _():
        for i in range(n):
            value = pres[i][...]
            sigma = jax.nn.sigmoid(value)
            grad = back[i] * sigma * (1.0 + value * (1.0 - sigma))
            grads[i][...] = grad.astype(jnp.bfloat16)

    @pl.when(step >= half)
    def _():
        for i in range(n):
            rows[i][...] = dot(grads[i][...], up[...], COLS_LAST).astype(jnp.bfloat16)


def expert_back(gs, pres, down, up):
    n, (width, hidden) = len(gs), up.shape
    tiles = width // TILE
    out = pl.pallas_call(
        functools.partial(back_kernel, n),
        out_shape=(jax.ShapeDtypeStruct((ROWS, hidden), jnp.bfloat16),) * n
        + (jax.ShapeDtypeStruct((ROWS, width), jnp.bfloat16),) * n,
        grid=(2 * tiles,),
        in_specs=[pl.BlockSpec((ROWS, TILE), lambda c: (0, jnp.minimum(c, tiles - 1)))] * n
        + [pl.BlockSpec((ROWS, hidden), lambda c: (0, 0))] * n
        + [
            pl.BlockSpec((hidden, TILE), lambda c: (0, jnp.minimum(c, tiles - 1))),
            pl.BlockSpec((TILE, hidden), lambda c: (jnp.maximum(c - tiles, 0), 0)),
        ],
        out_specs=(pl.BlockSpec((ROWS, hidden), lambda c: (0, 0)),) * n
        + (pl.BlockSpec((ROWS, TILE), lambda c: (0, jnp.maximum(c - tiles, 0))),) * n,
        scratch_shapes=[pltpu.VMEM((n, ROWS, hidden), jnp.float32)],
        compiler_params=PARAMS,
        cost_estimate=FREE,
        name="expert_back",
    )(*gs, *pres, down, up)
    return list(zip(out[:n], out[n:]))


def up_kernel(kept, idx, *refs):
    xs, grads = refs[:SIDE], refs[SIDE : 2 * SIDE]
    total = sum(dot(x[...], p[...], ROWS_FIRST) for x, p in zip(xs, grads))
    if not kept:
        refs[-1][0] = total.astype(jnp.bfloat16)
        return
    total += refs[2 * SIDE][0].astype(jnp.float32)
    for k, out in enumerate(refs[2 * SIDE + 1 :]):

        @pl.when(pl.program_id(0) == k)
        def _():
            out[...] = total.astype(jnp.bfloat16)


def up_part(idx, xs, grads, received=None):
    hidden = grads[0].shape[1]
    kept = received is not None
    block = xs[0].shape[1] // 8
    slab = pl.BlockSpec((1, block, hidden), lambda s, idx: (s, 0, 0))
    if kept:
        shape = (jax.ShapeDtypeStruct((block, hidden), jnp.bfloat16),) * SIDE
        out_specs = (pl.BlockSpec((block, hidden), lambda s, idx: (0, 0)),) * SIDE
    else:
        shape = jax.ShapeDtypeStruct((SIDE, block, hidden), jnp.bfloat16)
        out_specs = slab
    return pl.pallas_call(
        functools.partial(up_kernel, kept),
        out_shape=shape,
        grid_spec=pltpu.PrefetchScalarGridSpec(
            num_scalar_prefetch=1,
            grid=(SIDE,),
            in_specs=[pl.BlockSpec((ROWS, block), lambda s, idx: (0, idx[s]))] * SIDE
            + [pl.BlockSpec((ROWS, hidden), lambda s, idx: (0, 0))] * SIDE
            + ([slab] if kept else []),
            out_specs=out_specs,
        ),
        compiler_params=PARAMS,
        cost_estimate=FREE,
        name="up_keep" if kept else "up_give",
    )(idx, *xs, *grads, *([received] if kept else []))


def down_kernel(kept, idx, *refs):
    acts, gs, lhs = refs[:SIDE], refs[SIDE : 2 * SIDE], refs[-1]
    part = acts[0].shape[1]

    @pl.when(pl.program_id(0) == 0)
    def _():
        for j, act in enumerate(acts):
            for s in range(SIDE):
                lhs[j, s * part : (s + 1) * part, :] = act[idx[s]]

    total = sum(dot(lhs[j], g[...]) for j, g in enumerate(gs))
    for s in range(SIDE):
        piece = total[s * part : (s + 1) * part, :]
        if kept:
            piece += refs[2 * SIDE][s].astype(jnp.float32)
            refs[2 * SIDE + 1 + s][...] = piece.astype(jnp.bfloat16)
        else:
            refs[2 * SIDE][s] = piece.astype(jnp.bfloat16)


def down_part(idx, acts, gs, received=None):
    kept = received is not None
    part, width = acts[0].shape[1], gs[0].shape[1]
    slab = pl.BlockSpec((SIDE, part, TILE), lambda c, idx: (0, 0, c))
    if kept:
        shape = (jax.ShapeDtypeStruct((part, width), jnp.bfloat16),) * SIDE
        out_specs = (pl.BlockSpec((part, TILE), lambda c, idx: (0, c)),) * SIDE
    else:
        shape = jax.ShapeDtypeStruct((SIDE, part, width), jnp.bfloat16)
        out_specs = slab
    return pl.pallas_call(
        functools.partial(down_kernel, kept),
        out_shape=shape,
        grid_spec=pltpu.PrefetchScalarGridSpec(
            num_scalar_prefetch=1,
            grid=(width // TILE,),
            in_specs=[pl.BlockSpec((8, part, ROWS), lambda c, idx: (0, 0, 0))] * SIDE
            + [pl.BlockSpec((ROWS, TILE), lambda c, idx: (0, c))] * SIDE
            + ([slab] if kept else []),
            out_specs=out_specs,
            scratch_shapes=[pltpu.VMEM((SIDE, SIDE * part, ROWS), jnp.bfloat16)],
        ),
        compiler_params=PARAMS,
        cost_estimate=FREE,
        name="down_keep" if kept else "down_give",
    )(idx, *acts, *gs, *([received] if kept else []))


def swap_cores(value):
    return lax.ppermute(value, "dp", [(d, d ^ 1) for d in range(8)])


def send_z(value, shift):
    pairs = [(z * 2 + c, (z + shift) % SIDE * 2 + c) for z in range(SIDE) for c in range(2)]
    return value if shift == 0 else lax.ppermute(value, "dp", pairs)


def after(value, *earlier):
    return lax.optimization_barrier((value, *earlier))[0]


def body(tokens, cotangent, expert_ids, route_weight, up_weight, down_weight):
    width = tokens.shape[1]
    up_matrix = up_weight[0]
    down_matrix = down_weight[0]
    dp = lax.axis_index("dp")
    core, z = dp & 1, dp >> 1
    place = lax.axis_index("expert")
    y, x = place >> 2, place & 3
    shifts = jnp.array(OFFSETS, jnp.int32)
    dest = jnp.where(core == 1, y * SIDE + ((x + shifts) & 3), ((y + shifts) & 3) * SIDE + x)
    keep = ((z + shifts) & 3) * 2 + core
    give = ((z + shifts) & 3) * 2 + 1 - core
    meta = jnp.concatenate([expert_ids.astype(jnp.float32).T, route_weight.T], axis=0)

    metas = [send(meta, True, o) for o in OFFSETS]
    token_blocks = [send(tokens, True, o) for o in OFFSETS]
    pick, put, weight = route(dest, metas)
    cotangent = after(cotangent, *token_blocks)
    cot_blocks = [send(cotangent, True, o) for o in OFFSETS]

    out_x = select(pick, weight, token_blocks, False)
    rx = [None] * SIDE
    rx[0], rx[1], rx[2] = (send(out_x[i], False, OFFSETS[i]) for i in range(3))
    rx[3] = send(after(out_x[3], rx[1], rx[2]), False, OFFSETS[3])
    out_g = select(pick, weight, cot_blocks, True)
    rg = [None] * SIDE
    rg[0] = out_g[0]
    rg[1], rg[2] = (send(after(out_g[i], rx[1], rx[2]), False, OFFSETS[i]) for i in (1, 2))
    rg[3] = send(after(out_g[3], rg[1], rg[2], rx[3]), False, OFFSETS[3])
    rx = [r.reshape(ROWS, width) for r in rx]
    rg = [r.reshape(ROWS, width) for r in rg]

    pre, back = [], []
    for group in ((0,), (1, 2), (3,)):
        pre += expert_pre([rx[i] for i in group], up_matrix)
    for group in ((0,), (1, 2), (3,)):
        back += expert_back(
            [rg[i] for i in group], [pre[i][0] for i in group], down_matrix, up_matrix
        )
    acts = [p[1] for p in pre]
    grads = [b[0] for b in back]
    row_grads = [b[1].reshape(SIDE, SLOTS, width) for b in back]
    returned = [send(r, False, -o) for r, o in zip(row_grads, OFFSETS)]

    acts[3] = after(acts[3], row_grads[3])
    down_give = down_part(give, acts, rg)
    up_give = up_part(give, rx, grads)
    down_keep = down_part(keep, acts, rg, swap_cores(down_give))
    up_keep = up_part(keep, rx, grads, swap_cores(up_give))
    down_sum = [send_z(p, o).astype(jnp.float32) for p, o in zip(down_keep, OFFSETS)]
    up_sum = [send_z(p, o).astype(jnp.float32) for p, o in zip(up_keep, OFFSETS)]

    parts = combine(put, returned)
    parts = [send(p, True, -o) for p, o in zip(parts, OFFSETS)]
    token_grad = sum(p.astype(jnp.float32) for p in parts).astype(jnp.bfloat16)
    return token_grad, sum(up_sum)[None], sum(down_sum)[None]


def solution(mesh):
    rows = P(("dp", "expert"), None)
    weights = P("expert", None, None)
    return jax.shard_map(
        body,
        mesh=mesh,
        in_specs=(rows, rows, rows, rows, weights, weights),
        out_specs=(rows, P("expert", "dp", None), P("expert", "dp", None)),
        check_vma=False,
    )
```

```python
import functools

import jax
import jax.numpy as jnp
from jax import lax
from jax.experimental import pallas as pl
from jax.experimental.pallas import tpu as pltpu
from jax.sharding import PartitionSpec as P

SIDE = 4
OFFSETS = (0, 1, 3, 2)
SLOTS = 72
BOTH = ("dp", "expert")
VMEM_LIMIT = 58 * 1024 * 1024


def cost(m, k, n):
    return pl.CostEstimate(
        flops=2 * m * k * n, bytes_accessed=2 * (m * k + k * n + m * n), transcendentals=0
    )


HEAVY = pl.CostEstimate(flops=30_000_000_000, bytes_accessed=1, transcendentals=0)
LIGHT = pl.CostEstimate(flops=1_000_000, bytes_accessed=1, transcendentals=0)
PARAMS = pltpu.CompilerParams(vmem_limit_bytes=VMEM_LIMIT)


def ring(first, shift):
    pairs = []
    for dp in range(8):
        along_x = first == (dp % 2 == 0)
        for y in range(SIDE):
            for x in range(SIDE):
                to = y * SIDE + (x + shift) % SIDE if along_x else ((y + shift) % SIDE) * SIDE + x
                pairs.append((dp * 16 + y * SIDE + x, dp * 16 + to))
    return pairs


def send(value, first, shift):
    shift = shift % SIDE
    return value if shift == 0 else lax.ppermute(value, BOTH, ring(first, shift))


def route_kernel(dest_ref, m0, m1, m2, m3, pick_ref, put_ref, weight_ref):
    rows = lax.broadcasted_iota(jnp.int32, (16, 128), 0)
    masks = jnp.zeros((16, 128), jnp.float32)
    weights = []
    for i, meta in enumerate((m0, m1, m2, m3)):
        ids, route = meta[0:8, :], meta[8:16, :]
        for j in range(SIDE):
            hit = ids == dest_ref[j].astype(jnp.float32)
            mask = jnp.sum(jnp.where(hit, 1.0, 0.0), axis=0, keepdims=True)
            weights.append(jnp.sum(jnp.where(hit, route, 0.0), axis=0, keepdims=True))
            masks = jnp.where(rows == i * SIDE + j, mask, masks)
    before = lax.broadcasted_iota(jnp.int32, (128, 128), 0) < lax.broadcasted_iota(
        jnp.int32, (128, 128), 1
    )
    rank = jnp.dot(
        masks.astype(jnp.bfloat16),
        before.astype(jnp.float32).astype(jnp.bfloat16),
        preferred_element_type=jnp.float32,
    )
    rank = jnp.where(masks > 0.5, rank, -1.0)
    slot = lax.broadcasted_iota(jnp.int32, (SLOTS, 128), 0).astype(jnp.float32)
    for i in range(SIDE):
        for j in range(SIDE):
            n = i * SIDE + j
            pick = jnp.where(slot == rank[n : n + 1, :], 1.0, 0.0)
            pick_ref[i, j * SLOTS : (j + 1) * SLOTS, :] = pick.astype(jnp.bfloat16)
            put_ref[i, j, :, :] = pick.T.astype(jnp.bfloat16)
            column = jnp.sum(pick * weights[n], axis=1, keepdims=True)
            weight_ref[i, j * SLOTS : (j + 1) * SLOTS, :] = jnp.broadcast_to(column, (SLOTS, 128))


def route(dest, metas):
    return pl.pallas_call(
        route_kernel,
        out_shape=(
            jax.ShapeDtypeStruct((SIDE, SIDE * SLOTS, 128), jnp.bfloat16),
            jax.ShapeDtypeStruct((SIDE, SIDE, 128, SLOTS), jnp.bfloat16),
            jax.ShapeDtypeStruct((SIDE, SIDE * SLOTS, 128), jnp.float32),
        ),
        in_specs=[pl.BlockSpec(memory_space=pltpu.SMEM)]
        + [pl.BlockSpec(memory_space=pltpu.VMEM)] * 4,
        out_specs=(pl.BlockSpec(memory_space=pltpu.VMEM),) * 3,
        cost_estimate=LIGHT,
        name="route",
    )(dest, *metas)


def select_kernel(scaled, pick_ref, weight_ref, b0, b1, b2, b3, o0, o1, o2, o3):
    outs = (o0, o1, o2, o3)
    for i, block in enumerate((b0, b1, b2, b3)):
        rows = jnp.dot(pick_ref[i], block[...], preferred_element_type=jnp.float32)
        if scaled:
            rows = rows * weight_ref[i][:, 0:1]
        rows = rows.astype(jnp.bfloat16)
        for j in range(SIDE):
            outs[j][i, :, :] = rows[j * SLOTS : (j + 1) * SLOTS, :]


def select(pick, weight, blocks, scaled):
    width = blocks[0].shape[1]
    tile = 512
    return pl.pallas_call(
        functools.partial(select_kernel, scaled),
        out_shape=(jax.ShapeDtypeStruct((SIDE, SLOTS, width), jnp.bfloat16),) * SIDE,
        grid=(width // tile,),
        in_specs=[
            pl.BlockSpec((SIDE, SIDE * SLOTS, 128), lambda c: (0, 0, 0)),
            pl.BlockSpec((SIDE, SIDE * SLOTS, 128), lambda c: (0, 0, 0)),
        ]
        + [pl.BlockSpec((128, tile), lambda c: (0, c))] * SIDE,
        out_specs=(pl.BlockSpec((SIDE, SLOTS, tile), lambda c: (0, 0, c)),) * SIDE,
        compiler_params=PARAMS,
        cost_estimate=HEAVY,
        name="select_scaled" if scaled else "select",
    )(pick, weight, *blocks)


def combine_kernel(put_ref, r0, r1, r2, r3, o0, o1, o2, o3):
    returned = (r0, r1, r2, r3)
    for i, out in enumerate((o0, o1, o2, o3)):
        total = jnp.dot(put_ref[i, 0], r0[i], preferred_element_type=jnp.float32)
        for j in range(1, SIDE):
            total += jnp.dot(put_ref[i, j], returned[j][i], preferred_element_type=jnp.float32)
        out[...] = total.astype(jnp.bfloat16)


def combine(put, returned):
    width = returned[0].shape[2]
    tile = 512
    return pl.pallas_call(
        combine_kernel,
        out_shape=(jax.ShapeDtypeStruct((128, width), jnp.bfloat16),) * SIDE,
        grid=(width // tile,),
        in_specs=[pl.BlockSpec((SIDE, SIDE, 128, SLOTS), lambda c: (0, 0, 0, 0))]
        + [pl.BlockSpec((SIDE, SLOTS, tile), lambda c: (0, 0, c))] * SIDE,
        out_specs=(pl.BlockSpec((128, tile), lambda c: (0, c)),) * SIDE,
        compiler_params=PARAMS,
        cost_estimate=HEAVY,
        name="combine",
    )(put, *returned)


TILE = 512
ROWS = SIDE * SLOTS
COLS_LAST = (((1,), (1,)), ((), ()))


def dot(a, b, dims=(((1,), (0,)), ((), ()))):
    return lax.dot_general(a, b, dims, preferred_element_type=jnp.float32)


def stacked(refs):
    return jnp.concatenate([r[...] for r in refs], axis=0)


def up_kernel(kept, idx, *refs):
    x, grads = refs[0], refs[1 : SIDE + 1]
    total = dot(x[0], stacked(grads))
    if not kept:
        refs[-1][0] = total.astype(jnp.bfloat16)
        return
    total += refs[SIDE + 1][0].astype(jnp.float32)
    for k, out in enumerate(refs[SIDE + 2 :]):

        @pl.when(pl.program_id(0) == k)
        def _():
            out[...] = total.astype(jnp.bfloat16)


def up_part(idx, xt, grads, received=None):
    hidden = grads[0].shape[1]
    kept = received is not None
    block, rows = xt.shape[1:]
    slab = pl.BlockSpec((1, block, hidden), lambda s, idx: (s, 0, 0))
    if kept:
        shape = (jax.ShapeDtypeStruct((block, hidden), jnp.bfloat16),) * SIDE
        out_specs = (pl.BlockSpec((block, hidden), lambda s, idx: (0, 0)),) * SIDE
    else:
        shape = jax.ShapeDtypeStruct((SIDE, block, hidden), jnp.bfloat16)
        out_specs = slab
    return pl.pallas_call(
        functools.partial(up_kernel, kept),
        out_shape=shape,
        grid_spec=pltpu.PrefetchScalarGridSpec(
            num_scalar_prefetch=1,
            grid=(SIDE,),
            in_specs=[pl.BlockSpec((1, block, rows), lambda s, idx: (idx[s], 0, 0))]
            + [pl.BlockSpec((ROWS, hidden), lambda s, idx: (0, 0))] * SIDE
            + ([slab] if kept else []),
            out_specs=out_specs,
        ),
        compiler_params=PARAMS,
        cost_estimate=cost(SIDE * block, rows, hidden),
        name="up_keep" if kept else "up_give",
    )(idx, xt, *grads, *([received] if kept else []))


def down_kernel(kept, idx, *refs):
    act, gs, lhs = refs[0], refs[1 : SIDE + 1], refs[-1]
    part = act.shape[1]

    @pl.when(pl.program_id(0) == 0)
    def _():
        for s in range(SIDE):
            lhs[s * part : (s + 1) * part, :] = act[idx[s]]

    total = dot(lhs[...], stacked(gs))
    for s in range(SIDE):
        piece = total[s * part : (s + 1) * part, :]
        if kept:
            piece += refs[SIDE + 1][s].astype(jnp.float32)
            refs[SIDE + 2 + s][...] = piece.astype(jnp.bfloat16)
        else:
            refs[SIDE + 1][s] = piece.astype(jnp.bfloat16)


def down_part(idx, act, gs, received=None):
    kept = received is not None
    part, rows = act.shape[1:]
    width = gs[0].shape[1]
    slab = pl.BlockSpec((SIDE, part, TILE), lambda c, idx: (0, 0, c))
    if kept:
        shape = (jax.ShapeDtypeStruct((part, width), jnp.bfloat16),) * SIDE
        out_specs = (pl.BlockSpec((part, TILE), lambda c, idx: (0, c)),) * SIDE
    else:
        shape = jax.ShapeDtypeStruct((SIDE, part, width), jnp.bfloat16)
        out_specs = slab
    return pl.pallas_call(
        functools.partial(down_kernel, kept),
        out_shape=shape,
        grid_spec=pltpu.PrefetchScalarGridSpec(
            num_scalar_prefetch=1,
            grid=(width // TILE,),
            in_specs=[pl.BlockSpec((8, part, rows), lambda c, idx: (0, 0, 0))]
            + [pl.BlockSpec((ROWS, TILE), lambda c, idx: (0, c))] * SIDE
            + ([slab] if kept else []),
            out_specs=out_specs,
            scratch_shapes=[pltpu.VMEM((SIDE * part, rows), jnp.bfloat16)],
        ),
        compiler_params=PARAMS,
        cost_estimate=cost(SIDE * part, rows, width),
        name="down_keep" if kept else "down_give",
    )(idx, act, *gs, *([received] if kept else []))


def swap_cores(value):
    return lax.ppermute(value, "dp", [(d, d ^ 1) for d in range(8)])


def send_z(value, shift):
    pairs = [(z * 2 + c, (z + shift) % SIDE * 2 + c) for z in range(SIDE) for c in range(2)]
    return value if shift == 0 else lax.ppermute(value, "dp", pairs)


def after(value, *earlier):
    return lax.optimization_barrier((value, *earlier))[0]


def body(tokens, cotangent, expert_ids, route_weight, up_weight, down_weight):
    width = tokens.shape[1]
    up_matrix = up_weight[0]
    down_matrix = down_weight[0]
    dp = lax.axis_index("dp")
    core, z = dp & 1, dp >> 1
    place = lax.axis_index("expert")
    y, x = place >> 2, place & 3
    shifts = jnp.array(OFFSETS, jnp.int32)
    dest = jnp.where(core == 1, y * SIDE + ((x + shifts) & 3), ((y + shifts) & 3) * SIDE + x)
    keep = ((z + shifts) & 3) * 2 + core
    give = ((z + shifts) & 3) * 2 + 1 - core
    meta = jnp.concatenate([expert_ids.astype(jnp.float32).T, route_weight.T], axis=0)

    with jax.named_scope("p1m"):
        metas = [send(meta, True, o) for o in OFFSETS]
    with jax.named_scope("p1x"):
        token_blocks = [send(tokens, True, o) for o in OFFSETS]
    pick, put, weight = route(dest, metas)
    cotangent = after(cotangent, *token_blocks)
    with jax.named_scope("p1g"):
        cot_blocks = [send(cotangent, True, o) for o in OFFSETS]

    out_x = select(pick, weight, token_blocks, False)
    with jax.named_scope("p2x"):
        rx = [send(r, False, o) for r, o in zip(out_x, OFFSETS)]
    out_g = select(pick, weight, cot_blocks, True)
    with jax.named_scope("p2g"):
        rg = [send(r, False, o) for r, o in zip(out_g[:3], OFFSETS)]
    with jax.named_scope("p2g2"):
        rg.append(send(after(out_g[3], *rx), False, OFFSETS[3]))
    rx = [r.reshape(ROWS, width) for r in rx]
    rg = [r.reshape(ROWS, width) for r in rg]

    pres = [dot(r, up_matrix) for r in rx]
    sigmas = [jax.nn.sigmoid(p) for p in pres]
    acts = [(p * s).astype(jnp.bfloat16) for p, s in zip(pres, sigmas)]
    act_t = jnp.concatenate(acts, axis=0).T.reshape(8, -1, SIDE * ROWS)
    x_t = jnp.concatenate(rx, axis=0).T.reshape(8, -1, SIDE * ROWS)
    grads, row_grads, returned = [], [], []
    for i, o in enumerate(OFFSETS):
        if i == 3:
            rg[3], act_t, x_t, _ = lax.optimization_barrier((rg[3], act_t, x_t, row_grads))
        back = dot(rg[i], down_matrix, COLS_LAST)
        grad = (back * sigmas[i] * (1.0 + pres[i] * (1.0 - sigmas[i]))).astype(jnp.bfloat16)
        grads.append(grad)
        row_grad = dot(grad, up_matrix, COLS_LAST).astype(jnp.bfloat16)
        row_grads.append(row_grad)
        with jax.named_scope("r2"):
            returned.append(send(row_grad.reshape(SIDE, SLOTS, width), False, -o))
    act_t = after(act_t, row_grads[3])

    down_give = down_part(give, act_t, rg)
    up_give = up_part(give, x_t, grads)
    with jax.named_scope("swap"):
        swapped_down, swapped_up = swap_cores(down_give), swap_cores(up_give)
    down_keep = down_part(keep, act_t, rg, swapped_down)
    up_keep = up_part(keep, x_t, grads, swapped_up)
    with jax.named_scope("zd"):
        down_sum = [send_z(p, o).astype(jnp.float32) for p, o in zip(down_keep, OFFSETS)]
    with jax.named_scope("zu"):
        up_sum = [send_z(p, o).astype(jnp.float32) for p, o in zip(up_keep, OFFSETS)]

    parts = combine(after(put, up_keep[0]), returned)
    with jax.named_scope("r1"):
        parts = [send(p, True, -o) for p, o in zip(parts, OFFSETS)]
    token_grad = sum(p.astype(jnp.float32) for p in parts).astype(jnp.bfloat16)
    return token_grad, sum(up_sum)[None], sum(down_sum)[None]


def solution(mesh):
    rows = P(("dp", "expert"), None)
    weights = P("expert", None, None)
    return jax.shard_map(
        body,
        mesh=mesh,
        in_specs=(rows, rows, rows, rows, weights, weights),
        out_specs=(rows, P("expert", "dp", None), P("expert", "dp", None)),
        check_vma=False,
    )
```

```python
import functools

import jax
import jax.numpy as jnp
from jax import lax
from jax.experimental import pallas as pl
from jax.experimental.pallas import tpu as pltpu
from jax.sharding import PartitionSpec as P

SIDE = 4
OFFSETS = (0, 1, 3, 2)
SLOTS = 72
BOTH = ("dp", "expert")
TILE = 1024
ROWS = SIDE * SLOTS
WIDE = 3 * ROWS
COLS_LAST = (((1,), (1,)), ((), ()))
ROWS_FIRST = (((0,), (0,)), ((), ()))
VMEM_LIMIT = 58 * 1024 * 1024


def cost(m, k, n):
    return pl.CostEstimate(
        flops=2 * m * k * n, bytes_accessed=2 * (m * k + k * n + m * n), transcendentals=0
    )


HEAVY = pl.CostEstimate(flops=30_000_000_000, bytes_accessed=1, transcendentals=0)
LIGHT = pl.CostEstimate(flops=1_000_000, bytes_accessed=1, transcendentals=0)
PARAMS = pltpu.CompilerParams(vmem_limit_bytes=VMEM_LIMIT)


def ring(first, shift):
    pairs = []
    for dp in range(8):
        along_x = first == (dp % 2 == 0)
        for y in range(SIDE):
            for x in range(SIDE):
                to = y * SIDE + (x + shift) % SIDE if along_x else ((y + shift) % SIDE) * SIDE + x
                pairs.append((dp * 16 + y * SIDE + x, dp * 16 + to))
    return pairs


def send(value, first, shift):
    shift = shift % SIDE
    return value if shift == 0 else lax.ppermute(value, BOTH, ring(first, shift))


def route_kernel(dest_ref, m0, m1, m2, m3, pick_ref, put_ref, weight_ref):
    rows = lax.broadcasted_iota(jnp.int32, (16, 128), 0)
    masks = jnp.zeros((16, 128), jnp.float32)
    weights = []
    for i, meta in enumerate((m0, m1, m2, m3)):
        packed = meta[...].astype(jnp.float32)
        ids = packed[:, 0:128]
        route = packed[:, 128:256] + packed[:, 256:384] + packed[:, 384:512]
        for j in range(SIDE):
            hit = ids == dest_ref[j].astype(jnp.float32)
            mask = jnp.sum(jnp.where(hit, 1.0, 0.0), axis=0, keepdims=True)
            weights.append(jnp.sum(jnp.where(hit, route, 0.0), axis=0, keepdims=True))
            masks = jnp.where(rows == i * SIDE + j, mask, masks)
    before = lax.broadcasted_iota(jnp.int32, (128, 128), 0) < lax.broadcasted_iota(
        jnp.int32, (128, 128), 1
    )
    rank = jnp.dot(
        masks.astype(jnp.bfloat16),
        before.astype(jnp.float32).astype(jnp.bfloat16),
        preferred_element_type=jnp.float32,
    )
    rank = jnp.where(masks > 0.5, rank, -1.0)
    slot = lax.broadcasted_iota(jnp.int32, (SLOTS, 128), 0).astype(jnp.float32)
    for i in range(SIDE):
        for j in range(SIDE):
            n = i * SIDE + j
            pick = jnp.where(slot == rank[n : n + 1, :], 1.0, 0.0)
            pick_ref[i, j * SLOTS : (j + 1) * SLOTS, :] = pick.astype(jnp.bfloat16)
            put_ref[i, j, :, :] = pick.T.astype(jnp.bfloat16)
            column = jnp.sum(pick * weights[n], axis=1, keepdims=True)
            weight_ref[i, j * SLOTS : (j + 1) * SLOTS, :] = jnp.broadcast_to(column, (SLOTS, 128))


def route(dest, blocks):
    return pl.pallas_call(
        route_kernel,
        out_shape=(
            jax.ShapeDtypeStruct((SIDE, SIDE * SLOTS, 128), jnp.bfloat16),
            jax.ShapeDtypeStruct((SIDE, SIDE, 128, SLOTS), jnp.bfloat16),
            jax.ShapeDtypeStruct((SIDE, SIDE * SLOTS, 128), jnp.float32),
        ),
        grid=(1,),
        in_specs=[pl.BlockSpec(memory_space=pltpu.SMEM)]
        + [pl.BlockSpec((8, 512), lambda c: (16, 0))] * SIDE,
        out_specs=(
            pl.BlockSpec((SIDE, ROWS, 128), lambda c: (0, 0, 0)),
            pl.BlockSpec((SIDE, SIDE, 128, SLOTS), lambda c: (0, 0, 0, 0)),
            pl.BlockSpec((SIDE, ROWS, 128), lambda c: (0, 0, 0)),
        ),
        cost_estimate=LIGHT,
        name="route",
    )(dest, *blocks)


def select_kernel(scaled, pick_ref, weight_ref, b0, b1, b2, b3, o0, o1, o2, o3):
    outs = (o0, o1, o2, o3)
    for i, block in enumerate((b0, b1, b2, b3)):
        rows = jnp.dot(pick_ref[i], block[...], preferred_element_type=jnp.float32)
        if scaled:
            rows = rows * weight_ref[i][:, 0:1]
        rows = rows.astype(jnp.bfloat16)
        for j in range(SIDE):
            outs[j][i, :, :] = rows[j * SLOTS : (j + 1) * SLOTS, :]


def select(pick, weight, blocks, scaled):
    width = blocks[0].shape[1]
    tile = TILE
    return pl.pallas_call(
        functools.partial(select_kernel, scaled),
        out_shape=(jax.ShapeDtypeStruct((SIDE, SLOTS, width), jnp.bfloat16),) * SIDE,
        grid=(width // tile,),
        in_specs=[
            pl.BlockSpec((SIDE, SIDE * SLOTS, 128), lambda c: (0, 0, 0)),
            pl.BlockSpec((SIDE, SIDE * SLOTS, 128), lambda c: (0, 0, 0)),
        ]
        + [pl.BlockSpec((128, tile), lambda c: (0, c))] * SIDE,
        out_specs=(pl.BlockSpec((SIDE, SLOTS, tile), lambda c: (0, 0, c)),) * SIDE,
        compiler_params=PARAMS,
        cost_estimate=HEAVY,
        name="select_scaled" if scaled else "select",
    )(pick, weight, *blocks)


def combine_kernel(put_ref, r0, r1, r2, r3, o0, o1, o2, o3):
    returned = (r0, r1, r2, r3)
    for i, out in enumerate((o0, o1, o2, o3)):
        total = jnp.dot(put_ref[i, 0], r0[i], preferred_element_type=jnp.float32)
        for j in range(1, SIDE):
            total += jnp.dot(put_ref[i, j], returned[j][i], preferred_element_type=jnp.float32)
        out[...] = total.astype(jnp.bfloat16)


def combine(put, returned):
    width = returned[0].shape[2]
    tile = TILE
    return pl.pallas_call(
        combine_kernel,
        out_shape=(jax.ShapeDtypeStruct((128, width), jnp.bfloat16),) * SIDE,
        grid=(width // tile,),
        in_specs=[pl.BlockSpec((SIDE, SIDE, 128, SLOTS), lambda c: (0, 0, 0, 0))]
        + [pl.BlockSpec((SIDE, SLOTS, tile), lambda c: (0, 0, c))] * SIDE,
        out_specs=(pl.BlockSpec((128, tile), lambda c: (0, c)),) * SIDE,
        compiler_params=PARAMS,
        cost_estimate=LIGHT,
        name="combine",
    )(put, *returned)


def dot(a, b, dims=(((1,), (0,)), ((), ()))):
    return lax.dot_general(a, b, dims, preferred_element_type=jnp.float32)


def stacked(refs):
    return jnp.concatenate([r[...] for r in refs], axis=0)


def pre_kernel(*refs):
    xs, up, pre, wide, last = refs[:SIDE], refs[SIDE], *refs[SIDE + 1 :]
    step = pl.program_id(0)
    part = dot(stacked(xs), up[...])

    @pl.when(step == 0)
    def _():
        pre[...] = part

    @pl.when(step > 0)
    def _():
        pre[...] += part

    @pl.when(step == pl.num_programs(0) - 1)
    def _():
        for rows, out in ((slice(0, WIDE), wide), (slice(WIDE, WIDE + ROWS), last)):
            value = pre[rows, :]
            out[...] = (value * jax.nn.sigmoid(value)).T.astype(jnp.bfloat16)


def expert_pre(xs, up):
    width, hidden = up.shape
    return pl.pallas_call(
        pre_kernel,
        out_shape=(
            jax.ShapeDtypeStruct((WIDE + ROWS, hidden), jnp.float32),
            jax.ShapeDtypeStruct((hidden, WIDE), jnp.bfloat16),
            jax.ShapeDtypeStruct((hidden, ROWS), jnp.bfloat16),
        ),
        grid=(width // TILE,),
        in_specs=[pl.BlockSpec((ROWS, TILE), lambda c: (0, c))] * SIDE
        + [pl.BlockSpec((TILE, hidden), lambda c: (c, 0))],
        out_specs=(
            pl.BlockSpec((WIDE + ROWS, hidden), lambda c: (0, 0)),
            pl.BlockSpec((hidden, WIDE), lambda c: (0, 0)),
            pl.BlockSpec((hidden, ROWS), lambda c: (0, 0)),
        ),
        compiler_params=PARAMS,
        cost_estimate=cost(WIDE + ROWS, width, hidden),
        name="expert_pre",
    )(*xs, up)


def back_kernel(n, *refs):
    gs, pre, down, up, grad, rows, back = refs[:n], *refs[n : n + 4], refs[n + 4 : -1], refs[-1]
    step = pl.program_id(0)
    half = pl.num_programs(0) // 2

    @pl.when(step == 0)
    def _():
        back[...] = dot(stacked(gs), down[...], COLS_LAST)

    @pl.when(jnp.logical_and(step > 0, step < half))
    def _():
        back[...] += dot(stacked(gs), down[...], COLS_LAST)

    @pl.when(step == half - 1)
    def _():
        value = pre[...]
        sigma = jax.nn.sigmoid(value)
        grad[...] = (back[...] * sigma * (1.0 + value * (1.0 - sigma))).astype(jnp.bfloat16)

    @pl.when(step >= half)
    def _():
        out = dot(grad[...], up[...], COLS_LAST).astype(jnp.bfloat16)
        for i in range(n):
            rows[i][...] = out[i * ROWS : (i + 1) * ROWS, :]


def expert_back(gs, pre, place, down, up):
    n, (width, hidden) = len(gs), up.shape
    tiles = width // TILE
    out = pl.pallas_call(
        functools.partial(back_kernel, n),
        out_shape=(jax.ShapeDtypeStruct((n * ROWS, hidden), jnp.bfloat16),)
        + (jax.ShapeDtypeStruct((ROWS, width), jnp.bfloat16),) * n,
        grid=(2 * tiles,),
        in_specs=[pl.BlockSpec((ROWS, TILE), lambda c: (0, jnp.minimum(c, tiles - 1)))] * n
        + [
            pl.BlockSpec((n * ROWS, hidden), lambda c: (place, 0)),
            pl.BlockSpec((hidden, TILE), lambda c: (0, jnp.minimum(c, tiles - 1))),
            pl.BlockSpec((TILE, hidden), lambda c: (jnp.maximum(c - tiles, 0), 0)),
        ],
        out_specs=(pl.BlockSpec((n * ROWS, hidden), lambda c: (0, 0)),)
        + (pl.BlockSpec((ROWS, TILE), lambda c: (0, jnp.maximum(c - tiles, 0))),) * n,
        scratch_shapes=[pltpu.VMEM((n * ROWS, hidden), jnp.float32)],
        compiler_params=PARAMS,
        cost_estimate=cost(2 * n * ROWS, width, hidden) if n > 1 else LIGHT,
        name="expert_back",
    )(*gs, pre, down, up)
    return out[0], list(out[1:])


def up_first_kernel(x0, x1, x2, grad, out):
    out[...] = dot(stacked((x0, x1, x2)), grad[...], ROWS_FIRST)


def up_first(xs, grad):
    width, hidden = xs[0].shape[1], grad.shape[1]
    return pl.pallas_call(
        up_first_kernel,
        out_shape=jax.ShapeDtypeStruct((width, hidden), jnp.float32),
        grid=(width // TILE,),
        in_specs=[pl.BlockSpec((ROWS, TILE), lambda c: (0, c))] * 3
        + [pl.BlockSpec((WIDE, hidden), lambda c: (0, 0))],
        out_specs=pl.BlockSpec((TILE, hidden), lambda c: (c, 0)),
        compiler_params=PARAMS,
        cost_estimate=cost(width, WIDE, hidden),
        name="up_first",
    )(*xs, grad)


def down_first_kernel(act, g0, g1, g2, out):
    out[...] = dot(act[...], stacked((g0, g1, g2)))


def down_first(act, gs):
    width, hidden = gs[0].shape[1], act.shape[0]
    return pl.pallas_call(
        down_first_kernel,
        out_shape=jax.ShapeDtypeStruct((hidden, width), jnp.float32),
        grid=(width // TILE,),
        in_specs=[pl.BlockSpec((hidden, WIDE), lambda c: (0, 0))]
        + [pl.BlockSpec((ROWS, TILE), lambda c: (0, c))] * 3,
        out_specs=pl.BlockSpec((hidden, TILE), lambda c: (0, c)),
        compiler_params=PARAMS,
        cost_estimate=cost(hidden, WIDE, width),
        name="down_first",
    )(act, *gs)


def up_last_kernel(idx, x, grad, acc, give, keep):
    total = (acc[...] + dot(x[...], grad[...], ROWS_FIRST)).astype(jnp.bfloat16)
    half = total.shape[0] // 2

    @pl.when(idx[SIDE] == 0)
    def _():
        keep[0], give[0] = total[:half], total[half:]

    @pl.when(idx[SIDE] == 1)
    def _():
        give[0], keep[0] = total[:half], total[half:]


def up_last(idx, x, grad, acc):
    width, hidden = acc.shape
    tile = width // SIDE
    slab = pl.BlockSpec((1, tile // 2, hidden), lambda s, idx: (s, 0, 0))
    return pl.pallas_call(
        up_last_kernel,
        out_shape=(jax.ShapeDtypeStruct((SIDE, tile // 2, hidden), jnp.bfloat16),) * 2,
        grid_spec=pltpu.PrefetchScalarGridSpec(
            num_scalar_prefetch=1,
            grid=(SIDE,),
            in_specs=[
                pl.BlockSpec((ROWS, tile), lambda s, idx: (0, idx[s])),
                pl.BlockSpec((ROWS, hidden), lambda s, idx: (0, 0)),
                pl.BlockSpec((tile, hidden), lambda s, idx: (idx[s], 0)),
            ],
            out_specs=(slab, slab),
        ),
        compiler_params=PARAMS,
        cost_estimate=LIGHT,
        name="up_last",
    )(idx, x, grad, acc)


def down_last_kernel(idx, act, g, acc, give, keep, total):
    value = acc[...] + dot(act[...], g[...])
    total[...] = value.reshape(total.shape)
    core = idx[SIDE]
    for s in range(SIDE):
        keep[s] = total[2 * idx[s] + core].astype(jnp.bfloat16)
        give[s] = total[2 * idx[s] + 1 - core].astype(jnp.bfloat16)


def down_last(idx, act, g, acc):
    hidden, width = acc.shape
    part = hidden // 8
    slab = pl.BlockSpec((SIDE, part, TILE), lambda c, idx: (0, 0, c))
    return pl.pallas_call(
        down_last_kernel,
        out_shape=(jax.ShapeDtypeStruct((SIDE, part, width), jnp.bfloat16),) * 2,
        grid_spec=pltpu.PrefetchScalarGridSpec(
            num_scalar_prefetch=1,
            grid=(width // TILE,),
            in_specs=[
                pl.BlockSpec((hidden, ROWS), lambda c, idx: (0, 0)),
                pl.BlockSpec((ROWS, TILE), lambda c, idx: (0, c)),
                pl.BlockSpec((hidden, TILE), lambda c, idx: (0, c)),
            ],
            out_specs=(slab, slab),
            scratch_shapes=[pltpu.VMEM((8, part, TILE), jnp.float32)],
        ),
        compiler_params=PARAMS,
        cost_estimate=LIGHT,
        name="down_last",
    )(idx, act, g, acc)


def swap_cores(value):
    return lax.ppermute(value, "dp", [(d, d ^ 1) for d in range(8)])


def send_z(value, shift):
    pairs = [(z * 2 + c, (z + shift) % SIDE * 2 + c) for z in range(SIDE) for c in range(2)]
    return value if shift == 0 else lax.ppermute(value, "dp", pairs)


def pairs_kernel(own, other, *outs):
    total = own[...].astype(jnp.float32) + other[...].astype(jnp.float32)
    for i, out in enumerate(outs):
        out[...] = total[i].astype(jnp.bfloat16)


def sum_pairs(own, other, dim):
    _, rows, columns = own.shape
    tile = (rows // SIDE, columns) if dim == 0 else (rows, columns // SIDE)

    def index(c):
        return (c, 0) if dim == 0 else (0, c)

    return pl.pallas_call(
        pairs_kernel,
        out_shape=(jax.ShapeDtypeStruct((rows, columns), jnp.bfloat16),) * SIDE,
        grid=(SIDE,),
        in_specs=[pl.BlockSpec((SIDE, *tile), lambda c: (0, *index(c)))] * 2,
        out_specs=(pl.BlockSpec(tile, index),) * SIDE,
        compiler_params=PARAMS,
        cost_estimate=LIGHT,
        name="sum_pairs",
    )(own, other)


def after(value, *earlier):
    return lax.optimization_barrier((value, *earlier))[0]


def body(tokens, cotangent, expert_ids, route_weight, up_weight, down_weight):
    width = tokens.shape[1]
    up_matrix = up_weight[0]
    down_matrix = down_weight[0]
    dp = lax.axis_index("dp")
    core, z = dp & 1, dp >> 1
    place = lax.axis_index("expert")
    y, x = place >> 2, place & 3
    shifts = jnp.array(OFFSETS, jnp.int32)
    dest = jnp.where(core == 1, y * SIDE + ((x + shifts) & 3), ((y + shifts) & 3) * SIDE + x)
    pieces = jnp.concatenate([(z + shifts) & 3, core[None]])
    high = lax.reduce_precision(route_weight, 8, 7)
    middle = lax.reduce_precision(route_weight - high, 8, 7)
    low = route_weight - high - middle
    meta = jnp.concatenate(
        [m.astype(jnp.bfloat16).T for m in (expert_ids, high, middle, low)], axis=1
    )
    message = jnp.concatenate([tokens, jnp.pad(meta, ((0, 0), (0, width - 512)))], axis=0)

    with jax.named_scope("p1x"):
        token_blocks = [send(message, True, o) for o in OFFSETS]
    cotangent = after(cotangent, *token_blocks)
    with jax.named_scope("p1g"):
        cot_blocks = [send(cotangent, True, o) for o in OFFSETS]
    pick, put, weight = route(dest, token_blocks)

    out_x = select(pick, weight, token_blocks, False)
    with jax.named_scope("p2x"):
        rx = [send(r, False, o).reshape(ROWS, width) for r, o in zip(out_x, OFFSETS)]
    out_g = select(pick, weight, cot_blocks, True)
    with jax.named_scope("p2g"):
        rg = [send(r, False, o).reshape(ROWS, width) for r, o in zip(out_g[:3], OFFSETS)]
    pre, act, act_last = expert_pre(rx, up_matrix)
    with jax.named_scope("p2g2"):
        last = send(after(out_g[3], *rx), False, OFFSETS[3]).reshape(ROWS, width)

    grad, rows = expert_back(rg, pre, 0, down_matrix, up_matrix)
    with jax.named_scope("r2"):
        returned = [send(r.reshape(SIDE, SLOTS, width), False, -o) for r, o in zip(rows, OFFSETS)]
    down_acc = down_first(act, rg)
    up_acc = up_first(rx[:3], grad)
    last, act_last, _ = lax.optimization_barrier((last, act_last, (rows, down_acc, up_acc)))

    down_give, down_keep = down_last(pieces, act_last, last, down_acc)
    with jax.named_scope("swap"):
        down_other = swap_cores(down_give)
    last = after(last, down_give)
    grad_last, rows_last = expert_back([last], pre, 3, down_matrix, up_matrix)
    with jax.named_scope("r2"):
        returned.append(send(rows_last[0].reshape(SIDE, SLOTS, width), False, -OFFSETS[3]))
    down_pairs = sum_pairs(down_keep, down_other, 1)
    grad_last = after(grad_last, rows_last[0], *down_pairs, *returned[:3])
    up_give, up_keep = up_last(pieces, rx[3], grad_last, up_acc)
    with jax.named_scope("swap"):
        up_other = swap_cores(up_give)
    up_pairs = sum_pairs(up_keep, up_other, 0)

    with jax.named_scope("zd"):
        down_sum = [send_z(p, o).astype(jnp.float32) for p, o in zip(down_pairs, OFFSETS)]
    with jax.named_scope("zu"):
        up_sum = [send_z(p, o).astype(jnp.float32) for p, o in zip(up_pairs, OFFSETS)]

    parts = combine(after(put, *up_pairs), returned)
    with jax.named_scope("r1"):
        parts = [send(p, True, -o) for p, o in zip(parts, OFFSETS)]
    token_grad = sum(p.astype(jnp.float32) for p in parts).astype(jnp.bfloat16)
    return token_grad, sum(up_sum)[None], sum(down_sum)[None]


def solution(mesh):
    rows = P(("dp", "expert"), None)
    weights = P("expert", None, None)
    return jax.shard_map(
        body,
        mesh=mesh,
        in_specs=(rows, rows, rows, rows, weights, weights),
        out_specs=(rows, P("expert", "dp", None), P("expert", "dp", None)),
        check_vma=False,
    )
```

```python
import functools

import jax
import jax.numpy as jnp
from jax import lax
from jax.experimental import pallas as pl
from jax.experimental.pallas import tpu as pltpu
from jax.sharding import PartitionSpec as P

SIDE = 4
OFFSETS = (0, 1, 3, 2)
SLOTS = 72
BOTH = ("dp", "expert")
TILE = 1024
ROWS = SIDE * SLOTS
WIDE = 3 * ROWS
COLS_LAST = (((1,), (1,)), ((), ()))
ROWS_FIRST = (((0,), (0,)), ((), ()))
VMEM_LIMIT = 58 * 1024 * 1024


def cost(m, k, n):
    return pl.CostEstimate(
        flops=2 * m * k * n, bytes_accessed=2 * (m * k + k * n + m * n), transcendentals=0
    )


HEAVY = pl.CostEstimate(flops=30_000_000_000, bytes_accessed=1, transcendentals=0)
LONGEST = pl.CostEstimate(flops=300_000_000_000, bytes_accessed=1, transcendentals=0)
LIGHT = pl.CostEstimate(flops=1_000_000, bytes_accessed=1, transcendentals=0)
PARAMS = pltpu.CompilerParams(vmem_limit_bytes=VMEM_LIMIT)


def ring(first, shift):
    pairs = []
    for dp in range(8):
        along_x = first == (dp % 2 == 0)
        for y in range(SIDE):
            for x in range(SIDE):
                to = y * SIDE + (x + shift) % SIDE if along_x else ((y + shift) % SIDE) * SIDE + x
                pairs.append((dp * 16 + y * SIDE + x, dp * 16 + to))
    return pairs


def send(value, first, shift):
    shift = shift % SIDE
    return value if shift == 0 else lax.ppermute(value, BOTH, ring(first, shift))


def route_kernel(dest_ref, m0, m1, m2, m3, pick_ref, put_ref, weight_ref):
    rows = lax.broadcasted_iota(jnp.int32, (16, 128), 0)
    masks = jnp.zeros((16, 128), jnp.float32)
    weights = []
    for i, meta in enumerate((m0, m1, m2, m3)):
        packed = meta[...].astype(jnp.float32)
        ids = packed[:, 0:128]
        route = packed[:, 128:256] + packed[:, 256:384] + packed[:, 384:512]
        for j in range(SIDE):
            hit = ids == dest_ref[j].astype(jnp.float32)
            mask = jnp.sum(jnp.where(hit, 1.0, 0.0), axis=0, keepdims=True)
            weights.append(jnp.sum(jnp.where(hit, route, 0.0), axis=0, keepdims=True))
            masks = jnp.where(rows == i * SIDE + j, mask, masks)
    before = lax.broadcasted_iota(jnp.int32, (128, 128), 0) < lax.broadcasted_iota(
        jnp.int32, (128, 128), 1
    )
    rank = jnp.dot(
        masks.astype(jnp.bfloat16),
        before.astype(jnp.float32).astype(jnp.bfloat16),
        preferred_element_type=jnp.float32,
    )
    rank = jnp.where(masks > 0.5, rank, -1.0)
    slot = lax.broadcasted_iota(jnp.int32, (SLOTS, 128), 0).astype(jnp.float32)
    for i in range(SIDE):
        for j in range(SIDE):
            n = i * SIDE + j
            pick = jnp.where(slot == rank[n : n + 1, :], 1.0, 0.0)
            pick_ref[i, j * SLOTS : (j + 1) * SLOTS, :] = pick.astype(jnp.bfloat16)
            put_ref[i, j, :, :] = pick.T.astype(jnp.bfloat16)
            column = jnp.sum(pick * weights[n], axis=1, keepdims=True)
            weight_ref[i, j * SLOTS : (j + 1) * SLOTS, :] = jnp.broadcast_to(column, (SLOTS, 128))


def route(dest, blocks):
    return pl.pallas_call(
        route_kernel,
        out_shape=(
            jax.ShapeDtypeStruct((SIDE, SIDE * SLOTS, 128), jnp.bfloat16),
            jax.ShapeDtypeStruct((SIDE, SIDE, 128, SLOTS), jnp.bfloat16),
            jax.ShapeDtypeStruct((SIDE, SIDE * SLOTS, 128), jnp.float32),
        ),
        grid=(1,),
        in_specs=[pl.BlockSpec(memory_space=pltpu.SMEM)]
        + [pl.BlockSpec((8, 512), lambda c: (16, 0))] * SIDE,
        out_specs=(
            pl.BlockSpec((SIDE, ROWS, 128), lambda c: (0, 0, 0)),
            pl.BlockSpec((SIDE, SIDE, 128, SLOTS), lambda c: (0, 0, 0, 0)),
            pl.BlockSpec((SIDE, ROWS, 128), lambda c: (0, 0, 0)),
        ),
        cost_estimate=LIGHT,
        name="route",
    )(dest, *blocks)


def select_kernel(scaled, pick_ref, weight_ref, b0, b1, b2, b3, o0, o1, o2, o3):
    outs = (o0, o1, o2, o3)
    for i, block in enumerate((b0, b1, b2, b3)):
        rows = jnp.dot(pick_ref[i], block[...], preferred_element_type=jnp.float32)
        if scaled:
            rows = rows * weight_ref[i][:, 0:1]
        rows = rows.astype(jnp.bfloat16)
        for j in range(SIDE):
            outs[j][i, :, :] = rows[j * SLOTS : (j + 1) * SLOTS, :]


def select(pick, weight, blocks, scaled):
    width = blocks[0].shape[1]
    tile = TILE
    return pl.pallas_call(
        functools.partial(select_kernel, scaled),
        out_shape=(jax.ShapeDtypeStruct((SIDE, SLOTS, width), jnp.bfloat16),) * SIDE,
        grid=(width // tile,),
        in_specs=[
            pl.BlockSpec((SIDE, SIDE * SLOTS, 128), lambda c: (0, 0, 0)),
            pl.BlockSpec((SIDE, SIDE * SLOTS, 128), lambda c: (0, 0, 0)),
        ]
        + [pl.BlockSpec((128, tile), lambda c: (0, c))] * SIDE,
        out_specs=(pl.BlockSpec((SIDE, SLOTS, tile), lambda c: (0, 0, c)),) * SIDE,
        compiler_params=PARAMS,
        cost_estimate=HEAVY,
        name="select_scaled" if scaled else "select",
    )(pick, weight, *blocks)


def combine_kernel(put_ref, r0, r1, r2, r3, o0, o1, o2, o3):
    returned = (r0, r1, r2, r3)
    for i, out in enumerate((o0, o1, o2, o3)):
        total = jnp.dot(put_ref[i, 0], r0[i], preferred_element_type=jnp.float32)
        for j in range(1, SIDE):
            total += jnp.dot(put_ref[i, j], returned[j][i], preferred_element_type=jnp.float32)
        out[...] = total.astype(jnp.bfloat16)


def combine(put, returned):
    width = returned[0].shape[2]
    tile = TILE
    return pl.pallas_call(
        combine_kernel,
        out_shape=(jax.ShapeDtypeStruct((128, width), jnp.bfloat16),) * SIDE,
        grid=(width // tile,),
        in_specs=[pl.BlockSpec((SIDE, SIDE, 128, SLOTS), lambda c: (0, 0, 0, 0))]
        + [pl.BlockSpec((SIDE, SLOTS, tile), lambda c: (0, 0, c))] * SIDE,
        out_specs=(pl.BlockSpec((128, tile), lambda c: (0, c)),) * SIDE,
        compiler_params=PARAMS,
        cost_estimate=LIGHT,
        name="combine",
    )(put, *returned)


def dot(a, b, dims=(((1,), (0,)), ((), ()))):
    return lax.dot_general(a, b, dims, preferred_element_type=jnp.float32)


def stacked(refs):
    return jnp.concatenate([r[...] for r in refs], axis=0)


def pre_kernel(*refs):
    xs, up, pre, act = refs[:SIDE], refs[SIDE], *refs[SIDE + 1 :]
    step = pl.program_id(0)
    part = dot(stacked(xs), up[...])

    @pl.when(step == 0)
    def _():
        pre[...] = part

    @pl.when(step > 0)
    def _():
        pre[...] += part

    @pl.when(step == pl.num_programs(0) - 1)
    def _():
        value = pre[...]
        act[...] = (value * jax.nn.sigmoid(value)).T.astype(jnp.bfloat16)


def expert_pre(xs, up):
    width, hidden = up.shape
    return pl.pallas_call(
        pre_kernel,
        out_shape=(
            jax.ShapeDtypeStruct((WIDE + ROWS, hidden), jnp.float32),
            jax.ShapeDtypeStruct((hidden, WIDE + ROWS), jnp.bfloat16),
        ),
        grid=(width // TILE,),
        in_specs=[pl.BlockSpec((ROWS, TILE), lambda c: (0, c))] * SIDE
        + [pl.BlockSpec((TILE, hidden), lambda c: (c, 0))],
        out_specs=(
            pl.BlockSpec((WIDE + ROWS, hidden), lambda c: (0, 0)),
            pl.BlockSpec((hidden, WIDE + ROWS), lambda c: (0, 0)),
        ),
        compiler_params=PARAMS,
        cost_estimate=cost(WIDE + ROWS, width, hidden),
        name="expert_pre",
    )(*xs, up)


def back_kernel(n, *refs):
    gs, pre, down, up, grad, rows, back = refs[:n], *refs[n : n + 4], refs[n + 4 : -1], refs[-1]
    step = pl.program_id(0)
    half = pl.num_programs(0) // 2

    @pl.when(step == 0)
    def _():
        back[...] = dot(stacked(gs), down[...], COLS_LAST)

    @pl.when(jnp.logical_and(step > 0, step < half))
    def _():
        back[...] += dot(stacked(gs), down[...], COLS_LAST)

    @pl.when(step == half - 1)
    def _():
        value = pre[...]
        sigma = jax.nn.sigmoid(value)
        grad[...] = (back[...] * sigma * (1.0 + value * (1.0 - sigma))).astype(jnp.bfloat16)

    @pl.when(step >= half)
    def _():
        out = dot(grad[...], up[...], COLS_LAST).astype(jnp.bfloat16)
        for i in range(n):
            rows[i][...] = out[i * ROWS : (i + 1) * ROWS, :]


def expert_back(gs, pre, place, down, up):
    n, (width, hidden) = len(gs), up.shape
    tiles = width // TILE
    out = pl.pallas_call(
        functools.partial(back_kernel, n),
        out_shape=(jax.ShapeDtypeStruct((n * ROWS, hidden), jnp.bfloat16),)
        + (jax.ShapeDtypeStruct((ROWS, width), jnp.bfloat16),) * n,
        grid=(2 * tiles,),
        in_specs=[pl.BlockSpec((ROWS, TILE), lambda c: (0, jnp.minimum(c, tiles - 1)))] * n
        + [
            pl.BlockSpec((n * ROWS, hidden), lambda c: (place, 0)),
            pl.BlockSpec((hidden, TILE), lambda c: (0, jnp.minimum(c, tiles - 1))),
            pl.BlockSpec((TILE, hidden), lambda c: (jnp.maximum(c - tiles, 0), 0)),
        ],
        out_specs=(pl.BlockSpec((n * ROWS, hidden), lambda c: (0, 0)),)
        + (pl.BlockSpec((ROWS, TILE), lambda c: (0, jnp.maximum(c - tiles, 0))),) * n,
        scratch_shapes=[pltpu.VMEM((n * ROWS, hidden), jnp.float32)],
        compiler_params=PARAMS,
        cost_estimate=cost(2 * n * ROWS, width, hidden) if n > 1 else LIGHT,
        name="expert_back",
    )(*gs, pre, down, up)
    return out[0], list(out[1:])


def up_kernel(x0, x1, x2, x3, grad, grad_last, out):
    total = dot(stacked((x0, x1, x2, x3)), stacked((grad, grad_last)), ROWS_FIRST)
    out[...] = total.astype(jnp.bfloat16)


def up_partial(xs, grads):
    width, hidden = xs[0].shape[1], grads[0].shape[1]
    return pl.pallas_call(
        up_kernel,
        out_shape=jax.ShapeDtypeStruct((width, hidden), jnp.bfloat16),
        grid=(width // TILE,),
        in_specs=[pl.BlockSpec((ROWS, TILE), lambda c: (0, c))] * SIDE
        + [pl.BlockSpec(g.shape, lambda c: (0, 0)) for g in grads],
        out_specs=pl.BlockSpec((TILE, hidden), lambda c: (c, 0)),
        compiler_params=PARAMS,
        cost_estimate=LIGHT,
        name="up_partial",
    )(*xs, *grads)


def down_kernel(act, g0, g1, g2, g3, out):
    out[...] = dot(act[...], stacked((g0, g1, g2, g3))).astype(jnp.bfloat16)


def down_partial(act, gs):
    hidden, rows = act.shape
    width = gs[0].shape[1]
    return pl.pallas_call(
        down_kernel,
        out_shape=jax.ShapeDtypeStruct((hidden, width), jnp.bfloat16),
        grid=(width // TILE,),
        in_specs=[pl.BlockSpec((hidden, rows), lambda c: (0, 0))]
        + [pl.BlockSpec((ROWS, TILE), lambda c: (0, c))] * SIDE,
        out_specs=pl.BlockSpec((hidden, TILE), lambda c: (0, c)),
        compiler_params=PARAMS,
        cost_estimate=LIGHT,
        name="down_partial",
    )(act, *gs)


def parts_kernel(p0, p1, p2, p3, out):
    total = sum(p[...].astype(jnp.float32) for p in (p0, p1, p2, p3))
    out[...] = total.astype(jnp.bfloat16)


def sum_parts(parts):
    rows, width = parts[0].shape
    spec = pl.BlockSpec((rows // SIDE, width), lambda c: (c, 0))
    return pl.pallas_call(
        parts_kernel,
        out_shape=jax.ShapeDtypeStruct((rows, width), jnp.bfloat16),
        grid=(SIDE,),
        in_specs=[spec] * SIDE,
        out_specs=spec,
        compiler_params=PARAMS,
        cost_estimate=LONGEST,
        name="sum_parts",
    )(*parts)


def after(value, *earlier):
    return lax.optimization_barrier((value, *earlier))[0]


def body(tokens, cotangent, expert_ids, route_weight, up_weight, down_weight):
    width = tokens.shape[1]
    up_matrix = up_weight[0]
    down_matrix = down_weight[0]
    dp = lax.axis_index("dp")
    core = dp & 1
    place = lax.axis_index("expert")
    y, x = place >> 2, place & 3
    shifts = jnp.array(OFFSETS, jnp.int32)
    dest = jnp.where(core == 1, y * SIDE + ((x + shifts) & 3), ((y + shifts) & 3) * SIDE + x)
    high = lax.reduce_precision(route_weight, 8, 7)
    middle = lax.reduce_precision(route_weight - high, 8, 7)
    low = route_weight - high - middle
    meta = jnp.concatenate(
        [m.astype(jnp.bfloat16).T for m in (expert_ids, high, middle, low)], axis=1
    )
    message = jnp.concatenate([tokens, jnp.pad(meta, ((0, 0), (0, width - 512)))], axis=0)

    with jax.named_scope("p1x"):
        token_blocks = [send(message, True, o) for o in OFFSETS]
    cotangent = after(cotangent, *token_blocks)
    with jax.named_scope("p1g"):
        cot_blocks = [send(cotangent, True, o) for o in OFFSETS]
    pick, put, weight = route(dest, token_blocks)

    out_x = select(pick, weight, token_blocks, False)
    with jax.named_scope("p2x"):
        rx = [send(r, False, o).reshape(ROWS, width) for r, o in zip(out_x, OFFSETS)]
    out_g = select(pick, weight, cot_blocks, True)
    with jax.named_scope("p2g"):
        rg = [send(r, False, o).reshape(ROWS, width) for r, o in zip(out_g[:3], OFFSETS)]
    pre, act = expert_pre(rx, up_matrix)
    with jax.named_scope("p2g2"):
        last = send(after(out_g[3], *rx, *rg), False, OFFSETS[3]).reshape(ROWS, width)

    grad, rows = expert_back(rg, pre, 0, down_matrix, up_matrix)
    with jax.named_scope("r2"):
        returned = [send(r.reshape(SIDE, SLOTS, width), False, -o) for r, o in zip(rows, OFFSETS)]

    last = after(last, *rows)
    down_part = down_partial(act, [*rg, last])
    down_grad = lax.psum_scatter(down_part, "dp", scatter_dimension=0, tiled=True)
    last = after(last, down_part)
    grad_last, rows_last = expert_back([last], pre, 3, down_matrix, up_matrix)
    with jax.named_scope("r2"):
        returned.append(send(rows_last[0].reshape(SIDE, SLOTS, width), False, -OFFSETS[3]))
    grad_last = after(grad_last, rows_last[0], *returned[:3])
    up_part = up_partial(rx, [grad, grad_last])
    up_grad = lax.psum_scatter(up_part, "dp", scatter_dimension=0, tiled=True)

    parts = combine(after(put, up_part), returned)
    with jax.named_scope("r1"):
        parts = [send(p, True, -o) for p, o in zip(parts, OFFSETS)]
    token_grad = sum_parts(parts)
    token_grad, up_grad, down_grad = lax.optimization_barrier((token_grad, up_grad, down_grad))
    return token_grad, up_grad.astype(jnp.float32)[None], down_grad.astype(jnp.float32)[None]


def solution(mesh):
    rows = P(("dp", "expert"), None)
    weights = P("expert", None, None)
    return jax.shard_map(
        body,
        mesh=mesh,
        in_specs=(rows, rows, rows, rows, weights, weights),
        out_specs=(rows, P("expert", "dp", None), P("expert", "dp", None)),
        check_vma=False,
    )
```

```python
import functools

import jax
import jax.numpy as jnp
from jax import lax
from jax.experimental import pallas as pl
from jax.experimental.pallas import tpu as pltpu
from jax.sharding import PartitionSpec as P

SIDE = 4
OFFSETS = (0, 1, 3, 2)
SLOTS = 72
BOTH = ("dp", "expert")
TILE = 1024
ROWS = SIDE * SLOTS
WIDE = 3 * ROWS
COLS_LAST = (((1,), (1,)), ((), ()))
ROWS_FIRST = (((0,), (0,)), ((), ()))
VMEM_LIMIT = 58 * 1024 * 1024


def cost(m, k, n):
    return pl.CostEstimate(
        flops=2 * m * k * n, bytes_accessed=2 * (m * k + k * n + m * n), transcendentals=0
    )


HEAVY = pl.CostEstimate(flops=30_000_000_000, bytes_accessed=1, transcendentals=0)
LONGEST = pl.CostEstimate(flops=300_000_000_000, bytes_accessed=1, transcendentals=0)
LIGHT = pl.CostEstimate(flops=1_000_000, bytes_accessed=1, transcendentals=0)
PARAMS = pltpu.CompilerParams(vmem_limit_bytes=VMEM_LIMIT)


def ring(first, shift):
    pairs = []
    for dp in range(8):
        along_x = first == (dp % 2 == 0)
        for y in range(SIDE):
            for x in range(SIDE):
                to = y * SIDE + (x + shift) % SIDE if along_x else ((y + shift) % SIDE) * SIDE + x
                pairs.append((dp * 16 + y * SIDE + x, dp * 16 + to))
    return pairs


def send(value, first, shift):
    shift = shift % SIDE
    return value if shift == 0 else lax.ppermute(value, BOTH, ring(first, shift))


def route_kernel(dest_ref, m0, m1, m2, m3, pick_ref, put_ref, weight_ref):
    rows = lax.broadcasted_iota(jnp.int32, (16, 128), 0)
    masks = jnp.zeros((16, 128), jnp.float32)
    weights = []
    for i, meta in enumerate((m0, m1, m2, m3)):
        packed = meta[...].astype(jnp.float32)
        ids = packed[:, 0:128]
        route = packed[:, 128:256] + packed[:, 256:384] + packed[:, 384:512]
        for j in range(SIDE):
            hit = ids == dest_ref[j].astype(jnp.float32)
            mask = jnp.sum(jnp.where(hit, 1.0, 0.0), axis=0, keepdims=True)
            weights.append(jnp.sum(jnp.where(hit, route, 0.0), axis=0, keepdims=True))
            masks = jnp.where(rows == i * SIDE + j, mask, masks)
    before = lax.broadcasted_iota(jnp.int32, (128, 128), 0) < lax.broadcasted_iota(
        jnp.int32, (128, 128), 1
    )
    rank = jnp.dot(
        masks.astype(jnp.bfloat16),
        before.astype(jnp.float32).astype(jnp.bfloat16),
        preferred_element_type=jnp.float32,
    )
    rank = jnp.where(masks > 0.5, rank, -1.0)
    slot = lax.broadcasted_iota(jnp.int32, (SLOTS, 128), 0).astype(jnp.float32)
    for i in range(SIDE):
        for j in range(SIDE):
            n = i * SIDE + j
            pick = jnp.where(slot == rank[n : n + 1, :], 1.0, 0.0)
            pick_ref[i, j * SLOTS : (j + 1) * SLOTS, :] = pick.astype(jnp.bfloat16)
            put_ref[i, j, :, :] = pick.T.astype(jnp.bfloat16)
            column = jnp.sum(pick * weights[n], axis=1, keepdims=True)
            weight_ref[i, j * SLOTS : (j + 1) * SLOTS, :] = jnp.broadcast_to(column, (SLOTS, 128))


def route(dest, blocks):
    return pl.pallas_call(
        route_kernel,
        out_shape=(
            jax.ShapeDtypeStruct((SIDE, SIDE * SLOTS, 128), jnp.bfloat16),
            jax.ShapeDtypeStruct((SIDE, SIDE, 128, SLOTS), jnp.bfloat16),
            jax.ShapeDtypeStruct((SIDE, SIDE * SLOTS, 128), jnp.float32),
        ),
        grid=(1,),
        in_specs=[pl.BlockSpec(memory_space=pltpu.SMEM)]
        + [pl.BlockSpec((8, 512), lambda c: (16, 0))] * SIDE,
        out_specs=(
            pl.BlockSpec((SIDE, ROWS, 128), lambda c: (0, 0, 0)),
            pl.BlockSpec((SIDE, SIDE, 128, SLOTS), lambda c: (0, 0, 0, 0)),
            pl.BlockSpec((SIDE, ROWS, 128), lambda c: (0, 0, 0)),
        ),
        cost_estimate=LIGHT,
        name="route",
    )(dest, *blocks)


def select_kernel(scaled, pick_ref, weight_ref, b0, b1, b2, b3, o0, o1, o2, o3):
    outs = (o0, o1, o2, o3)
    for i, block in enumerate((b0, b1, b2, b3)):
        rows = jnp.dot(pick_ref[i], block[...], preferred_element_type=jnp.float32)
        if scaled:
            rows = rows * weight_ref[i][:, 0:1]
        rows = rows.astype(jnp.bfloat16)
        for j in range(SIDE):
            outs[j][i, :, :] = rows[j * SLOTS : (j + 1) * SLOTS, :]


def select(pick, weight, blocks, scaled):
    width = blocks[0].shape[1]
    tile = TILE
    return pl.pallas_call(
        functools.partial(select_kernel, scaled),
        out_shape=(jax.ShapeDtypeStruct((SIDE, SLOTS, width), jnp.bfloat16),) * SIDE,
        grid=(width // tile,),
        in_specs=[
            pl.BlockSpec((SIDE, SIDE * SLOTS, 128), lambda c: (0, 0, 0)),
            pl.BlockSpec((SIDE, SIDE * SLOTS, 128), lambda c: (0, 0, 0)),
        ]
        + [pl.BlockSpec((128, tile), lambda c: (0, c))] * SIDE,
        out_specs=(pl.BlockSpec((SIDE, SLOTS, tile), lambda c: (0, 0, c)),) * SIDE,
        compiler_params=PARAMS,
        cost_estimate=HEAVY,
        name="select_scaled" if scaled else "select",
    )(pick, weight, *blocks)


def combine_kernel(put_ref, r0, r1, r2, r3, o0, o1, o2, o3):
    returned = (r0, r1, r2, r3)
    for i, out in enumerate((o0, o1, o2, o3)):
        total = jnp.dot(put_ref[i, 0], r0[i], preferred_element_type=jnp.float32)
        for j in range(1, SIDE):
            total += jnp.dot(put_ref[i, j], returned[j][i], preferred_element_type=jnp.float32)
        out[...] = total.astype(jnp.bfloat16)


def combine(put, returned):
    width = returned[0].shape[2]
    tile = TILE
    return pl.pallas_call(
        combine_kernel,
        out_shape=(jax.ShapeDtypeStruct((128, width), jnp.bfloat16),) * SIDE,
        grid=(width // tile,),
        in_specs=[pl.BlockSpec((SIDE, SIDE, 128, SLOTS), lambda c: (0, 0, 0, 0))]
        + [pl.BlockSpec((SIDE, SLOTS, tile), lambda c: (0, 0, c))] * SIDE,
        out_specs=(pl.BlockSpec((128, tile), lambda c: (0, c)),) * SIDE,
        compiler_params=PARAMS,
        cost_estimate=LIGHT,
        name="combine",
    )(put, *returned)


def dot(a, b, dims=(((1,), (0,)), ((), ()))):
    return lax.dot_general(a, b, dims, preferred_element_type=jnp.float32)


def stacked(refs):
    return jnp.concatenate([r[...] for r in refs], axis=0)


def pre_kernel(*refs):
    xs, up, pre, act = refs[:SIDE], refs[SIDE], *refs[SIDE + 1 :]
    step = pl.program_id(0)
    part = dot(stacked(xs), up[...])

    @pl.when(step == 0)
    def _():
        pre[...] = part

    @pl.when(step > 0)
    def _():
        pre[...] += part

    @pl.when(step == pl.num_programs(0) - 1)
    def _():
        value = pre[...]
        act[...] = (value * jax.nn.sigmoid(value)).T.astype(jnp.bfloat16)


def expert_pre(xs, up):
    width, hidden = up.shape
    return pl.pallas_call(
        pre_kernel,
        out_shape=(
            jax.ShapeDtypeStruct((WIDE + ROWS, hidden), jnp.float32),
            jax.ShapeDtypeStruct((hidden, WIDE + ROWS), jnp.bfloat16),
        ),
        grid=(width // TILE,),
        in_specs=[pl.BlockSpec((ROWS, TILE), lambda c: (0, c))] * SIDE
        + [pl.BlockSpec((TILE, hidden), lambda c: (c, 0))],
        out_specs=(
            pl.BlockSpec((WIDE + ROWS, hidden), lambda c: (0, 0)),
            pl.BlockSpec((hidden, WIDE + ROWS), lambda c: (0, 0)),
        ),
        compiler_params=PARAMS,
        cost_estimate=cost(WIDE + ROWS, width, hidden),
        name="expert_pre",
    )(*xs, up)


def back_kernel(n, *refs):
    gs, pre, down, up, grad, rows, back = refs[:n], *refs[n : n + 4], refs[n + 4 : -1], refs[-1]
    step = pl.program_id(0)
    half = pl.num_programs(0) // 2

    @pl.when(step == 0)
    def _():
        back[...] = dot(stacked(gs), down[...], COLS_LAST)

    @pl.when(jnp.logical_and(step > 0, step < half))
    def _():
        back[...] += dot(stacked(gs), down[...], COLS_LAST)

    @pl.when(step == half - 1)
    def _():
        value = pre[...]
        sigma = jax.nn.sigmoid(value)
        grad[...] = (back[...] * sigma * (1.0 + value * (1.0 - sigma))).astype(jnp.bfloat16)

    @pl.when(step >= half)
    def _():
        out = dot(grad[...], up[...], COLS_LAST).astype(jnp.bfloat16)
        for i in range(n):
            rows[i][...] = out[i * ROWS : (i + 1) * ROWS, :]


def expert_back(gs, pre, place, down, up):
    n, (width, hidden) = len(gs), up.shape
    tiles = width // TILE
    out = pl.pallas_call(
        functools.partial(back_kernel, n),
        out_shape=(jax.ShapeDtypeStruct((n * ROWS, hidden), jnp.bfloat16),)
        + (jax.ShapeDtypeStruct((ROWS, width), jnp.bfloat16),) * n,
        grid=(2 * tiles,),
        in_specs=[pl.BlockSpec((ROWS, TILE), lambda c: (0, jnp.minimum(c, tiles - 1)))] * n
        + [
            pl.BlockSpec((n * ROWS, hidden), lambda c: (place, 0)),
            pl.BlockSpec((hidden, TILE), lambda c: (0, jnp.minimum(c, tiles - 1))),
            pl.BlockSpec((TILE, hidden), lambda c: (jnp.maximum(c - tiles, 0), 0)),
        ],
        out_specs=(pl.BlockSpec((n * ROWS, hidden), lambda c: (0, 0)),)
        + (pl.BlockSpec((ROWS, TILE), lambda c: (0, jnp.maximum(c - tiles, 0))),) * n,
        scratch_shapes=[pltpu.VMEM((n * ROWS, hidden), jnp.float32)],
        compiler_params=PARAMS,
        cost_estimate=cost(2 * n * ROWS, width, hidden) if n > 1 else LIGHT,
        name="expert_back",
    )(*gs, pre, down, up)
    return out[0], list(out[1:])


def up_kernel(x0, x1, x2, x3, grad, grad_last, out):
    total = dot(stacked((x0, x1, x2, x3)), stacked((grad, grad_last)), ROWS_FIRST)
    out[...] = total.astype(jnp.bfloat16)


def up_partial(xs, grads):
    width, hidden = xs[0].shape[1], grads[0].shape[1]
    return pl.pallas_call(
        up_kernel,
        out_shape=jax.ShapeDtypeStruct((width, hidden), jnp.bfloat16),
        grid=(width // TILE,),
        in_specs=[pl.BlockSpec((ROWS, TILE), lambda c: (0, c))] * SIDE
        + [pl.BlockSpec(g.shape, lambda c: (0, 0)) for g in grads],
        out_specs=pl.BlockSpec((TILE, hidden), lambda c: (c, 0)),
        compiler_params=PARAMS,
        cost_estimate=LONGEST,
        name="up_partial",
    )(*xs, *grads)


def down_kernel(act, g0, g1, g2, g3, out):
    out[...] = dot(act[...], stacked((g0, g1, g2, g3))).astype(jnp.bfloat16)


def down_partial(act, gs):
    hidden, rows = act.shape
    width = gs[0].shape[1]
    return pl.pallas_call(
        down_kernel,
        out_shape=jax.ShapeDtypeStruct((hidden, width), jnp.bfloat16),
        grid=(width // TILE,),
        in_specs=[pl.BlockSpec((hidden, rows), lambda c: (0, 0))]
        + [pl.BlockSpec((ROWS, TILE), lambda c: (0, c))] * SIDE,
        out_specs=pl.BlockSpec((hidden, TILE), lambda c: (0, c)),
        compiler_params=PARAMS,
        cost_estimate=LIGHT,
        name="down_partial",
    )(act, *gs)


def parts_kernel(p0, p1, p2, p3, out):
    total = sum(p[...].astype(jnp.float32) for p in (p0, p1, p2, p3))
    out[...] = total.astype(jnp.bfloat16)


def sum_parts(parts):
    rows, width = parts[0].shape
    spec = pl.BlockSpec((rows // SIDE, width), lambda c: (c, 0))
    return pl.pallas_call(
        parts_kernel,
        out_shape=jax.ShapeDtypeStruct((rows, width), jnp.bfloat16),
        grid=(SIDE,),
        in_specs=[spec] * SIDE,
        out_specs=spec,
        compiler_params=PARAMS,
        cost_estimate=LIGHT,
        name="sum_parts",
    )(*parts)


def after(value, *earlier):
    return lax.optimization_barrier((value, *earlier))[0]


def body(tokens, cotangent, expert_ids, route_weight, up_weight, down_weight):
    width = tokens.shape[1]
    up_matrix = up_weight[0]
    down_matrix = down_weight[0]
    dp = lax.axis_index("dp")
    core = dp & 1
    place = lax.axis_index("expert")
    y, x = place >> 2, place & 3
    shifts = jnp.array(OFFSETS, jnp.int32)
    dest = jnp.where(core == 1, y * SIDE + ((x + shifts) & 3), ((y + shifts) & 3) * SIDE + x)
    high = lax.reduce_precision(route_weight, 8, 7)
    middle = lax.reduce_precision(route_weight - high, 8, 7)
    low = route_weight - high - middle
    meta = jnp.concatenate(
        [m.astype(jnp.bfloat16).T for m in (expert_ids, high, middle, low)], axis=1
    )
    message = jnp.concatenate([tokens, jnp.pad(meta, ((0, 0), (0, width - 512)))], axis=0)

    with jax.named_scope("p1x"):
        token_blocks = [send(message, True, o) for o in OFFSETS]
    cotangent = after(cotangent, *token_blocks)
    with jax.named_scope("p1g"):
        cot_blocks = [send(cotangent, True, o) for o in OFFSETS]
    pick, put, weight = route(dest, token_blocks)

    out_x = select(pick, weight, token_blocks, False)
    with jax.named_scope("p2x"):
        rx = [send(r, False, o).reshape(ROWS, width) for r, o in zip(out_x, OFFSETS)]
    out_g = select(pick, weight, cot_blocks, True)
    with jax.named_scope("p2g"):
        rg = [send(r, False, o).reshape(ROWS, width) for r, o in zip(out_g[:3], OFFSETS)]
    pre, act = expert_pre(rx, up_matrix)
    with jax.named_scope("p2g2"):
        last = send(after(out_g[3], pre, *rx, *rg), False, OFFSETS[3]).reshape(ROWS, width)

    grad, rows = expert_back(rg, pre, 0, down_matrix, up_matrix)
    with jax.named_scope("r2"):
        returned = [send(r.reshape(SIDE, SLOTS, width), False, -o) for r, o in zip(rows, OFFSETS)]

    last = after(last, *rows)
    down_part = down_partial(act, [*rg, last])
    down_grad = lax.psum_scatter(down_part, "dp", scatter_dimension=0, tiled=True)
    last = after(last, down_part)
    grad_last, rows_last = expert_back([last], pre, 3, down_matrix, up_matrix)
    with jax.named_scope("r2"):
        rows_last = after(rows_last[0], *returned).reshape(SIDE, SLOTS, width)
        returned.append(send(rows_last, False, -OFFSETS[3]))
    grad_last = after(grad_last, *returned[:3])
    up_part = up_partial(rx, [grad, grad_last])
    up_done, up_part = up_part, after(up_part, down_grad, returned[3])
    up_grad = lax.psum_scatter(up_part, "dp", scatter_dimension=0, tiled=True)

    parts = combine(after(put, up_done), returned)
    with jax.named_scope("r1"):
        parts = [send(p, True, -o) for p, o in zip(parts, OFFSETS)]
    token_grad = sum_parts(parts)
    token_grad, up_grad, down_grad = lax.optimization_barrier((token_grad, up_grad, down_grad))
    return token_grad, up_grad.astype(jnp.float32)[None], down_grad.astype(jnp.float32)[None]


def solution(mesh):
    rows = P(("dp", "expert"), None)
    weights = P("expert", None, None)
    return jax.shard_map(
        body,
        mesh=mesh,
        in_specs=(rows, rows, rows, rows, weights, weights),
        out_specs=(rows, P("expert", "dp", None), P("expert", "dp", None)),
        check_vma=False,
    )
```

```python
import functools

import jax
import jax.numpy as jnp
from jax import lax
from jax.experimental import pallas as pl
from jax.experimental.pallas import tpu as pltpu
from jax.sharding import PartitionSpec as P

SIDE = 4
OFFSETS = (0, 1, 3, 2)
SLOTS = 72
BOTH = ("dp", "expert")
TILE = 1024
ROWS = SIDE * SLOTS
WIDE = 3 * ROWS
COLS_LAST = (((1,), (1,)), ((), ()))
ROWS_FIRST = (((0,), (0,)), ((), ()))
VMEM_LIMIT = 58 * 1024 * 1024


def cost(m, k, n):
    return pl.CostEstimate(
        flops=2 * m * k * n, bytes_accessed=2 * (m * k + k * n + m * n), transcendentals=0
    )


HEAVY = pl.CostEstimate(flops=30_000_000_000, bytes_accessed=1, transcendentals=0)
LIGHT = pl.CostEstimate(flops=1_000_000, bytes_accessed=1, transcendentals=0)
PARAMS = pltpu.CompilerParams(vmem_limit_bytes=VMEM_LIMIT)


def ring(first, shift):
    pairs = []
    for dp in range(8):
        along_x = first == (dp % 2 == 0)
        for y in range(SIDE):
            for x in range(SIDE):
                to = y * SIDE + (x + shift) % SIDE if along_x else ((y + shift) % SIDE) * SIDE + x
                pairs.append((dp * 16 + y * SIDE + x, dp * 16 + to))
    return pairs


def send(value, first, shift):
    shift = shift % SIDE
    return value if shift == 0 else lax.ppermute(value, BOTH, ring(first, shift))


def route_kernel(dest_ref, m0, m1, m2, m3, pick_ref, put_ref, weight_ref):
    rows = lax.broadcasted_iota(jnp.int32, (16, 128), 0)
    masks = jnp.zeros((16, 128), jnp.float32)
    weights = []
    for i, meta in enumerate((m0, m1, m2, m3)):
        packed = meta[...].astype(jnp.float32)
        ids = packed[:, 0:128]
        route = packed[:, 128:256] + packed[:, 256:384] + packed[:, 384:512]
        for j in range(SIDE):
            hit = ids == dest_ref[j].astype(jnp.float32)
            mask = jnp.sum(jnp.where(hit, 1.0, 0.0), axis=0, keepdims=True)
            weights.append(jnp.sum(jnp.where(hit, route, 0.0), axis=0, keepdims=True))
            masks = jnp.where(rows == i * SIDE + j, mask, masks)
    before = lax.broadcasted_iota(jnp.int32, (128, 128), 0) < lax.broadcasted_iota(
        jnp.int32, (128, 128), 1
    )
    rank = jnp.dot(
        masks.astype(jnp.bfloat16),
        before.astype(jnp.float32).astype(jnp.bfloat16),
        preferred_element_type=jnp.float32,
    )
    rank = jnp.where(masks > 0.5, rank, -1.0)
    slot = lax.broadcasted_iota(jnp.int32, (SLOTS, 128), 0).astype(jnp.float32)
    for i in range(SIDE):
        for j in range(SIDE):
            n = i * SIDE + j
            pick = jnp.where(slot == rank[n : n + 1, :], 1.0, 0.0)
            pick_ref[i, j * SLOTS : (j + 1) * SLOTS, :] = pick.astype(jnp.bfloat16)
            put_ref[i, j, :, :] = pick.T.astype(jnp.bfloat16)
            column = jnp.sum(pick * weights[n], axis=1, keepdims=True)
            weight_ref[i, j * SLOTS : (j + 1) * SLOTS, :] = jnp.broadcast_to(column, (SLOTS, 128))


def route(dest, blocks):
    return pl.pallas_call(
        route_kernel,
        out_shape=(
            jax.ShapeDtypeStruct((SIDE, SIDE * SLOTS, 128), jnp.bfloat16),
            jax.ShapeDtypeStruct((SIDE, SIDE, 128, SLOTS), jnp.bfloat16),
            jax.ShapeDtypeStruct((SIDE, SIDE * SLOTS, 128), jnp.float32),
        ),
        grid=(1,),
        in_specs=[pl.BlockSpec(memory_space=pltpu.SMEM)]
        + [pl.BlockSpec((8, 512), lambda c: (16, 0))] * SIDE,
        out_specs=(
            pl.BlockSpec((SIDE, ROWS, 128), lambda c: (0, 0, 0)),
            pl.BlockSpec((SIDE, SIDE, 128, SLOTS), lambda c: (0, 0, 0, 0)),
            pl.BlockSpec((SIDE, ROWS, 128), lambda c: (0, 0, 0)),
        ),
        cost_estimate=LIGHT,
        name="route",
    )(dest, *blocks)


def select_kernel(scaled, pick_ref, weight_ref, b0, b1, b2, b3, o0, o1, o2, o3):
    outs = (o0, o1, o2, o3)
    for i, block in enumerate((b0, b1, b2, b3)):
        rows = jnp.dot(pick_ref[i], block[...], preferred_element_type=jnp.float32)
        if scaled:
            rows = rows * weight_ref[i][:, 0:1]
        rows = rows.astype(jnp.bfloat16)
        for j in range(SIDE):
            outs[j][i, :, :] = rows[j * SLOTS : (j + 1) * SLOTS, :]


def select(pick, weight, blocks, scaled):
    width = blocks[0].shape[1]
    tile = TILE
    return pl.pallas_call(
        functools.partial(select_kernel, scaled),
        out_shape=(jax.ShapeDtypeStruct((SIDE, SLOTS, width), jnp.bfloat16),) * SIDE,
        grid=(width // tile,),
        in_specs=[
            pl.BlockSpec((SIDE, SIDE * SLOTS, 128), lambda c: (0, 0, 0)),
            pl.BlockSpec((SIDE, SIDE * SLOTS, 128), lambda c: (0, 0, 0)),
        ]
        + [pl.BlockSpec((128, tile), lambda c: (0, c))] * SIDE,
        out_specs=(pl.BlockSpec((SIDE, SLOTS, tile), lambda c: (0, 0, c)),) * SIDE,
        compiler_params=PARAMS,
        cost_estimate=HEAVY,
        name="select_scaled" if scaled else "select",
    )(pick, weight, *blocks)


def combine_kernel(put_ref, r0, r1, r2, r3, o0, o1, o2, o3):
    returned = (r0, r1, r2, r3)
    for i, out in enumerate((o0, o1, o2, o3)):
        total = jnp.dot(put_ref[i, 0], r0[i], preferred_element_type=jnp.float32)
        for j in range(1, SIDE):
            total += jnp.dot(put_ref[i, j], returned[j][i], preferred_element_type=jnp.float32)
        out[...] = total.astype(jnp.bfloat16)


def combine(put, returned, last, half):
    width = last.shape[2]
    first = half * (width // TILE)
    return pl.pallas_call(
        combine_kernel,
        out_shape=(jax.ShapeDtypeStruct((128, width), jnp.bfloat16),) * SIDE,
        grid=(width // TILE,),
        in_specs=[pl.BlockSpec((SIDE, SIDE, 128, SLOTS), lambda c: (0, 0, 0, 0))]
        + [pl.BlockSpec((SIDE, SLOTS, TILE), lambda c: (0, 0, c + first))] * 3
        + [pl.BlockSpec((SIDE, SLOTS, TILE), lambda c: (0, 0, c))],
        out_specs=(pl.BlockSpec((128, TILE), lambda c: (0, c)),) * SIDE,
        compiler_params=PARAMS,
        cost_estimate=LIGHT,
        name="combine",
    )(put, *returned, last)


def dot(a, b, dims=(((1,), (0,)), ((), ()))):
    return lax.dot_general(a, b, dims, preferred_element_type=jnp.float32)


def stacked(refs):
    return jnp.concatenate([r[...] for r in refs], axis=0)


def pre_kernel(*refs):
    xs, up, pre, act = refs[:SIDE], refs[SIDE], *refs[SIDE + 1 :]
    step = pl.program_id(0)
    part = dot(stacked(xs), up[...])

    @pl.when(step == 0)
    def _():
        pre[...] = part

    @pl.when(step > 0)
    def _():
        pre[...] += part

    @pl.when(step == pl.num_programs(0) - 1)
    def _():
        value = pre[...]
        act[...] = (value * jax.nn.sigmoid(value)).T.astype(jnp.bfloat16)


def expert_pre(xs, up):
    width, hidden = up.shape
    return pl.pallas_call(
        pre_kernel,
        out_shape=(
            jax.ShapeDtypeStruct((WIDE + ROWS, hidden), jnp.float32),
            jax.ShapeDtypeStruct((hidden, WIDE + ROWS), jnp.bfloat16),
        ),
        grid=(width // TILE,),
        in_specs=[pl.BlockSpec((ROWS, TILE), lambda c: (0, c))] * SIDE
        + [pl.BlockSpec((TILE, hidden), lambda c: (c, 0))],
        out_specs=(
            pl.BlockSpec((WIDE + ROWS, hidden), lambda c: (0, 0)),
            pl.BlockSpec((hidden, WIDE + ROWS), lambda c: (0, 0)),
        ),
        compiler_params=PARAMS,
        cost_estimate=cost(WIDE + ROWS, width, hidden),
        name="expert_pre",
    )(*xs, up)


def back_kernel(n, *refs):
    gs, pre, down, up, grad, rows, back = refs[:n], *refs[n : n + 4], refs[n + 4 : -1], refs[-1]
    step = pl.program_id(0)
    half = pl.num_programs(0) // 2

    @pl.when(step == 0)
    def _():
        back[...] = dot(stacked(gs), down[...], COLS_LAST)

    @pl.when(jnp.logical_and(step > 0, step < half))
    def _():
        back[...] += dot(stacked(gs), down[...], COLS_LAST)

    @pl.when(step == half - 1)
    def _():
        value = pre[...]
        sigma = jax.nn.sigmoid(value)
        grad[...] = (back[...] * sigma * (1.0 + value * (1.0 - sigma))).astype(jnp.bfloat16)

    @pl.when(step >= half)
    def _():
        out = dot(grad[...], up[...], COLS_LAST).astype(jnp.bfloat16)
        if n > 1:
            for i in range(n):
                rows[i][...] = out[i * ROWS : (i + 1) * ROWS, :]
            return
        left = step < half + half // 2

        @pl.when(left)
        def _():
            rows[0][...] = out

        @pl.when(jnp.logical_not(left))
        def _():
            rows[1][...] = out


def expert_back(gs, pre, place, down, up):
    n, (width, hidden) = len(gs), up.shape
    tiles = width // TILE
    middle = tiles // 2
    row_shapes = (jax.ShapeDtypeStruct((ROWS, width), jnp.bfloat16),) * n
    row_specs = (pl.BlockSpec((ROWS, TILE), lambda c: (0, jnp.maximum(c - tiles, 0))),) * n
    if n == 1:
        row_shapes = (jax.ShapeDtypeStruct((ROWS, width // 2), jnp.bfloat16),) * 2
        row_specs = (
            pl.BlockSpec((ROWS, TILE), lambda c: (0, jnp.clip(c - tiles, 0, middle - 1))),
            pl.BlockSpec((ROWS, TILE), lambda c: (0, jnp.maximum(c - tiles - middle, 0))),
        )
    out = pl.pallas_call(
        functools.partial(back_kernel, n),
        out_shape=(jax.ShapeDtypeStruct((n * ROWS, hidden), jnp.bfloat16),) + row_shapes,
        grid=(2 * tiles,),
        in_specs=[pl.BlockSpec((ROWS, TILE), lambda c: (0, jnp.minimum(c, tiles - 1)))] * n
        + [
            pl.BlockSpec((n * ROWS, hidden), lambda c: (place, 0)),
            pl.BlockSpec((hidden, TILE), lambda c: (0, jnp.minimum(c, tiles - 1))),
            pl.BlockSpec((TILE, hidden), lambda c: (jnp.maximum(c - tiles, 0), 0)),
        ],
        out_specs=(pl.BlockSpec((n * ROWS, hidden), lambda c: (0, 0)),) + row_specs,
        scratch_shapes=[pltpu.VMEM((n * ROWS, hidden), jnp.float32)],
        compiler_params=PARAMS,
        cost_estimate=cost(2 * n * ROWS, width, hidden) if n > 1 else LIGHT,
        name="expert_back",
    )(*gs, pre, down, up)
    return out[0], list(out[1:])


STRIP = 128


def up_kernel(x0, x1, x2, x3, grad, grad_last, out):
    total = dot(stacked((x0, x1, x2, x3)), stacked((grad, grad_last)), ROWS_FIRST)
    total = total.astype(jnp.bfloat16)
    blocks = out.shape[0]
    rows = total.shape[0] // blocks
    for d in range(blocks):
        for k in range(total.shape[1] // STRIP):
            strip = total[d * rows : (d + 1) * rows, k * STRIP : (k + 1) * STRIP]
            out[d, 0, k * rows : (k + 1) * rows, :] = strip


def up_partial(xs, grads):
    width, hidden = xs[0].shape[1], grads[0].shape[1]
    strips = width // 8 * hidden // STRIP
    blocks = TILE * 8 // width
    return pl.pallas_call(
        up_kernel,
        out_shape=jax.ShapeDtypeStruct((8, 2, strips, STRIP), jnp.bfloat16),
        grid=(width // TILE,),
        in_specs=[pl.BlockSpec((ROWS, TILE), lambda c: (0, c))] * SIDE
        + [pl.BlockSpec(g.shape, lambda c: (0, 0)) for g in grads],
        out_specs=pl.BlockSpec((blocks, 1, strips, STRIP), lambda c: (c, 0, 0, 0)),
        compiler_params=PARAMS,
        cost_estimate=LIGHT,
        name="up_partial",
    )(*xs, *grads)


def down_kernel(act, g0, g1, g2, g3, shared, out):
    total = dot(act[...], stacked((g0, g1, g2, g3))).astype(jnp.bfloat16)
    rows = total.shape[0] // 8
    for d in range(8):
        for k in range(TILE // STRIP):
            strip = total[d * rows : (d + 1) * rows, k * STRIP : (k + 1) * STRIP]
            out[d, 0, k * rows : (k + 1) * rows, :] = strip


def down_partial(act, gs, shared):
    hidden, rows = act.shape
    width = gs[0].shape[1]
    tall = hidden // 8 * TILE // STRIP
    return pl.pallas_call(
        down_kernel,
        out_shape=jax.ShapeDtypeStruct(shared.shape, jnp.bfloat16),
        grid=(width // TILE,),
        in_specs=[pl.BlockSpec((hidden, rows), lambda c: (0, 0))]
        + [pl.BlockSpec((ROWS, TILE), lambda c: (0, c))] * SIDE
        + [pl.BlockSpec(memory_space=pl.ANY)],
        out_specs=pl.BlockSpec((8, 1, tall, STRIP), lambda c: (0, 1, c, 0)),
        input_output_aliases={5: 0},
        compiler_params=PARAMS,
        cost_estimate=LIGHT,
        name="down_partial",
    )(act, *gs, shared)


def widen_kernel(share, up, down):
    for half, out in ((0, up), (1, down)):
        rows = out.shape[1]
        for k in range(out.shape[2] // STRIP):
            strip = share[half, k * rows : (k + 1) * rows, :]
            out[0, :, k * STRIP : (k + 1) * STRIP] = strip.astype(jnp.float32)


def widen(share, up_shape, down_shape):
    return pl.pallas_call(
        widen_kernel,
        out_shape=(
            jax.ShapeDtypeStruct(up_shape, jnp.float32),
            jax.ShapeDtypeStruct(down_shape, jnp.float32),
        ),
        grid=(1,),
        in_specs=[pl.BlockSpec(share.shape, lambda c: (0, 0, 0))],
        out_specs=(
            pl.BlockSpec(up_shape, lambda c: (0, 0, 0)),
            pl.BlockSpec(down_shape, lambda c: (0, 0, 0)),
        ),
        compiler_params=PARAMS,
        cost_estimate=LIGHT,
        name="widen",
    )(share)


def parts_kernel(*refs):
    left, right, out = refs[:SIDE], refs[SIDE:-1], refs[-1]
    in_left = pl.program_id(0) < pl.num_programs(0) // 2

    @pl.when(in_left)
    def _():
        out[...] = sum(p[...].astype(jnp.float32) for p in left).astype(jnp.bfloat16)

    @pl.when(jnp.logical_not(in_left))
    def _():
        out[...] = sum(p[...].astype(jnp.float32) for p in right).astype(jnp.bfloat16)


def sum_parts(left, right):
    rows, width = left[0].shape
    tiles = width // TILE
    return pl.pallas_call(
        parts_kernel,
        out_shape=jax.ShapeDtypeStruct((rows, 2 * width), jnp.bfloat16),
        grid=(2 * tiles,),
        in_specs=[pl.BlockSpec((rows, TILE), lambda c: (0, jnp.minimum(c, tiles - 1)))] * SIDE
        + [pl.BlockSpec((rows, TILE), lambda c: (0, jnp.maximum(c - tiles, 0)))] * SIDE,
        out_specs=pl.BlockSpec((rows, TILE), lambda c: (0, c)),
        compiler_params=PARAMS,
        cost_estimate=LIGHT,
        name="sum_parts",
    )(*left, *right)


def after(value, *earlier):
    return lax.optimization_barrier((value, *earlier))[0]


def body(tokens, cotangent, expert_ids, route_weight, up_weight, down_weight):
    width = tokens.shape[1]
    up_matrix = up_weight[0]
    down_matrix = down_weight[0]
    dp = lax.axis_index("dp")
    core = dp & 1
    place = lax.axis_index("expert")
    y, x = place >> 2, place & 3
    shifts = jnp.array(OFFSETS, jnp.int32)
    dest = jnp.where(core == 1, y * SIDE + ((x + shifts) & 3), ((y + shifts) & 3) * SIDE + x)
    high = lax.reduce_precision(route_weight, 8, 7)
    middle = lax.reduce_precision(route_weight - high, 8, 7)
    low = route_weight - high - middle
    meta = jnp.concatenate(
        [m.astype(jnp.bfloat16).T for m in (expert_ids, high, middle, low)], axis=1
    )
    message = jnp.concatenate([tokens, jnp.pad(meta, ((0, 0), (0, width - 512)))], axis=0)

    with jax.named_scope("p1x"):
        token_blocks = [send(message, True, o) for o in OFFSETS]
    cotangent = after(cotangent, *token_blocks)
    with jax.named_scope("p1g"):
        cot_blocks = [send(cotangent, True, o) for o in OFFSETS]
    pick, put, weight = route(dest, token_blocks)

    out_x = select(pick, weight, token_blocks, False)
    with jax.named_scope("p2x"):
        rx = [send(r, False, o).reshape(ROWS, width) for r, o in zip(out_x, OFFSETS)]
    out_g = select(pick, weight, cot_blocks, True)
    with jax.named_scope("p2g"):
        rg = [send(r, False, o).reshape(ROWS, width) for r, o in zip(out_g[:3], OFFSETS)]
    pre, act = expert_pre(rx, up_matrix)
    with jax.named_scope("p2g2"):
        last = send(after(out_g[3], pre, *rx, *rg), False, OFFSETS[3]).reshape(ROWS, width)

    grad, rows = expert_back(rg, pre, 0, down_matrix, up_matrix)
    with jax.named_scope("r2"):
        returned = [send(r.reshape(SIDE, SLOTS, width), False, -o) for r, o in zip(rows, OFFSETS)]

    last = after(last, *rows)
    grad_last, (left, right) = expert_back([last], pre, 3, down_matrix, up_matrix)
    shared = up_partial(rx, [grad, grad_last])
    shared = after(shared, act, *returned)
    shared = down_partial(act, [*rg, last], shared)
    share = lax.psum_scatter(
        shared.reshape(-1, STRIP), "dp", scatter_dimension=0, tiled=True
    ).reshape(2, -1, STRIP)

    with jax.named_scope("r2l"):
        left = send(after(left, *returned).reshape(SIDE, SLOTS, -1), False, -OFFSETS[3])
    with jax.named_scope("r2r"):
        right = send(after(right, left).reshape(SIDE, SLOTS, -1), False, -OFFSETS[3])
    put = after(put, shared)
    with jax.named_scope("r1l"):
        parts = combine(put, returned, left, 0)
        left_parts = [send(p, True, -o) for p, o in zip(parts, OFFSETS)]
    with jax.named_scope("r1r"):
        parts = combine(put, returned, right, 1)
        right_parts = [send(p, True, -o) for p, o in zip(parts, OFFSETS)]
    token_grad = sum_parts(left_parts, right_parts)
    token_grad, share = lax.optimization_barrier((token_grad, share))
    up_grad, down_grad = widen(
        share, (1, width // 8, up_matrix.shape[1]), (1, down_matrix.shape[0] // 8, width)
    )
    return token_grad, up_grad, down_grad


def solution(mesh):
    rows = P(("dp", "expert"), None)
    weights = P("expert", None, None)
    return jax.shard_map(
        body,
        mesh=mesh,
        in_specs=(rows, rows, rows, rows, weights, weights),
        out_specs=(rows, P("expert", "dp", None), P("expert", "dp", None)),
        check_vma=False,
    )
```

```python
import functools

import jax
import jax.numpy as jnp
from jax import lax
from jax.experimental import pallas as pl
from jax.experimental.pallas import tpu as pltpu
from jax.sharding import PartitionSpec as P

SIDE = 4
OFFSETS = (0, 1, 3, 2)
SLOTS = 72
BOTH = ("dp", "expert")
TILE = 1024
ROWS = SIDE * SLOTS
WIDE = 3 * ROWS
COLS_LAST = (((1,), (1,)), ((), ()))
ROWS_FIRST = (((0,), (0,)), ((), ()))
VMEM_LIMIT = 58 * 1024 * 1024


def cost(m, k, n):
    return pl.CostEstimate(
        flops=2 * m * k * n, bytes_accessed=2 * (m * k + k * n + m * n), transcendentals=0
    )


HEAVY = pl.CostEstimate(flops=30_000_000_000, bytes_accessed=1, transcendentals=0)
LONGEST = pl.CostEstimate(flops=300_000_000_000, bytes_accessed=1, transcendentals=0)
LIGHT = pl.CostEstimate(flops=1_000_000, bytes_accessed=1, transcendentals=0)
PARAMS = pltpu.CompilerParams(vmem_limit_bytes=VMEM_LIMIT)


def ring(first, shift):
    pairs = []
    for dp in range(8):
        along_x = first == (dp % 2 == 0)
        for y in range(SIDE):
            for x in range(SIDE):
                to = y * SIDE + (x + shift) % SIDE if along_x else ((y + shift) % SIDE) * SIDE + x
                pairs.append((dp * 16 + y * SIDE + x, dp * 16 + to))
    return pairs


def send(value, first, shift):
    shift = shift % SIDE
    return value if shift == 0 else lax.ppermute(value, BOTH, ring(first, shift))


def route_kernel(dest_ref, m0, m1, m2, m3, pick_ref, put_ref, weight_ref):
    rows = lax.broadcasted_iota(jnp.int32, (16, 128), 0)
    masks = jnp.zeros((16, 128), jnp.float32)
    weights = []
    for i, meta in enumerate((m0, m1, m2, m3)):
        packed = meta[...].astype(jnp.float32)
        ids = packed[:, 0:128]
        route = packed[:, 128:256] + packed[:, 256:384] + packed[:, 384:512]
        for j in range(SIDE):
            hit = ids == dest_ref[j].astype(jnp.float32)
            mask = jnp.sum(jnp.where(hit, 1.0, 0.0), axis=0, keepdims=True)
            weights.append(jnp.sum(jnp.where(hit, route, 0.0), axis=0, keepdims=True))
            masks = jnp.where(rows == i * SIDE + j, mask, masks)
    before = lax.broadcasted_iota(jnp.int32, (128, 128), 0) < lax.broadcasted_iota(
        jnp.int32, (128, 128), 1
    )
    rank = jnp.dot(
        masks.astype(jnp.bfloat16),
        before.astype(jnp.float32).astype(jnp.bfloat16),
        preferred_element_type=jnp.float32,
    )
    rank = jnp.where(masks > 0.5, rank, -1.0)
    slot = lax.broadcasted_iota(jnp.int32, (SLOTS, 128), 0).astype(jnp.float32)
    for i in range(SIDE):
        for j in range(SIDE):
            n = i * SIDE + j
            pick = jnp.where(slot == rank[n : n + 1, :], 1.0, 0.0)
            pick_ref[i, j * SLOTS : (j + 1) * SLOTS, :] = pick.astype(jnp.bfloat16)
            put_ref[i, j, :, :] = pick.T.astype(jnp.bfloat16)
            column = jnp.sum(pick * weights[n], axis=1, keepdims=True)
            weight_ref[i, j * SLOTS : (j + 1) * SLOTS, :] = jnp.broadcast_to(column, (SLOTS, 128))


def route(dest, blocks):
    return pl.pallas_call(
        route_kernel,
        out_shape=(
            jax.ShapeDtypeStruct((SIDE, SIDE * SLOTS, 128), jnp.bfloat16),
            jax.ShapeDtypeStruct((SIDE, SIDE, 128, SLOTS), jnp.bfloat16),
            jax.ShapeDtypeStruct((SIDE, SIDE * SLOTS, 128), jnp.float32),
        ),
        grid=(1,),
        in_specs=[pl.BlockSpec(memory_space=pltpu.SMEM)]
        + [pl.BlockSpec((8, 512), lambda c: (16, 0))] * SIDE,
        out_specs=(
            pl.BlockSpec((SIDE, ROWS, 128), lambda c: (0, 0, 0)),
            pl.BlockSpec((SIDE, SIDE, 128, SLOTS), lambda c: (0, 0, 0, 0)),
            pl.BlockSpec((SIDE, ROWS, 128), lambda c: (0, 0, 0)),
        ),
        cost_estimate=LIGHT,
        name="route",
    )(dest, *blocks)


def select_kernel(scaled, pick_ref, weight_ref, *refs):
    blocks, outs = [r[...] for r in refs[:-SIDE]], refs[-SIDE:]
    if len(blocks) > SIDE:
        blocks[3:] = [jnp.concatenate(blocks[3:], axis=0)]
    for i, block in enumerate(blocks):
        rows = jnp.dot(pick_ref[i], block, preferred_element_type=jnp.float32)
        if scaled:
            rows = rows * weight_ref[i][:, 0:1]
        rows = rows.astype(jnp.bfloat16)
        for j in range(SIDE):
            outs[j][i, :, :] = rows[j * SLOTS : (j + 1) * SLOTS, :]


def select(pick, weight, blocks, scaled):
    width = blocks[0].shape[1]
    tile = TILE
    return pl.pallas_call(
        functools.partial(select_kernel, scaled),
        out_shape=(jax.ShapeDtypeStruct((SIDE, SLOTS, width), jnp.bfloat16),) * SIDE,
        grid=(width // tile,),
        in_specs=[
            pl.BlockSpec((SIDE, SIDE * SLOTS, 128), lambda c: (0, 0, 0)),
            pl.BlockSpec((SIDE, SIDE * SLOTS, 128), lambda c: (0, 0, 0)),
        ]
        + [pl.BlockSpec((min(b.shape[0], 128), tile), lambda c: (0, c)) for b in blocks],
        out_specs=(pl.BlockSpec((SIDE, SLOTS, tile), lambda c: (0, 0, c)),) * SIDE,
        compiler_params=PARAMS,
        cost_estimate=HEAVY,
        name="select_scaled" if scaled else "select",
    )(pick, weight, *blocks)


def combine_kernel(put_ref, r0, r1, r2, r3, o0, o1, o2, o3):
    returned = (r0, r1, r2, r3)
    for i, out in enumerate((o0, o1, o2, o3)):
        total = jnp.dot(put_ref[i, 0], r0[i], preferred_element_type=jnp.float32)
        for j in range(1, SIDE):
            total += jnp.dot(put_ref[i, j], returned[j][i], preferred_element_type=jnp.float32)
        out[...] = total.astype(jnp.bfloat16)


def combine(put, returned):
    width = returned[0].shape[2]
    tile = TILE
    return pl.pallas_call(
        combine_kernel,
        out_shape=(jax.ShapeDtypeStruct((128, width), jnp.bfloat16),) * SIDE,
        grid=(width // tile,),
        in_specs=[pl.BlockSpec((SIDE, SIDE, 128, SLOTS), lambda c: (0, 0, 0, 0))]
        + [pl.BlockSpec((SIDE, SLOTS, tile), lambda c: (0, 0, c))] * SIDE,
        out_specs=(pl.BlockSpec((128, tile), lambda c: (0, c)),) * SIDE,
        compiler_params=PARAMS,
        cost_estimate=LIGHT,
        name="combine",
    )(put, *returned)


def dot(a, b, dims=(((1,), (0,)), ((), ()))):
    return lax.dot_general(a, b, dims, preferred_element_type=jnp.float32)


def stacked(refs):
    return jnp.concatenate([r[...] for r in refs], axis=0)


def pre_kernel(*refs):
    xs, up, pre, act = refs[:SIDE], refs[SIDE], *refs[SIDE + 1 :]
    step = pl.program_id(0)
    part = dot(stacked(xs), up[...])

    @pl.when(step == 0)
    def _():
        pre[...] = part

    @pl.when(step > 0)
    def _():
        pre[...] += part

    @pl.when(step == pl.num_programs(0) - 1)
    def _():
        value = pre[...]
        act[...] = (value * jax.nn.sigmoid(value)).T.astype(jnp.bfloat16)


def expert_pre(xs, up):
    width, hidden = up.shape
    return pl.pallas_call(
        pre_kernel,
        out_shape=(
            jax.ShapeDtypeStruct((WIDE + ROWS, hidden), jnp.float32),
            jax.ShapeDtypeStruct((hidden, WIDE + ROWS), jnp.bfloat16),
        ),
        grid=(width // TILE,),
        in_specs=[pl.BlockSpec((ROWS, TILE), lambda c: (0, c))] * SIDE
        + [pl.BlockSpec((TILE, hidden), lambda c: (c, 0))],
        out_specs=(
            pl.BlockSpec((WIDE + ROWS, hidden), lambda c: (0, 0)),
            pl.BlockSpec((hidden, WIDE + ROWS), lambda c: (0, 0)),
        ),
        compiler_params=PARAMS,
        cost_estimate=cost(WIDE + ROWS, width, hidden),
        name="expert_pre",
    )(*xs, up)


def back_kernel(n, *refs):
    gs, pre, down, up, grad, rows, back = refs[:n], *refs[n : n + 4], refs[n + 4 : -1], refs[-1]
    step = pl.program_id(0)
    half = pl.num_programs(0) // 2

    @pl.when(step == 0)
    def _():
        back[...] = dot(stacked(gs), down[...], COLS_LAST)

    @pl.when(jnp.logical_and(step > 0, step < half))
    def _():
        back[...] += dot(stacked(gs), down[...], COLS_LAST)

    @pl.when(step == half - 1)
    def _():
        value = pre[...]
        sigma = jax.nn.sigmoid(value)
        grad[...] = (back[...] * sigma * (1.0 + value * (1.0 - sigma))).astype(jnp.bfloat16)

    @pl.when(step >= half)
    def _():
        out = dot(grad[...], up[...], COLS_LAST).astype(jnp.bfloat16)
        for i in range(n):
            rows[i][...] = out[i * ROWS : (i + 1) * ROWS, :]


def expert_back(gs, pre, place, down, up):
    n, (width, hidden) = len(gs), up.shape
    tiles = width // TILE
    out = pl.pallas_call(
        functools.partial(back_kernel, n),
        out_shape=(jax.ShapeDtypeStruct((n * ROWS, hidden), jnp.bfloat16),)
        + (jax.ShapeDtypeStruct((ROWS, width), jnp.bfloat16),) * n,
        grid=(2 * tiles,),
        in_specs=[pl.BlockSpec((ROWS, TILE), lambda c: (0, jnp.minimum(c, tiles - 1)))] * n
        + [
            pl.BlockSpec((n * ROWS, hidden), lambda c: (place, 0)),
            pl.BlockSpec((hidden, TILE), lambda c: (0, jnp.minimum(c, tiles - 1))),
            pl.BlockSpec((TILE, hidden), lambda c: (jnp.maximum(c - tiles, 0), 0)),
        ],
        out_specs=(pl.BlockSpec((n * ROWS, hidden), lambda c: (0, 0)),)
        + (pl.BlockSpec((ROWS, TILE), lambda c: (0, jnp.maximum(c - tiles, 0))),) * n,
        scratch_shapes=[pltpu.VMEM((n * ROWS, hidden), jnp.float32)],
        compiler_params=PARAMS,
        cost_estimate=cost(2 * n * ROWS, width, hidden) if n > 1 else LIGHT,
        name="expert_back",
    )(*gs, pre, down, up)
    return out[0], list(out[1:])


def up_kernel(x0, x1, x2, x3, grad, grad_last, out):
    total = dot(stacked((x0, x1, x2, x3)), stacked((grad, grad_last)), ROWS_FIRST)
    out[...] = total.astype(jnp.bfloat16)


def up_partial(xs, grads):
    width, hidden = xs[0].shape[1], grads[0].shape[1]
    return pl.pallas_call(
        up_kernel,
        out_shape=jax.ShapeDtypeStruct((width, hidden), jnp.bfloat16),
        grid=(width // TILE,),
        in_specs=[pl.BlockSpec((ROWS, TILE), lambda c: (0, c))] * SIDE
        + [pl.BlockSpec(g.shape, lambda c: (0, 0)) for g in grads],
        out_specs=pl.BlockSpec((TILE, hidden), lambda c: (c, 0)),
        compiler_params=PARAMS,
        cost_estimate=LONGEST,
        name="up_partial",
    )(*xs, *grads)


def down_kernel(act, g0, g1, g2, g3, out):
    out[...] = dot(act[...], stacked((g0, g1, g2, g3))).astype(jnp.bfloat16)


def down_partial(act, gs):
    hidden, rows = act.shape
    width = gs[0].shape[1]
    return pl.pallas_call(
        down_kernel,
        out_shape=jax.ShapeDtypeStruct((hidden, width), jnp.bfloat16),
        grid=(width // TILE,),
        in_specs=[pl.BlockSpec((hidden, rows), lambda c: (0, 0))]
        + [pl.BlockSpec((ROWS, TILE), lambda c: (0, c))] * SIDE,
        out_specs=pl.BlockSpec((hidden, TILE), lambda c: (0, c)),
        compiler_params=PARAMS,
        cost_estimate=LIGHT,
        name="down_partial",
    )(act, *gs)


def after(value, *earlier):
    return lax.optimization_barrier((value, *earlier))[0]


def body(tokens, cotangent, expert_ids, route_weight, up_weight, down_weight):
    width = tokens.shape[1]
    up_matrix = up_weight[0]
    down_matrix = down_weight[0]
    dp = lax.axis_index("dp")
    core = dp & 1
    place = lax.axis_index("expert")
    y, x = place >> 2, place & 3
    shifts = jnp.array(OFFSETS, jnp.int32)
    dest = jnp.where(core == 1, y * SIDE + ((x + shifts) & 3), ((y + shifts) & 3) * SIDE + x)
    high = lax.reduce_precision(route_weight, 8, 7)
    middle = lax.reduce_precision(route_weight - high, 8, 7)
    low = route_weight - high - middle
    meta = jnp.concatenate(
        [m.astype(jnp.bfloat16).T for m in (expert_ids, high, middle, low)], axis=1
    )
    message = jnp.concatenate([tokens, jnp.pad(meta, ((0, 0), (0, width - 512)))], axis=0)

    with jax.named_scope("p1x"):
        token_blocks = [send(message, True, o) for o in OFFSETS]
    cotangent = after(cotangent, *token_blocks)
    with jax.named_scope("p1g"):
        cot_blocks = [send(cotangent, True, o) for o in OFFSETS[:3]]
    pick, put, weight = route(dest, token_blocks)

    out_x = select(pick, weight, token_blocks, False)
    with jax.named_scope("p1f"):
        _, low, high = lax.optimization_barrier((out_x, cot_blocks[1], cot_blocks[2]))
        cot_blocks.append(send(low[:64], True, 1))
        cot_blocks.append(send(high[64:], True, -1))
    with jax.named_scope("p2x"):
        rx = [send(r, False, o).reshape(ROWS, width) for r, o in zip(out_x, OFFSETS)]
    out_g = select(pick, weight, cot_blocks, True)
    with jax.named_scope("p2g"):
        rg = [send(r, False, o).reshape(ROWS, width) for r, o in zip(out_g[:3], OFFSETS)]
    pre, act = expert_pre(rx, up_matrix)
    with jax.named_scope("p2g2"):
        last = send(after(out_g[3], pre, *rx, *rg), False, OFFSETS[3]).reshape(ROWS, width)

    grad, rows = expert_back(rg, pre, 0, down_matrix, up_matrix)
    with jax.named_scope("r2"):
        returned = [send(r.reshape(SIDE, SLOTS, width), False, -o) for r, o in zip(rows, OFFSETS)]

    last = after(last, *rows)
    down_part = down_partial(act, [*rg, last])
    down_grad = lax.psum_scatter(down_part, "dp", scatter_dimension=0, tiled=True)
    last = after(last, down_part)
    grad_last, rows_last = expert_back([last], pre, 3, down_matrix, up_matrix)
    with jax.named_scope("r2"):
        rows_last = after(rows_last[0], *returned).reshape(SIDE, SLOTS, width)
        returned.append(send(rows_last, False, -OFFSETS[3]))
    grad_last = after(grad_last, *returned[:3])
    up_part = up_partial(rx, [grad, grad_last])
    up_done, up_part = up_part, after(up_part, down_grad, returned[3])
    up_grad = lax.psum_scatter(up_part, "dp", scatter_dimension=0, tiled=True)

    parts = combine(after(put, up_done), returned)
    with jax.named_scope("r1"):
        parts = [send(p, True, -o) for p, o in zip(parts, OFFSETS)]
    token_grad = sum(p.astype(jnp.float32) for p in parts).astype(jnp.bfloat16)
    token_grad, up_grad = lax.optimization_barrier((token_grad, up_grad))
    return token_grad, up_grad.astype(jnp.float32)[None], down_grad.astype(jnp.float32)[None]


def solution(mesh):
    rows = P(("dp", "expert"), None)
    weights = P("expert", None, None)
    return jax.shard_map(
        body,
        mesh=mesh,
        in_specs=(rows, rows, rows, rows, weights, weights),
        out_specs=(rows, P("expert", "dp", None), P("expert", "dp", None)),
        check_vma=False,
    )
```

```python
import functools

import jax
import jax.numpy as jnp
from jax import lax
from jax.experimental import pallas as pl
from jax.experimental.pallas import tpu as pltpu
from jax.sharding import PartitionSpec as P

SIDE = 4
OFFSETS = (0, 1, 3, 2)
SLOTS = 72
BOTH = ("dp", "expert")
TILE = 1024
ROWS = SIDE * SLOTS
WIDE = 3 * ROWS
COLS_LAST = (((1,), (1,)), ((), ()))
ROWS_FIRST = (((0,), (0,)), ((), ()))
VMEM_LIMIT = 58 * 1024 * 1024


def cost(m, k, n):
    return pl.CostEstimate(
        flops=2 * m * k * n, bytes_accessed=2 * (m * k + k * n + m * n), transcendentals=0
    )


HEAVY = pl.CostEstimate(flops=30_000_000_000, bytes_accessed=1, transcendentals=0)
LONGEST = pl.CostEstimate(flops=300_000_000_000, bytes_accessed=1, transcendentals=0)
LIGHT = pl.CostEstimate(flops=1_000_000, bytes_accessed=1, transcendentals=0)
PARAMS = pltpu.CompilerParams(vmem_limit_bytes=VMEM_LIMIT)


def ring(first, shift):
    pairs = []
    for dp in range(8):
        along_x = first == (dp % 2 == 0)
        for y in range(SIDE):
            for x in range(SIDE):
                to = y * SIDE + (x + shift) % SIDE if along_x else ((y + shift) % SIDE) * SIDE + x
                pairs.append((dp * 16 + y * SIDE + x, dp * 16 + to))
    return pairs


def send(value, first, shift):
    shift = shift % SIDE
    return value if shift == 0 else lax.ppermute(value, BOTH, ring(first, shift))


def route_kernel(dest_ref, m0, m1, m2, m3, pick_ref, put_ref, weight_ref):
    rows = lax.broadcasted_iota(jnp.int32, (16, 128), 0)
    masks = jnp.zeros((16, 128), jnp.float32)
    weights = []
    for i, meta in enumerate((m0, m1, m2, m3)):
        packed = meta[...].astype(jnp.float32)
        ids = packed[:, 0:128]
        route = packed[:, 128:256] + packed[:, 256:384] + packed[:, 384:512]
        for j in range(SIDE):
            hit = ids == dest_ref[j].astype(jnp.float32)
            mask = jnp.sum(jnp.where(hit, 1.0, 0.0), axis=0, keepdims=True)
            weights.append(jnp.sum(jnp.where(hit, route, 0.0), axis=0, keepdims=True))
            masks = jnp.where(rows == i * SIDE + j, mask, masks)
    before = lax.broadcasted_iota(jnp.int32, (128, 128), 0) < lax.broadcasted_iota(
        jnp.int32, (128, 128), 1
    )
    rank = jnp.dot(
        masks.astype(jnp.bfloat16),
        before.astype(jnp.float32).astype(jnp.bfloat16),
        preferred_element_type=jnp.float32,
    )
    rank = jnp.where(masks > 0.5, rank, -1.0)
    slot = lax.broadcasted_iota(jnp.int32, (SLOTS, 128), 0).astype(jnp.float32)
    for i in range(SIDE):
        for j in range(SIDE):
            n = i * SIDE + j
            pick = jnp.where(slot == rank[n : n + 1, :], 1.0, 0.0)
            pick_ref[i, j * SLOTS : (j + 1) * SLOTS, :] = pick.astype(jnp.bfloat16)
            put_ref[i, j, :, :] = pick.T.astype(jnp.bfloat16)
            column = jnp.sum(pick * weights[n], axis=1, keepdims=True)
            weight_ref[i, j * SLOTS : (j + 1) * SLOTS, :] = jnp.broadcast_to(column, (SLOTS, 128))


def route(dest, blocks):
    return pl.pallas_call(
        route_kernel,
        out_shape=(
            jax.ShapeDtypeStruct((SIDE, SIDE * SLOTS, 128), jnp.bfloat16),
            jax.ShapeDtypeStruct((SIDE, SIDE, 128, SLOTS), jnp.bfloat16),
            jax.ShapeDtypeStruct((SIDE, SIDE * SLOTS, 128), jnp.float32),
        ),
        grid=(1,),
        in_specs=[pl.BlockSpec(memory_space=pltpu.SMEM)]
        + [pl.BlockSpec((8, 512), lambda c: (16, 0))] * 3
        + [pl.BlockSpec((8, 512), lambda c: (8, 0))],
        out_specs=(
            pl.BlockSpec((SIDE, ROWS, 128), lambda c: (0, 0, 0)),
            pl.BlockSpec((SIDE, SIDE, 128, SLOTS), lambda c: (0, 0, 0, 0)),
            pl.BlockSpec((SIDE, ROWS, 128), lambda c: (0, 0, 0)),
        ),
        cost_estimate=LIGHT,
        name="route",
    )(dest, *blocks)


def select_kernel(scaled, pick_ref, weight_ref, *refs):
    blocks, outs = [r[...] for r in refs[:-SIDE]], refs[-SIDE:]
    if len(blocks) > SIDE:
        blocks[3:] = [jnp.concatenate(blocks[3:], axis=0)]
    for i, block in enumerate(blocks):
        rows = jnp.dot(pick_ref[i], block, preferred_element_type=jnp.float32)
        if scaled:
            rows = rows * weight_ref[i][:, 0:1]
        rows = rows.astype(jnp.bfloat16)
        for j in range(SIDE):
            outs[j][i, :, :] = rows[j * SLOTS : (j + 1) * SLOTS, :]


def select(pick, weight, blocks, scaled):
    width = blocks[0].shape[1]
    tile = TILE
    return pl.pallas_call(
        functools.partial(select_kernel, scaled),
        out_shape=(jax.ShapeDtypeStruct((SIDE, SLOTS, width), jnp.bfloat16),) * SIDE,
        grid=(width // tile,),
        in_specs=[
            pl.BlockSpec((SIDE, SIDE * SLOTS, 128), lambda c: (0, 0, 0)),
            pl.BlockSpec((SIDE, SIDE * SLOTS, 128), lambda c: (0, 0, 0)),
        ]
        + [pl.BlockSpec((b.shape[0] // 64 * 64, tile), lambda c: (0, c)) for b in blocks],
        out_specs=(pl.BlockSpec((SIDE, SLOTS, tile), lambda c: (0, 0, c)),) * SIDE,
        compiler_params=PARAMS,
        cost_estimate=HEAVY,
        name="select_scaled" if scaled else "select",
    )(pick, weight, *blocks)


def combine_kernel(put_ref, r0, r1, r2, r3, o0, o1, o2, o3):
    returned = (r0, r1, r2, r3)
    for i, out in enumerate((o0, o1, o2, o3)):
        total = jnp.dot(put_ref[i, 0], r0[i], preferred_element_type=jnp.float32)
        for j in range(1, SIDE):
            total += jnp.dot(put_ref[i, j], returned[j][i], preferred_element_type=jnp.float32)
        out[...] = total.astype(jnp.bfloat16)


def combine(put, returned):
    width = returned[0].shape[2]
    tile = TILE
    return pl.pallas_call(
        combine_kernel,
        out_shape=(jax.ShapeDtypeStruct((128, width), jnp.bfloat16),) * SIDE,
        grid=(width // tile,),
        in_specs=[pl.BlockSpec((SIDE, SIDE, 128, SLOTS), lambda c: (0, 0, 0, 0))]
        + [pl.BlockSpec((SIDE, SLOTS, tile), lambda c: (0, 0, c))] * SIDE,
        out_specs=(pl.BlockSpec((128, tile), lambda c: (0, c)),) * SIDE,
        compiler_params=PARAMS,
        cost_estimate=LIGHT,
        name="combine",
    )(put, *returned)


def dot(a, b, dims=(((1,), (0,)), ((), ()))):
    return lax.dot_general(a, b, dims, preferred_element_type=jnp.float32)


def stacked(refs):
    return jnp.concatenate([r[...] for r in refs], axis=0)


def pre_kernel(*refs):
    xs, up, pre, act = refs[:SIDE], refs[SIDE], *refs[SIDE + 1 :]
    step = pl.program_id(0)
    part = dot(stacked(xs), up[...])

    @pl.when(step == 0)
    def _():
        pre[...] = part

    @pl.when(step > 0)
    def _():
        pre[...] += part

    @pl.when(step == pl.num_programs(0) - 1)
    def _():
        value = pre[...]
        act[...] = (value * jax.nn.sigmoid(value)).T.astype(jnp.bfloat16)


def expert_pre(xs, up):
    width, hidden = up.shape
    return pl.pallas_call(
        pre_kernel,
        out_shape=(
            jax.ShapeDtypeStruct((WIDE + ROWS, hidden), jnp.float32),
            jax.ShapeDtypeStruct((hidden, WIDE + ROWS), jnp.bfloat16),
        ),
        grid=(width // TILE,),
        in_specs=[pl.BlockSpec((ROWS, TILE), lambda c: (0, c))] * SIDE
        + [pl.BlockSpec((TILE, hidden), lambda c: (c, 0))],
        out_specs=(
            pl.BlockSpec((WIDE + ROWS, hidden), lambda c: (0, 0)),
            pl.BlockSpec((hidden, WIDE + ROWS), lambda c: (0, 0)),
        ),
        compiler_params=PARAMS,
        cost_estimate=cost(WIDE + ROWS, width, hidden),
        name="expert_pre",
    )(*xs, up)


def back_kernel(n, *refs):
    gs, pre, down, up, grad, rows, back = refs[:n], *refs[n : n + 4], refs[n + 4 : -1], refs[-1]
    step = pl.program_id(0)
    half = pl.num_programs(0) // 2

    @pl.when(step == 0)
    def _():
        back[...] = dot(stacked(gs), down[...], COLS_LAST)

    @pl.when(jnp.logical_and(step > 0, step < half))
    def _():
        back[...] += dot(stacked(gs), down[...], COLS_LAST)

    @pl.when(step == half - 1)
    def _():
        value = pre[...]
        sigma = jax.nn.sigmoid(value)
        grad[...] = (back[...] * sigma * (1.0 + value * (1.0 - sigma))).astype(jnp.bfloat16)

    @pl.when(step >= half)
    def _():
        out = dot(grad[...], up[...], COLS_LAST).astype(jnp.bfloat16)
        for i in range(n):
            rows[i][...] = out[i * ROWS : (i + 1) * ROWS, :]


def expert_back(gs, pre, place, down, up):
    n, (width, hidden) = len(gs), up.shape
    tiles = width // TILE
    out = pl.pallas_call(
        functools.partial(back_kernel, n),
        out_shape=(jax.ShapeDtypeStruct((n * ROWS, hidden), jnp.bfloat16),)
        + (jax.ShapeDtypeStruct((ROWS, width), jnp.bfloat16),) * n,
        grid=(2 * tiles,),
        in_specs=[pl.BlockSpec((ROWS, TILE), lambda c: (0, jnp.minimum(c, tiles - 1)))] * n
        + [
            pl.BlockSpec((n * ROWS, hidden), lambda c: (place, 0)),
            pl.BlockSpec((hidden, TILE), lambda c: (0, jnp.minimum(c, tiles - 1))),
            pl.BlockSpec((TILE, hidden), lambda c: (jnp.maximum(c - tiles, 0), 0)),
        ],
        out_specs=(pl.BlockSpec((n * ROWS, hidden), lambda c: (0, 0)),)
        + (pl.BlockSpec((ROWS, TILE), lambda c: (0, jnp.maximum(c - tiles, 0))),) * n,
        scratch_shapes=[pltpu.VMEM((n * ROWS, hidden), jnp.float32)],
        compiler_params=PARAMS,
        cost_estimate=cost(2 * n * ROWS, width, hidden) if n > 1 else LIGHT,
        name="expert_back",
    )(*gs, pre, down, up)
    return out[0], list(out[1:])


def up_kernel(x0, x1, x2, x3, grad, grad_last, out):
    total = dot(stacked((x0, x1, x2, x3)), stacked((grad, grad_last)), ROWS_FIRST)
    out[...] = total.astype(jnp.bfloat16)


def up_partial(xs, grads):
    width, hidden = xs[0].shape[1], grads[0].shape[1]
    return pl.pallas_call(
        up_kernel,
        out_shape=jax.ShapeDtypeStruct((width, hidden), jnp.bfloat16),
        grid=(width // TILE,),
        in_specs=[pl.BlockSpec((ROWS, TILE), lambda c: (0, c))] * SIDE
        + [pl.BlockSpec(g.shape, lambda c: (0, 0)) for g in grads],
        out_specs=pl.BlockSpec((TILE, hidden), lambda c: (c, 0)),
        compiler_params=PARAMS,
        cost_estimate=LONGEST,
        name="up_partial",
    )(*xs, *grads)


def down_kernel(act, g0, g1, g2, g3, out):
    out[...] = dot(act[...], stacked((g0, g1, g2, g3))).astype(jnp.bfloat16)


def down_partial(act, gs):
    hidden, rows = act.shape
    width = gs[0].shape[1]
    return pl.pallas_call(
        down_kernel,
        out_shape=jax.ShapeDtypeStruct((hidden, width), jnp.bfloat16),
        grid=(width // TILE,),
        in_specs=[pl.BlockSpec((hidden, rows), lambda c: (0, 0))]
        + [pl.BlockSpec((ROWS, TILE), lambda c: (0, c))] * SIDE,
        out_specs=pl.BlockSpec((hidden, TILE), lambda c: (0, c)),
        compiler_params=PARAMS,
        cost_estimate=LIGHT,
        name="down_partial",
    )(act, *gs)


def after(value, *earlier):
    return lax.optimization_barrier((value, *earlier))[0]


def body(tokens, cotangent, expert_ids, route_weight, up_weight, down_weight):
    width = tokens.shape[1]
    up_matrix = up_weight[0]
    down_matrix = down_weight[0]
    dp = lax.axis_index("dp")
    core = dp & 1
    place = lax.axis_index("expert")
    y, x = place >> 2, place & 3
    shifts = jnp.array(OFFSETS, jnp.int32)
    dest = jnp.where(core == 1, y * SIDE + ((x + shifts) & 3), ((y + shifts) & 3) * SIDE + x)
    first = lax.reduce_precision(route_weight, 8, 7)
    second = lax.reduce_precision(route_weight - first, 8, 7)
    third = route_weight - first - second
    meta = jnp.concatenate(
        [m.astype(jnp.bfloat16).T for m in (expert_ids, first, second, third)], axis=1
    )
    message = jnp.concatenate([tokens, jnp.pad(meta, ((0, 0), (0, width - 512)))], axis=0)

    with jax.named_scope("p1x"):
        token_blocks = [send(message, True, o) for o in OFFSETS[:3]]
    with jax.named_scope("p1f"):
        low, high = token_blocks[1][:64], token_blocks[2][64:]
        token_blocks += [send(low, True, 1), send(high, True, -1)]
    cotangent = after(cotangent, *token_blocks[:3])
    with jax.named_scope("p1g"):
        cot_blocks = [send(cotangent, True, o) for o in OFFSETS]
    pick, put, weight = route(dest, [*token_blocks[:3], token_blocks[4]])

    out_x = select(pick, weight, token_blocks, False)
    with jax.named_scope("p2x"):
        rx = [send(r, False, o).reshape(ROWS, width) for r, o in zip(out_x, OFFSETS)]
    out_g = select(pick, weight, cot_blocks, True)
    with jax.named_scope("p2g"):
        rg = [send(r, False, o).reshape(ROWS, width) for r, o in zip(out_g[:3], OFFSETS)]
    pre, act = expert_pre(rx, up_matrix)
    with jax.named_scope("p2g2"):
        last = send(after(out_g[3], pre, *rx, *rg), False, OFFSETS[3]).reshape(ROWS, width)

    grad, rows = expert_back(rg, pre, 0, down_matrix, up_matrix)
    with jax.named_scope("r2"):
        returned = [send(r.reshape(SIDE, SLOTS, width), False, -o) for r, o in zip(rows, OFFSETS)]

    last = after(last, *rows)
    down_part = down_partial(act, [*rg, last])
    down_grad = lax.psum_scatter(down_part, "dp", scatter_dimension=0, tiled=True)
    last = after(last, down_part)
    grad_last, rows_last = expert_back([last], pre, 3, down_matrix, up_matrix)
    with jax.named_scope("r2"):
        rows_last = after(rows_last[0], *returned).reshape(SIDE, SLOTS, width)
        returned.append(send(rows_last, False, -OFFSETS[3]))
    grad_last = after(grad_last, *returned[:3])
    up_part = up_partial(rx, [grad, grad_last])
    up_done, up_part = up_part, after(up_part, down_grad, returned[3])
    up_grad = lax.psum_scatter(up_part, "dp", scatter_dimension=0, tiled=True)

    parts = combine(after(put, up_done), returned)
    with jax.named_scope("r1"):
        parts = [send(p, True, -o) for p, o in zip(parts, OFFSETS)]
    token_grad = sum(p.astype(jnp.float32) for p in parts).astype(jnp.bfloat16)
    token_grad, up_grad = lax.optimization_barrier((token_grad, up_grad))
    return token_grad, up_grad.astype(jnp.float32)[None], down_grad.astype(jnp.float32)[None]


def solution(mesh):
    rows = P(("dp", "expert"), None)
    weights = P("expert", None, None)
    return jax.shard_map(
        body,
        mesh=mesh,
        in_specs=(rows, rows, rows, rows, weights, weights),
        out_specs=(rows, P("expert", "dp", None), P("expert", "dp", None)),
        check_vma=False,
    )
```

```python
import functools

import jax
import jax.numpy as jnp
from jax import lax
from jax.experimental import pallas as pl
from jax.experimental.pallas import tpu as pltpu
from jax.sharding import PartitionSpec as P

SIDE = 4
OFFSETS = (0, 1, 3, 2)
SLOTS = 72
BOTH = ("dp", "expert")
TILE = 1024
ROWS = SIDE * SLOTS
WIDE = 3 * ROWS
COLS_LAST = (((1,), (1,)), ((), ()))
ROWS_FIRST = (((0,), (0,)), ((), ()))
VMEM_LIMIT = 58 * 1024 * 1024


def cost(m, k, n):
    return pl.CostEstimate(
        flops=2 * m * k * n, bytes_accessed=2 * (m * k + k * n + m * n), transcendentals=0
    )


HEAVY = pl.CostEstimate(flops=30_000_000_000, bytes_accessed=1, transcendentals=0)
LONGEST = pl.CostEstimate(flops=300_000_000_000, bytes_accessed=1, transcendentals=0)
LIGHT = pl.CostEstimate(flops=1_000_000, bytes_accessed=1, transcendentals=0)
PARAMS = pltpu.CompilerParams(vmem_limit_bytes=VMEM_LIMIT)


def ring(first, shift):
    pairs = []
    for dp in range(8):
        along_x = first == (dp % 2 == 0)
        for y in range(SIDE):
            for x in range(SIDE):
                to = y * SIDE + (x + shift) % SIDE if along_x else ((y + shift) % SIDE) * SIDE + x
                pairs.append((dp * 16 + y * SIDE + x, dp * 16 + to))
    return pairs


def send(value, first, shift):
    shift = shift % SIDE
    return value if shift == 0 else lax.ppermute(value, BOTH, ring(first, shift))


def route_kernel(dest_ref, m0, m1, m2, m3, pick_ref, put_ref, weight_ref):
    rows = lax.broadcasted_iota(jnp.int32, (16, 128), 0)
    masks = jnp.zeros((16, 128), jnp.float32)
    weights = []
    for i, meta in enumerate((m0, m1, m2, m3)):
        packed = meta[...].astype(jnp.float32)
        ids = packed[:, 0:128]
        route = packed[:, 128:256] + packed[:, 256:384] + packed[:, 384:512]
        for j in range(SIDE):
            hit = ids == dest_ref[j].astype(jnp.float32)
            mask = jnp.sum(jnp.where(hit, 1.0, 0.0), axis=0, keepdims=True)
            weights.append(jnp.sum(jnp.where(hit, route, 0.0), axis=0, keepdims=True))
            masks = jnp.where(rows == i * SIDE + j, mask, masks)
    before = lax.broadcasted_iota(jnp.int32, (128, 128), 0) < lax.broadcasted_iota(
        jnp.int32, (128, 128), 1
    )
    rank = jnp.dot(
        masks.astype(jnp.bfloat16),
        before.astype(jnp.float32).astype(jnp.bfloat16),
        preferred_element_type=jnp.float32,
    )
    rank = jnp.where(masks > 0.5, rank, -1.0)
    slot = lax.broadcasted_iota(jnp.int32, (SLOTS, 128), 0).astype(jnp.float32)
    for i in range(SIDE):
        for j in range(SIDE):
            n = i * SIDE + j
            pick = jnp.where(slot == rank[n : n + 1, :], 1.0, 0.0)
            pick_ref[i, j * SLOTS : (j + 1) * SLOTS, :] = pick.astype(jnp.bfloat16)
            put_ref[i, j, :, :] = pick.T.astype(jnp.bfloat16)
            column = jnp.sum(pick * weights[n], axis=1, keepdims=True)
            weight_ref[i, j * SLOTS : (j + 1) * SLOTS, :] = jnp.broadcast_to(column, (SLOTS, 128))


def route(dest, blocks):
    return pl.pallas_call(
        route_kernel,
        out_shape=(
            jax.ShapeDtypeStruct((SIDE, SIDE * SLOTS, 128), jnp.bfloat16),
            jax.ShapeDtypeStruct((SIDE, SIDE, 128, SLOTS), jnp.bfloat16),
            jax.ShapeDtypeStruct((SIDE, SIDE * SLOTS, 128), jnp.float32),
        ),
        grid=(1,),
        in_specs=[pl.BlockSpec(memory_space=pltpu.SMEM)]
        + [pl.BlockSpec((8, 512), lambda c: (16, 0))] * 3
        + [pl.BlockSpec((8, 512), lambda c: (8, 0))],
        out_specs=(
            pl.BlockSpec((SIDE, ROWS, 128), lambda c: (0, 0, 0)),
            pl.BlockSpec((SIDE, SIDE, 128, SLOTS), lambda c: (0, 0, 0, 0)),
            pl.BlockSpec((SIDE, ROWS, 128), lambda c: (0, 0, 0)),
        ),
        cost_estimate=LIGHT,
        name="route",
    )(dest, *blocks)


def select_kernel(scaled, pick_ref, weight_ref, *refs):
    blocks, outs = [r[...] for r in refs[:-SIDE]], refs[-SIDE:]
    if len(blocks) > SIDE:
        blocks[3:] = [jnp.concatenate(blocks[3:], axis=0)]
    for i, block in enumerate(blocks):
        rows = jnp.dot(pick_ref[i], block, preferred_element_type=jnp.float32)
        if scaled:
            rows = rows * weight_ref[i][:, 0:1]
        rows = rows.astype(jnp.bfloat16)
        for j in range(SIDE):
            outs[j][i, :, :] = rows[j * SLOTS : (j + 1) * SLOTS, :]


def select(pick, weight, blocks, scaled):
    width = blocks[0].shape[1]
    tile = TILE
    return pl.pallas_call(
        functools.partial(select_kernel, scaled),
        out_shape=(jax.ShapeDtypeStruct((SIDE, SLOTS, width), jnp.bfloat16),) * SIDE,
        grid=(width // tile,),
        in_specs=[
            pl.BlockSpec((SIDE, SIDE * SLOTS, 128), lambda c: (0, 0, 0)),
            pl.BlockSpec((SIDE, SIDE * SLOTS, 128), lambda c: (0, 0, 0)),
        ]
        + [pl.BlockSpec((b.shape[0] // 64 * 64, tile), lambda c: (0, c)) for b in blocks],
        out_specs=(pl.BlockSpec((SIDE, SLOTS, tile), lambda c: (0, 0, c)),) * SIDE,
        compiler_params=PARAMS,
        cost_estimate=HEAVY,
        name="select_scaled" if scaled else "select",
    )(pick, weight, *blocks)


def combine_kernel(put_ref, r0, r1, r2, r3, o0, o1, o2, o3):
    returned = (r0, r1, r2, r3)
    for i, out in enumerate((o0, o1, o2, o3)):
        total = jnp.dot(put_ref[i, 0], r0[i], preferred_element_type=jnp.float32)
        for j in range(1, SIDE):
            total += jnp.dot(put_ref[i, j], returned[j][i], preferred_element_type=jnp.float32)
        out[...] = total.astype(jnp.bfloat16)


def combine(put, returned):
    width = returned[0].shape[2]
    tile = TILE
    return pl.pallas_call(
        combine_kernel,
        out_shape=(jax.ShapeDtypeStruct((128, width), jnp.bfloat16),) * SIDE,
        grid=(width // tile,),
        in_specs=[pl.BlockSpec((SIDE, SIDE, 128, SLOTS), lambda c: (0, 0, 0, 0))]
        + [pl.BlockSpec((SIDE, SLOTS, tile), lambda c: (0, 0, c))] * SIDE,
        out_specs=(pl.BlockSpec((128, tile), lambda c: (0, c)),) * SIDE,
        compiler_params=PARAMS,
        cost_estimate=LIGHT,
        name="combine",
    )(put, *returned)


def dot(a, b, dims=(((1,), (0,)), ((), ()))):
    return lax.dot_general(a, b, dims, preferred_element_type=jnp.float32)


def stacked(refs):
    return jnp.concatenate([r[...] for r in refs], axis=0)


def pre_kernel(*refs):
    xs, up, pre, act = refs[:SIDE], refs[SIDE], *refs[SIDE + 1 :]
    step = pl.program_id(0)
    part = dot(stacked(xs), up[...])

    @pl.when(step == 0)
    def _():
        pre[...] = part

    @pl.when(step > 0)
    def _():
        pre[...] += part

    @pl.when(step == pl.num_programs(0) - 1)
    def _():
        value = pre[...]
        act[...] = (value * jax.nn.sigmoid(value)).T.astype(jnp.bfloat16)


def expert_pre(xs, up):
    width, hidden = up.shape
    return pl.pallas_call(
        pre_kernel,
        out_shape=(
            jax.ShapeDtypeStruct((WIDE + ROWS, hidden), jnp.float32),
            jax.ShapeDtypeStruct((hidden, WIDE + ROWS), jnp.bfloat16),
        ),
        grid=(width // TILE,),
        in_specs=[pl.BlockSpec((ROWS, TILE), lambda c: (0, c))] * SIDE
        + [pl.BlockSpec((TILE, hidden), lambda c: (c, 0))],
        out_specs=(
            pl.BlockSpec((WIDE + ROWS, hidden), lambda c: (0, 0)),
            pl.BlockSpec((hidden, WIDE + ROWS), lambda c: (0, 0)),
        ),
        compiler_params=PARAMS,
        cost_estimate=cost(WIDE + ROWS, width, hidden),
        name="expert_pre",
    )(*xs, up)


def back_kernel(n, *refs):
    gs, pre, down, up, grad, rows, back = refs[:n], *refs[n : n + 4], refs[n + 4 : -1], refs[-1]
    step = pl.program_id(0)
    half = pl.num_programs(0) // 2

    @pl.when(step == 0)
    def _():
        back[...] = dot(stacked(gs), down[...], COLS_LAST)

    @pl.when(jnp.logical_and(step > 0, step < half))
    def _():
        back[...] += dot(stacked(gs), down[...], COLS_LAST)

    @pl.when(step == half - 1)
    def _():
        value = pre[...]
        sigma = jax.nn.sigmoid(value)
        grad[...] = (back[...] * sigma * (1.0 + value * (1.0 - sigma))).astype(jnp.bfloat16)

    @pl.when(step >= half)
    def _():
        out = dot(grad[...], up[...], COLS_LAST).astype(jnp.bfloat16)
        for i in range(n):
            rows[i][...] = out[i * ROWS : (i + 1) * ROWS, :]


def expert_back(gs, pre, place, down, up):
    n, (width, hidden) = len(gs), up.shape
    tiles = width // TILE
    out = pl.pallas_call(
        functools.partial(back_kernel, n),
        out_shape=(jax.ShapeDtypeStruct((n * ROWS, hidden), jnp.bfloat16),)
        + (jax.ShapeDtypeStruct((ROWS, width), jnp.bfloat16),) * n,
        grid=(2 * tiles,),
        in_specs=[pl.BlockSpec((ROWS, TILE), lambda c: (0, jnp.minimum(c, tiles - 1)))] * n
        + [
            pl.BlockSpec((n * ROWS, hidden), lambda c: (place, 0)),
            pl.BlockSpec((hidden, TILE), lambda c: (0, jnp.minimum(c, tiles - 1))),
            pl.BlockSpec((TILE, hidden), lambda c: (jnp.maximum(c - tiles, 0), 0)),
        ],
        out_specs=(pl.BlockSpec((n * ROWS, hidden), lambda c: (0, 0)),)
        + (pl.BlockSpec((ROWS, TILE), lambda c: (0, jnp.maximum(c - tiles, 0))),) * n,
        scratch_shapes=[pltpu.VMEM((n * ROWS, hidden), jnp.float32)],
        compiler_params=PARAMS,
        cost_estimate=cost(2 * n * ROWS, width, hidden) if n > 1 else LIGHT,
        name="expert_back",
    )(*gs, pre, down, up)
    return out[0], list(out[1:])


def up_kernel(x0, x1, x2, x3, grad, grad_last, out):
    total = dot(stacked((x0, x1, x2, x3)), stacked((grad, grad_last)), ROWS_FIRST)
    out[...] = total.astype(jnp.bfloat16)


def up_partial(xs, grads):
    width, hidden = xs[0].shape[1], grads[0].shape[1]
    return pl.pallas_call(
        up_kernel,
        out_shape=jax.ShapeDtypeStruct((width, hidden), jnp.bfloat16),
        grid=(width // TILE,),
        in_specs=[pl.BlockSpec((ROWS, TILE), lambda c: (0, c))] * SIDE
        + [pl.BlockSpec(g.shape, lambda c: (0, 0)) for g in grads],
        out_specs=pl.BlockSpec((TILE, hidden), lambda c: (c, 0)),
        compiler_params=PARAMS,
        cost_estimate=LONGEST,
        name="up_partial",
    )(*xs, *grads)


def down_kernel(act, g0, g1, g2, g3, out):
    out[...] = dot(act[...], stacked((g0, g1, g2, g3))).astype(jnp.bfloat16)


def down_partial(act, gs):
    hidden, rows = act.shape
    width = gs[0].shape[1]
    return pl.pallas_call(
        down_kernel,
        out_shape=jax.ShapeDtypeStruct((hidden, width), jnp.bfloat16),
        grid=(width // TILE,),
        in_specs=[pl.BlockSpec((hidden, rows), lambda c: (0, 0))]
        + [pl.BlockSpec((ROWS, TILE), lambda c: (0, c))] * SIDE,
        out_specs=pl.BlockSpec((hidden, TILE), lambda c: (0, c)),
        compiler_params=PARAMS,
        cost_estimate=LIGHT,
        name="down_partial",
    )(act, *gs)


def after(value, *earlier):
    return lax.optimization_barrier((value, *earlier))[0]


def body(tokens, cotangent, expert_ids, route_weight, up_weight, down_weight):
    width = tokens.shape[1]
    up_matrix = up_weight[0]
    down_matrix = down_weight[0]
    dp = lax.axis_index("dp")
    core = dp & 1
    place = lax.axis_index("expert")
    y, x = place >> 2, place & 3
    shifts = jnp.array(OFFSETS, jnp.int32)
    dest = jnp.where(core == 1, y * SIDE + ((x + shifts) & 3), ((y + shifts) & 3) * SIDE + x)
    first = lax.reduce_precision(route_weight, 8, 7)
    second = lax.reduce_precision(route_weight - first, 8, 7)
    third = route_weight - first - second
    meta = jnp.concatenate(
        [m.astype(jnp.bfloat16).T for m in (expert_ids, first, second, third)], axis=1
    )
    message = jnp.concatenate([tokens, jnp.pad(meta, ((0, 0), (0, width - 512)))], axis=0)

    with jax.named_scope("p1x"):
        token_blocks = [send(message, True, o) for o in OFFSETS[:3]]
    with jax.named_scope("p1f"):
        low, high = token_blocks[1][:64], token_blocks[2][64:]
        token_blocks += [send(low, True, 1), send(high, True, -1)]
    cotangent = after(cotangent, *token_blocks)
    with jax.named_scope("p1g"):
        cot_blocks = [send(cotangent, True, o) for o in OFFSETS]
    pick, put, weight = route(dest, [*token_blocks[:3], token_blocks[4]])

    out_x = select(pick, weight, token_blocks, False)
    with jax.named_scope("p2x"):
        rx = [send(r, False, o).reshape(ROWS, width) for r, o in zip(out_x, OFFSETS)]
    out_g = select(pick, weight, cot_blocks, True)
    with jax.named_scope("p2g"):
        rg = [send(r, False, o).reshape(ROWS, width) for r, o in zip(out_g[:3], OFFSETS)]
    pre, act = expert_pre(rx, up_matrix)
    with jax.named_scope("p2g2"):
        last = send(after(out_g[3], pre, *rx, *rg), False, OFFSETS[3]).reshape(ROWS, width)

    grad, rows = expert_back(rg, pre, 0, down_matrix, up_matrix)
    with jax.named_scope("r2"):
        returned = [send(r.reshape(SIDE, SLOTS, width), False, -o) for r, o in zip(rows, OFFSETS)]

    last = after(last, *rows)
    down_part = down_partial(act, [*rg, last])
    down_grad = lax.psum_scatter(down_part, "dp", scatter_dimension=0, tiled=True)
    last = after(last, down_part)
    grad_last, rows_last = expert_back([last], pre, 3, down_matrix, up_matrix)
    with jax.named_scope("r2"):
        rows_last = after(rows_last[0], *returned).reshape(SIDE, SLOTS, width)
        returned.append(send(rows_last, False, -OFFSETS[3]))
    grad_last = after(grad_last, *returned[:3])
    up_part = up_partial(rx, [grad, grad_last])
    up_done, up_part = up_part, after(up_part, down_grad, returned[3])
    up_grad = lax.psum_scatter(up_part, "dp", scatter_dimension=0, tiled=True)

    parts = combine(after(put, up_done), returned)
    with jax.named_scope("r1"):
        parts = [send(p, True, -o) for p, o in zip(parts, OFFSETS)]
    token_grad = sum(p.astype(jnp.float32) for p in parts).astype(jnp.bfloat16)
    token_grad, up_grad = lax.optimization_barrier((token_grad, up_grad))
    return token_grad, up_grad.astype(jnp.float32)[None], down_grad.astype(jnp.float32)[None]


def solution(mesh):
    rows = P(("dp", "expert"), None)
    weights = P("expert", None, None)
    return jax.shard_map(
        body,
        mesh=mesh,
        in_specs=(rows, rows, rows, rows, weights, weights),
        out_specs=(rows, P("expert", "dp", None), P("expert", "dp", None)),
        check_vma=False,
    )
```

```python
import functools

import jax
import jax.numpy as jnp
from jax import lax
from jax.experimental import pallas as pl
from jax.experimental.pallas import tpu as pltpu
from jax.sharding import PartitionSpec as P

SIDE = 4
OFFSETS = (0, 1, 3, 2)
SLOTS = 72
BOTH = ("dp", "expert")
TILE = 1024
ROWS = SIDE * SLOTS
WIDE = 3 * ROWS
COLS_LAST = (((1,), (1,)), ((), ()))
ROWS_FIRST = (((0,), (0,)), ((), ()))
VMEM_LIMIT = 58 * 1024 * 1024


def cost(m, k, n):
    return pl.CostEstimate(
        flops=2 * m * k * n, bytes_accessed=2 * (m * k + k * n + m * n), transcendentals=0
    )


HEAVY = pl.CostEstimate(flops=30_000_000_000, bytes_accessed=1, transcendentals=0)
LONGEST = pl.CostEstimate(flops=300_000_000_000, bytes_accessed=1, transcendentals=0)
LIGHT = pl.CostEstimate(flops=1_000_000, bytes_accessed=1, transcendentals=0)
PARAMS = pltpu.CompilerParams(vmem_limit_bytes=VMEM_LIMIT)


def ring(first, shift):
    pairs = []
    for dp in range(8):
        along_x = first == (dp % 2 == 0)
        for y in range(SIDE):
            for x in range(SIDE):
                to = y * SIDE + (x + shift) % SIDE if along_x else ((y + shift) % SIDE) * SIDE + x
                pairs.append((dp * 16 + y * SIDE + x, dp * 16 + to))
    return pairs


def send(value, first, shift):
    shift = shift % SIDE
    return value if shift == 0 else lax.ppermute(value, BOTH, ring(first, shift))


def route_kernel(dest_ref, m0, m1, m2, m3, pick_ref, put_ref, weight_ref):
    rows = lax.broadcasted_iota(jnp.int32, (16, 128), 0)
    masks = jnp.zeros((16, 128), jnp.float32)
    weights = []
    for i, meta in enumerate((m0, m1, m2, m3)):
        packed = meta[...].astype(jnp.float32)
        ids = packed[:, 0:128]
        route = packed[:, 128:256] + packed[:, 256:384] + packed[:, 384:512]
        for j in range(SIDE):
            hit = ids == dest_ref[j].astype(jnp.float32)
            mask = jnp.sum(jnp.where(hit, 1.0, 0.0), axis=0, keepdims=True)
            weights.append(jnp.sum(jnp.where(hit, route, 0.0), axis=0, keepdims=True))
            masks = jnp.where(rows == i * SIDE + j, mask, masks)
    before = lax.broadcasted_iota(jnp.int32, (128, 128), 0) < lax.broadcasted_iota(
        jnp.int32, (128, 128), 1
    )
    rank = jnp.dot(
        masks.astype(jnp.bfloat16),
        before.astype(jnp.float32).astype(jnp.bfloat16),
        preferred_element_type=jnp.float32,
    )
    rank = jnp.where(masks > 0.5, rank, -1.0)
    slot = lax.broadcasted_iota(jnp.int32, (SLOTS, 128), 0).astype(jnp.float32)
    for i in range(SIDE):
        for j in range(SIDE):
            n = i * SIDE + j
            pick = jnp.where(slot == rank[n : n + 1, :], 1.0, 0.0)
            pick_ref[i, j * SLOTS : (j + 1) * SLOTS, :] = pick.astype(jnp.bfloat16)
            put_ref[i, j, :, :] = pick.T.astype(jnp.bfloat16)
            column = jnp.sum(pick * weights[n], axis=1, keepdims=True)
            weight_ref[i, j * SLOTS : (j + 1) * SLOTS, :] = jnp.broadcast_to(column, (SLOTS, 128))


def route(dest, blocks):
    return pl.pallas_call(
        route_kernel,
        out_shape=(
            jax.ShapeDtypeStruct((SIDE, SIDE * SLOTS, 128), jnp.bfloat16),
            jax.ShapeDtypeStruct((SIDE, SIDE, 128, SLOTS), jnp.bfloat16),
            jax.ShapeDtypeStruct((SIDE, SIDE * SLOTS, 128), jnp.float32),
        ),
        grid=(1,),
        in_specs=[pl.BlockSpec(memory_space=pltpu.SMEM)]
        + [pl.BlockSpec((8, 512), lambda c: (16, 0))] * SIDE,
        out_specs=(
            pl.BlockSpec((SIDE, ROWS, 128), lambda c: (0, 0, 0)),
            pl.BlockSpec((SIDE, SIDE, 128, SLOTS), lambda c: (0, 0, 0, 0)),
            pl.BlockSpec((SIDE, ROWS, 128), lambda c: (0, 0, 0)),
        ),
        cost_estimate=LIGHT,
        name="route",
    )(dest, *blocks)


def select_kernel(scaled, pick_ref, weight_ref, b0, b1, b2, b3, o0, o1, o2, o3):
    outs = (o0, o1, o2, o3)
    for i, block in enumerate((b0, b1, b2, b3)):
        rows = jnp.dot(pick_ref[i], block[...], preferred_element_type=jnp.float32)
        if scaled:
            rows = rows * weight_ref[i][:, 0:1]
        rows = rows.astype(jnp.bfloat16)
        for j in range(SIDE):
            outs[j][i, :, :] = rows[j * SLOTS : (j + 1) * SLOTS, :]


def select(pick, weight, blocks, scaled):
    width = blocks[0].shape[1]
    tile = TILE
    return pl.pallas_call(
        functools.partial(select_kernel, scaled),
        out_shape=(jax.ShapeDtypeStruct((SIDE, SLOTS, width), jnp.bfloat16),) * SIDE,
        grid=(width // tile,),
        in_specs=[
            pl.BlockSpec((SIDE, SIDE * SLOTS, 128), lambda c: (0, 0, 0)),
            pl.BlockSpec((SIDE, SIDE * SLOTS, 128), lambda c: (0, 0, 0)),
        ]
        + [pl.BlockSpec((128, tile), lambda c: (0, c))] * SIDE,
        out_specs=(pl.BlockSpec((SIDE, SLOTS, tile), lambda c: (0, 0, c)),) * SIDE,
        compiler_params=PARAMS,
        cost_estimate=HEAVY,
        name="select_scaled" if scaled else "select",
    )(pick, weight, *blocks)


def combine_kernel(put_ref, r0, r1, r2, r3, o0, o1, o2, o3):
    returned = (r0, r1, r2, r3)
    for i, out in enumerate((o0, o1, o2, o3)):
        total = jnp.dot(put_ref[i, 0], r0[i], preferred_element_type=jnp.float32)
        for j in range(1, SIDE):
            total += jnp.dot(put_ref[i, j], returned[j][i], preferred_element_type=jnp.float32)
        out[...] = total.astype(jnp.bfloat16)


def combine(put, returned):
    width = returned[0].shape[2]
    tile = TILE
    return pl.pallas_call(
        combine_kernel,
        out_shape=(jax.ShapeDtypeStruct((128, width), jnp.bfloat16),) * SIDE,
        grid=(width // tile,),
        in_specs=[pl.BlockSpec((SIDE, SIDE, 128, SLOTS), lambda c: (0, 0, 0, 0))]
        + [pl.BlockSpec((SIDE, SLOTS, tile), lambda c: (0, 0, c))] * SIDE,
        out_specs=(pl.BlockSpec((128, tile), lambda c: (0, c)),) * SIDE,
        compiler_params=PARAMS,
        cost_estimate=LIGHT,
        name="combine",
    )(put, *returned)


def dot(a, b, dims=(((1,), (0,)), ((), ()))):
    return lax.dot_general(a, b, dims, preferred_element_type=jnp.float32)


def stacked(refs):
    return jnp.concatenate([r[...] for r in refs], axis=0)


def pre_kernel(*refs):
    xs, up, pre, act = refs[:SIDE], refs[SIDE], *refs[SIDE + 1 :]
    step = pl.program_id(0)
    part = dot(stacked(xs), up[...])

    @pl.when(step == 0)
    def _():
        pre[...] = part

    @pl.when(step > 0)
    def _():
        pre[...] += part

    @pl.when(step == pl.num_programs(0) - 1)
    def _():
        value = pre[...]
        act[...] = (value * jax.nn.sigmoid(value)).T.astype(jnp.bfloat16)


def expert_pre(xs, up):
    width, hidden = up.shape
    return pl.pallas_call(
        pre_kernel,
        out_shape=(
            jax.ShapeDtypeStruct((WIDE + ROWS, hidden), jnp.float32),
            jax.ShapeDtypeStruct((hidden, WIDE + ROWS), jnp.bfloat16),
        ),
        grid=(width // TILE,),
        in_specs=[pl.BlockSpec((ROWS, TILE), lambda c: (0, c))] * SIDE
        + [pl.BlockSpec((TILE, hidden), lambda c: (c, 0))],
        out_specs=(
            pl.BlockSpec((WIDE + ROWS, hidden), lambda c: (0, 0)),
            pl.BlockSpec((hidden, WIDE + ROWS), lambda c: (0, 0)),
        ),
        compiler_params=PARAMS,
        cost_estimate=cost(WIDE + ROWS, width, hidden),
        name="expert_pre",
    )(*xs, up)


def back_kernel(n, *refs):
    gs, pre, down, up, grad, rows, back = refs[:n], *refs[n : n + 4], refs[n + 4 : -1], refs[-1]
    step = pl.program_id(0)
    half = pl.num_programs(0) // 2

    @pl.when(step == 0)
    def _():
        back[...] = dot(stacked(gs), down[...], COLS_LAST)

    @pl.when(jnp.logical_and(step > 0, step < half))
    def _():
        back[...] += dot(stacked(gs), down[...], COLS_LAST)

    @pl.when(step == half - 1)
    def _():
        value = pre[...]
        sigma = jax.nn.sigmoid(value)
        grad[...] = (back[...] * sigma * (1.0 + value * (1.0 - sigma))).astype(jnp.bfloat16)

    @pl.when(step >= half)
    def _():
        out = dot(grad[...], up[...], COLS_LAST).astype(jnp.bfloat16)
        for i in range(n):
            rows[i][...] = out[i * ROWS : (i + 1) * ROWS, :]


def expert_back(gs, pre, place, down, up):
    n, (width, hidden) = len(gs), up.shape
    tiles = width // TILE
    out = pl.pallas_call(
        functools.partial(back_kernel, n),
        out_shape=(jax.ShapeDtypeStruct((n * ROWS, hidden), jnp.bfloat16),)
        + (jax.ShapeDtypeStruct((ROWS, width), jnp.bfloat16),) * n,
        grid=(2 * tiles,),
        in_specs=[pl.BlockSpec((ROWS, TILE), lambda c: (0, jnp.minimum(c, tiles - 1)))] * n
        + [
            pl.BlockSpec((n * ROWS, hidden), lambda c: (place, 0)),
            pl.BlockSpec((hidden, TILE), lambda c: (0, jnp.minimum(c, tiles - 1))),
            pl.BlockSpec((TILE, hidden), lambda c: (jnp.maximum(c - tiles, 0), 0)),
        ],
        out_specs=(pl.BlockSpec((n * ROWS, hidden), lambda c: (0, 0)),)
        + (pl.BlockSpec((ROWS, TILE), lambda c: (0, jnp.maximum(c - tiles, 0))),) * n,
        scratch_shapes=[pltpu.VMEM((n * ROWS, hidden), jnp.float32)],
        compiler_params=PARAMS,
        cost_estimate=cost(2 * n * ROWS, width, hidden) if n > 1 else LIGHT,
        name="expert_back",
    )(*gs, pre, down, up)
    return out[0], list(out[1:])


def up_kernel(x0, x1, x2, x3, grad, grad_last, out):
    total = dot(stacked((x0, x1, x2, x3)), stacked((grad, grad_last)), ROWS_FIRST)
    out[...] = total.astype(jnp.bfloat16)


def up_partial(xs, grads):
    width, hidden = xs[0].shape[1], grads[0].shape[1]
    return pl.pallas_call(
        up_kernel,
        out_shape=jax.ShapeDtypeStruct((width, hidden), jnp.bfloat16),
        grid=(width // TILE,),
        in_specs=[pl.BlockSpec((ROWS, TILE), lambda c: (0, c))] * SIDE
        + [pl.BlockSpec(g.shape, lambda c: (0, 0)) for g in grads],
        out_specs=pl.BlockSpec((TILE, hidden), lambda c: (c, 0)),
        compiler_params=PARAMS,
        cost_estimate=LONGEST,
        name="up_partial",
    )(*xs, *grads)


def down_kernel(act, g0, g1, g2, g3, out):
    out[...] = dot(act[...], stacked((g0, g1, g2, g3))).astype(jnp.bfloat16)


def down_partial(act, gs):
    hidden, rows = act.shape
    width = gs[0].shape[1]
    return pl.pallas_call(
        down_kernel,
        out_shape=jax.ShapeDtypeStruct((hidden, width), jnp.bfloat16),
        grid=(width // TILE,),
        in_specs=[pl.BlockSpec((hidden, rows), lambda c: (0, 0))]
        + [pl.BlockSpec((ROWS, TILE), lambda c: (0, c))] * SIDE,
        out_specs=pl.BlockSpec((hidden, TILE), lambda c: (0, c)),
        compiler_params=PARAMS,
        cost_estimate=LIGHT,
        name="down_partial",
    )(act, *gs)


def after(value, *earlier):
    return lax.optimization_barrier((value, *earlier))[0]


def body(tokens, cotangent, expert_ids, route_weight, up_weight, down_weight):
    width = tokens.shape[1]
    up_matrix = up_weight[0]
    down_matrix = down_weight[0]
    dp = lax.axis_index("dp")
    core = dp & 1
    place = lax.axis_index("expert")
    y, x = place >> 2, place & 3
    shifts = jnp.array(OFFSETS, jnp.int32)
    dest = jnp.where(core == 1, y * SIDE + ((x + shifts) & 3), ((y + shifts) & 3) * SIDE + x)
    high = lax.reduce_precision(route_weight, 8, 7)
    middle = lax.reduce_precision(route_weight - high, 8, 7)
    low = route_weight - high - middle
    meta = jnp.concatenate(
        [m.astype(jnp.bfloat16).T for m in (expert_ids, high, middle, low)], axis=1
    )
    message = jnp.concatenate([tokens, jnp.pad(meta, ((0, 0), (0, width - 512)))], axis=0)

    with jax.named_scope("p1x"):
        token_blocks = [send(message, True, o) for o in OFFSETS]
    cotangent = after(cotangent, *token_blocks)
    with jax.named_scope("p1g"):
        cot_blocks = [send(cotangent, True, o) for o in OFFSETS]
    pick, put, weight = route(dest, token_blocks)

    out_x = select(pick, weight, token_blocks, False)
    with jax.named_scope("p2x"):
        rx = [send(r, False, o).reshape(ROWS, width) for r, o in zip(out_x, OFFSETS)]
    out_g = select(pick, weight, cot_blocks, True)
    with jax.named_scope("p2g"):
        rg = [send(r, False, o).reshape(ROWS, width) for r, o in zip(out_g[:3], OFFSETS)]
    pre, act = expert_pre(rx, up_matrix)
    with jax.named_scope("p2g2"):
        last = send(after(out_g[3], pre, *rx), False, OFFSETS[3]).reshape(ROWS, width)

    grad, rows = expert_back(rg, pre, 0, down_matrix, up_matrix)
    with jax.named_scope("r2"):
        returned = [send(r.reshape(SIDE, SLOTS, width), False, -o) for r, o in zip(rows, OFFSETS)]

    last = after(last, *rows)
    down_part = down_partial(act, [*rg, last])
    down_grad = lax.psum_scatter(down_part, "dp", scatter_dimension=0, tiled=True)
    last = after(last, down_part)
    grad_last, rows_last = expert_back([last], pre, 3, down_matrix, up_matrix)
    with jax.named_scope("r2"):
        rows_last = after(rows_last[0], *returned).reshape(SIDE, SLOTS, width)
        returned.append(send(rows_last, False, -OFFSETS[3]))
    grad_last = after(grad_last, *returned[:3])
    up_part = up_partial(rx, [grad, grad_last])
    up_done, up_part = up_part, after(up_part, down_grad, returned[3])
    up_grad = lax.psum_scatter(up_part, "dp", scatter_dimension=0, tiled=True)

    parts = combine(after(put, up_done), returned)
    with jax.named_scope("r1"):
        parts = [send(p, True, -o) for p, o in zip(parts, OFFSETS)]
    token_grad = sum(p.astype(jnp.float32) for p in parts).astype(jnp.bfloat16)
    token_grad, up_grad = lax.optimization_barrier((token_grad, up_grad))
    return token_grad, up_grad.astype(jnp.float32)[None], down_grad.astype(jnp.float32)[None]


def solution(mesh):
    rows = P(("dp", "expert"), None)
    weights = P("expert", None, None)
    return jax.shard_map(
        body,
        mesh=mesh,
        in_specs=(rows, rows, rows, rows, weights, weights),
        out_specs=(rows, P("expert", "dp", None), P("expert", "dp", None)),
        check_vma=False,
    )
```

```python
import functools

import jax
import jax.numpy as jnp
from jax import lax
from jax.experimental import pallas as pl
from jax.experimental.pallas import tpu as pltpu
from jax.sharding import PartitionSpec as P

SIDE = 4
OFFSETS = (0, 1, 3, 2)
SLOTS = 72
BOTH = ("dp", "expert")
TILE = 1024
ROWS = SIDE * SLOTS
WIDE = 3 * ROWS
COLS_LAST = (((1,), (1,)), ((), ()))
ROWS_FIRST = (((0,), (0,)), ((), ()))
VMEM_LIMIT = 58 * 1024 * 1024


def cost(m, k, n):
    return pl.CostEstimate(
        flops=2 * m * k * n, bytes_accessed=2 * (m * k + k * n + m * n), transcendentals=0
    )


HEAVY = pl.CostEstimate(flops=30_000_000_000, bytes_accessed=1, transcendentals=0)
LONGEST = pl.CostEstimate(flops=300_000_000_000, bytes_accessed=1, transcendentals=0)
LIGHT = pl.CostEstimate(flops=1_000_000, bytes_accessed=1, transcendentals=0)
PARAMS = pltpu.CompilerParams(vmem_limit_bytes=VMEM_LIMIT)


def ring(first, shift):
    pairs = []
    for dp in range(8):
        along_x = first == (dp % 2 == 0)
        for y in range(SIDE):
            for x in range(SIDE):
                to = y * SIDE + (x + shift) % SIDE if along_x else ((y + shift) % SIDE) * SIDE + x
                pairs.append((dp * 16 + y * SIDE + x, dp * 16 + to))
    return pairs


def send(value, first, shift):
    shift = shift % SIDE
    return value if shift == 0 else lax.ppermute(value, BOTH, ring(first, shift))


def route_kernel(dest_ref, m0, m1, m2, m3, pick_ref, put_ref, weight_ref):
    rows = lax.broadcasted_iota(jnp.int32, (16, 128), 0)
    masks = jnp.zeros((16, 128), jnp.float32)
    weights = []
    for i, meta in enumerate((m0, m1, m2, m3)):
        packed = meta[...].astype(jnp.float32)
        ids = packed[:, 0:128]
        route = packed[:, 128:256] + packed[:, 256:384] + packed[:, 384:512]
        for j in range(SIDE):
            hit = ids == dest_ref[j].astype(jnp.float32)
            mask = jnp.sum(jnp.where(hit, 1.0, 0.0), axis=0, keepdims=True)
            weights.append(jnp.sum(jnp.where(hit, route, 0.0), axis=0, keepdims=True))
            masks = jnp.where(rows == i * SIDE + j, mask, masks)
    before = lax.broadcasted_iota(jnp.int32, (128, 128), 0) < lax.broadcasted_iota(
        jnp.int32, (128, 128), 1
    )
    rank = jnp.dot(
        masks.astype(jnp.bfloat16),
        before.astype(jnp.float32).astype(jnp.bfloat16),
        preferred_element_type=jnp.float32,
    )
    rank = jnp.where(masks > 0.5, rank, -1.0)
    slot = lax.broadcasted_iota(jnp.int32, (SLOTS, 128), 0).astype(jnp.float32)
    for i in range(SIDE):
        for j in range(SIDE):
            n = i * SIDE + j
            pick = jnp.where(slot == rank[n : n + 1, :], 1.0, 0.0)
            pick_ref[i, j * SLOTS : (j + 1) * SLOTS, :] = pick.astype(jnp.bfloat16)
            put_ref[i, j, :, :] = pick.T.astype(jnp.bfloat16)
            column = jnp.sum(pick * weights[n], axis=1, keepdims=True)
            weight_ref[i, j * SLOTS : (j + 1) * SLOTS, :] = jnp.broadcast_to(column, (SLOTS, 128))


def route(dest, blocks):
    return pl.pallas_call(
        route_kernel,
        out_shape=(
            jax.ShapeDtypeStruct((SIDE, SIDE * SLOTS, 128), jnp.bfloat16),
            jax.ShapeDtypeStruct((SIDE, SIDE, 128, SLOTS), jnp.bfloat16),
            jax.ShapeDtypeStruct((SIDE, SIDE * SLOTS, 128), jnp.float32),
        ),
        grid=(1,),
        in_specs=[pl.BlockSpec(memory_space=pltpu.SMEM)]
        + [pl.BlockSpec((8, 512), lambda c: (16, 0))] * SIDE,
        out_specs=(
            pl.BlockSpec((SIDE, ROWS, 128), lambda c: (0, 0, 0)),
            pl.BlockSpec((SIDE, SIDE, 128, SLOTS), lambda c: (0, 0, 0, 0)),
            pl.BlockSpec((SIDE, ROWS, 128), lambda c: (0, 0, 0)),
        ),
        cost_estimate=LIGHT,
        name="route",
    )(dest, *blocks)


def select_kernel(scaled, pick_ref, weight_ref, b0, b1, b2, b3, o0, o1, o2, o3):
    outs = (o0, o1, o2, o3)
    for i, block in enumerate((b0, b1, b2, b3)):
        rows = jnp.dot(pick_ref[i], block[...], preferred_element_type=jnp.float32)
        if scaled:
            rows = rows * weight_ref[i][:, 0:1]
        rows = rows.astype(jnp.bfloat16)
        for j in range(SIDE):
            outs[j][i, :, :] = rows[j * SLOTS : (j + 1) * SLOTS, :]


def select(pick, weight, blocks, scaled):
    width = blocks[0].shape[1]
    tile = TILE
    return pl.pallas_call(
        functools.partial(select_kernel, scaled),
        out_shape=(jax.ShapeDtypeStruct((SIDE, SLOTS, width), jnp.bfloat16),) * SIDE,
        grid=(width // tile,),
        in_specs=[
            pl.BlockSpec((SIDE, SIDE * SLOTS, 128), lambda c: (0, 0, 0)),
            pl.BlockSpec((SIDE, SIDE * SLOTS, 128), lambda c: (0, 0, 0)),
        ]
        + [pl.BlockSpec((128, tile), lambda c: (0, c))] * SIDE,
        out_specs=(pl.BlockSpec((SIDE, SLOTS, tile), lambda c: (0, 0, c)),) * SIDE,
        compiler_params=PARAMS,
        cost_estimate=HEAVY,
        name="select_scaled" if scaled else "select",
    )(pick, weight, *blocks)


def combine_kernel(put_ref, r0, r1, r2, r3, o0, o1, o2, o3):
    returned = (r0, r1, r2, r3)
    for i, out in enumerate((o0, o1, o2, o3)):
        total = jnp.dot(put_ref[i, 0], r0[i], preferred_element_type=jnp.float32)
        for j in range(1, SIDE):
            total += jnp.dot(put_ref[i, j], returned[j][i], preferred_element_type=jnp.float32)
        out[...] = total.astype(jnp.bfloat16)


def combine(put, returned):
    width = returned[0].shape[2]
    tile = TILE
    return pl.pallas_call(
        combine_kernel,
        out_shape=(jax.ShapeDtypeStruct((128, width), jnp.bfloat16),) * SIDE,
        grid=(width // tile,),
        in_specs=[pl.BlockSpec((SIDE, SIDE, 128, SLOTS), lambda c: (0, 0, 0, 0))]
        + [pl.BlockSpec((SIDE, SLOTS, tile), lambda c: (0, 0, c))] * SIDE,
        out_specs=(pl.BlockSpec((128, tile), lambda c: (0, c)),) * SIDE,
        compiler_params=PARAMS,
        cost_estimate=LIGHT,
        name="combine",
    )(put, *returned)


def dot(a, b, dims=(((1,), (0,)), ((), ()))):
    return lax.dot_general(a, b, dims, preferred_element_type=jnp.float32)


def stacked(refs):
    return jnp.concatenate([r[...] for r in refs], axis=0)


def pre_kernel(*refs):
    xs, up, pre, act = refs[:SIDE], refs[SIDE], *refs[SIDE + 1 :]
    step = pl.program_id(0)
    part = dot(stacked(xs), up[...])

    @pl.when(step == 0)
    def _():
        pre[...] = part

    @pl.when(step > 0)
    def _():
        pre[...] += part

    @pl.when(step == pl.num_programs(0) - 1)
    def _():
        value = pre[...]
        act[...] = (value * jax.nn.sigmoid(value)).T.astype(jnp.bfloat16)


def expert_pre(xs, up):
    width, hidden = up.shape
    return pl.pallas_call(
        pre_kernel,
        out_shape=(
            jax.ShapeDtypeStruct((WIDE + ROWS, hidden), jnp.float32),
            jax.ShapeDtypeStruct((hidden, WIDE + ROWS), jnp.bfloat16),
        ),
        grid=(width // TILE,),
        in_specs=[pl.BlockSpec((ROWS, TILE), lambda c: (0, c))] * SIDE
        + [pl.BlockSpec((TILE, hidden), lambda c: (c, 0))],
        out_specs=(
            pl.BlockSpec((WIDE + ROWS, hidden), lambda c: (0, 0)),
            pl.BlockSpec((hidden, WIDE + ROWS), lambda c: (0, 0)),
        ),
        compiler_params=PARAMS,
        cost_estimate=cost(WIDE + ROWS, width, hidden),
        name="expert_pre",
    )(*xs, up)


def back_kernel(n, *refs):
    gs, pre, down, up, grad, rows, back = refs[:n], *refs[n : n + 4], refs[n + 4 : -1], refs[-1]
    step = pl.program_id(0)
    half = pl.num_programs(0) // 2

    @pl.when(step == 0)
    def _():
        back[...] = dot(stacked(gs), down[...], COLS_LAST)

    @pl.when(jnp.logical_and(step > 0, step < half))
    def _():
        back[...] += dot(stacked(gs), down[...], COLS_LAST)

    @pl.when(step == half - 1)
    def _():
        value = pre[...]
        sigma = jax.nn.sigmoid(value)
        grad[...] = (back[...] * sigma * (1.0 + value * (1.0 - sigma))).astype(jnp.bfloat16)

    @pl.when(step >= half)
    def _():
        out = dot(grad[...], up[...], COLS_LAST).astype(jnp.bfloat16)
        for i in range(n):
            rows[i][...] = out[i * ROWS : (i + 1) * ROWS, :]


def expert_back(gs, pre, place, down, up):
    n, (width, hidden) = len(gs), up.shape
    tiles = width // TILE
    out = pl.pallas_call(
        functools.partial(back_kernel, n),
        out_shape=(jax.ShapeDtypeStruct((n * ROWS, hidden), jnp.bfloat16),)
        + (jax.ShapeDtypeStruct((ROWS, width), jnp.bfloat16),) * n,
        grid=(2 * tiles,),
        in_specs=[pl.BlockSpec((ROWS, TILE), lambda c: (0, jnp.minimum(c, tiles - 1)))] * n
        + [
            pl.BlockSpec((n * ROWS, hidden), lambda c: (place, 0)),
            pl.BlockSpec((hidden, TILE), lambda c: (0, jnp.minimum(c, tiles - 1))),
            pl.BlockSpec((TILE, hidden), lambda c: (jnp.maximum(c - tiles, 0), 0)),
        ],
        out_specs=(pl.BlockSpec((n * ROWS, hidden), lambda c: (0, 0)),)
        + (pl.BlockSpec((ROWS, TILE), lambda c: (0, jnp.maximum(c - tiles, 0))),) * n,
        scratch_shapes=[pltpu.VMEM((n * ROWS, hidden), jnp.float32)],
        compiler_params=PARAMS,
        cost_estimate=cost(2 * n * ROWS, width, hidden) if n > 1 else LIGHT,
        name="expert_back",
    )(*gs, pre, down, up)
    return out[0], list(out[1:])


def up_kernel(x0, x1, x2, x3, p0, p1, p2, out):
    total = dot(stacked((x0, x1, x2, x3)), stacked((p0, p1, p2)), ROWS_FIRST)
    out[...] = total.astype(jnp.bfloat16)


def up_partial(xs, grads):
    width, hidden = xs[0].shape[1], grads[0].shape[1]
    return pl.pallas_call(
        up_kernel,
        out_shape=jax.ShapeDtypeStruct((width, hidden), jnp.bfloat16),
        grid=(width // TILE,),
        in_specs=[pl.BlockSpec((ROWS, TILE), lambda c: (0, c))] * SIDE
        + [pl.BlockSpec(g.shape, lambda c: (0, 0)) for g in grads],
        out_specs=pl.BlockSpec((TILE, hidden), lambda c: (c, 0)),
        compiler_params=PARAMS,
        cost_estimate=LONGEST,
        name="up_partial",
    )(*xs, *grads)


def down_kernel(act, g0, g1, g2, g3, out):
    out[...] = dot(act[...], stacked((g0, g1, g2, g3))).astype(jnp.bfloat16)


def down_partial(act, gs):
    hidden, rows = act.shape
    width = gs[0].shape[1]
    return pl.pallas_call(
        down_kernel,
        out_shape=jax.ShapeDtypeStruct((hidden, width), jnp.bfloat16),
        grid=(width // TILE,),
        in_specs=[pl.BlockSpec((hidden, rows), lambda c: (0, 0))]
        + [pl.BlockSpec((ROWS, TILE), lambda c: (0, c))] * SIDE,
        out_specs=pl.BlockSpec((hidden, TILE), lambda c: (0, c)),
        compiler_params=PARAMS,
        cost_estimate=LIGHT,
        name="down_partial",
    )(act, *gs)


def after(value, *earlier):
    return lax.optimization_barrier((value, *earlier))[0]


def body(tokens, cotangent, expert_ids, route_weight, up_weight, down_weight):
    width = tokens.shape[1]
    up_matrix = up_weight[0]
    down_matrix = down_weight[0]
    dp = lax.axis_index("dp")
    core = dp & 1
    place = lax.axis_index("expert")
    y, x = place >> 2, place & 3
    shifts = jnp.array(OFFSETS, jnp.int32)
    dest = jnp.where(core == 1, y * SIDE + ((x + shifts) & 3), ((y + shifts) & 3) * SIDE + x)
    high = lax.reduce_precision(route_weight, 8, 7)
    middle = lax.reduce_precision(route_weight - high, 8, 7)
    low = route_weight - high - middle
    meta = jnp.concatenate(
        [m.astype(jnp.bfloat16).T for m in (expert_ids, high, middle, low)], axis=1
    )
    message = jnp.concatenate([tokens, jnp.pad(meta, ((0, 0), (0, width - 512)))], axis=0)

    with jax.named_scope("p1x"):
        token_blocks = [send(message, True, o) for o in OFFSETS]
    cotangent = after(cotangent, *token_blocks)
    with jax.named_scope("p1g"):
        cot_blocks = [send(cotangent, True, o) for o in OFFSETS]
    pick, put, weight = route(dest, token_blocks)

    out_x = select(pick, weight, token_blocks, False)
    with jax.named_scope("p2x"):
        rx = [send(r, False, o).reshape(ROWS, width) for r, o in zip(out_x, OFFSETS)]
    out_g = select(pick, weight, cot_blocks, True)
    with jax.named_scope("p2g"):
        rg = [send(r, False, o).reshape(ROWS, width) for r, o in zip(out_g[:3], OFFSETS)]
    rx = [rx[1], rx[2], rx[0], rx[3]]
    pre, act = expert_pre(rx, up_matrix)
    with jax.named_scope("p2g2"):
        last = send(after(out_g[3], pre, *rx), False, OFFSETS[3]).reshape(ROWS, width)

    grad_own, (rows_own,) = expert_back([rg[0]], pre, 2, down_matrix, up_matrix)
    rg = [after(rg[1], rows_own), rg[2], rg[0]]
    grad, rows = expert_back(rg[:2], pre, 0, down_matrix, up_matrix)
    rows = [rows_own, *rows]
    with jax.named_scope("r2"):
        returned = [send(r.reshape(SIDE, SLOTS, width), False, -o) for r, o in zip(rows, OFFSETS)]

    last = after(last, *rows)
    down_part = down_partial(act, [*rg, last])
    down_grad = lax.psum_scatter(down_part, "dp", scatter_dimension=0, tiled=True)
    last = after(last, down_part)
    grad_last, rows_last = expert_back([last], pre, 3, down_matrix, up_matrix)
    with jax.named_scope("r2"):
        rows_last = after(rows_last[0], *returned).reshape(SIDE, SLOTS, width)
        returned.append(send(rows_last, False, -OFFSETS[3]))
    grad_last = after(grad_last, *returned[:3])
    up_part = up_partial(rx, [grad, grad_own, grad_last])
    up_done, up_part = up_part, after(up_part, down_grad, returned[3])
    up_grad = lax.psum_scatter(up_part, "dp", scatter_dimension=0, tiled=True)

    parts = combine(after(put, up_done), returned)
    with jax.named_scope("r1"):
        parts = [send(p, True, -o) for p, o in zip(parts, OFFSETS)]
    token_grad = sum(p.astype(jnp.float32) for p in parts).astype(jnp.bfloat16)
    token_grad, up_grad = lax.optimization_barrier((token_grad, up_grad))
    return token_grad, up_grad.astype(jnp.float32)[None], down_grad.astype(jnp.float32)[None]


def solution(mesh):
    rows = P(("dp", "expert"), None)
    weights = P("expert", None, None)
    return jax.shard_map(
        body,
        mesh=mesh,
        in_specs=(rows, rows, rows, rows, weights, weights),
        out_specs=(rows, P("expert", "dp", None), P("expert", "dp", None)),
        check_vma=False,
    )
```

```python
import functools

import jax
import jax.numpy as jnp
from jax import lax
from jax.experimental import pallas as pl
from jax.experimental.pallas import tpu as pltpu
from jax.sharding import PartitionSpec as P

SIDE = 4
OFFSETS = (0, 1, 3, 2)
SLOTS = 72
BOTH = ("dp", "expert")
TILE = 1024
ROWS = SIDE * SLOTS
WIDE = 3 * ROWS
COLS_LAST = (((1,), (1,)), ((), ()))
ROWS_FIRST = (((0,), (0,)), ((), ()))
VMEM_LIMIT = 58 * 1024 * 1024


def cost(m, k, n):
    return pl.CostEstimate(
        flops=2 * m * k * n, bytes_accessed=2 * (m * k + k * n + m * n), transcendentals=0
    )


HEAVY = pl.CostEstimate(flops=30_000_000_000, bytes_accessed=1, transcendentals=0)
LONGEST = pl.CostEstimate(flops=300_000_000_000, bytes_accessed=1, transcendentals=0)
LIGHT = pl.CostEstimate(flops=1_000_000, bytes_accessed=1, transcendentals=0)
PARAMS = pltpu.CompilerParams(vmem_limit_bytes=VMEM_LIMIT)


def ring(first, shift):
    pairs = []
    for dp in range(8):
        along_x = first == (dp % 2 == 0)
        for y in range(SIDE):
            for x in range(SIDE):
                to = y * SIDE + (x + shift) % SIDE if along_x else ((y + shift) % SIDE) * SIDE + x
                pairs.append((dp * 16 + y * SIDE + x, dp * 16 + to))
    return pairs


def send(value, first, shift):
    shift = shift % SIDE
    return value if shift == 0 else lax.ppermute(value, BOTH, ring(first, shift))


def route_kernel(dest_ref, m0, m1, m2, m3, pick_ref, put_ref, weight_ref):
    rows = lax.broadcasted_iota(jnp.int32, (16, 128), 0)
    masks = jnp.zeros((16, 128), jnp.float32)
    weights = []
    for i, meta in enumerate((m0, m1, m2, m3)):
        packed = meta[...].astype(jnp.float32)
        ids = packed[:, 0:128]
        route = packed[:, 128:256] + packed[:, 256:384] + packed[:, 384:512]
        for j in range(SIDE):
            hit = ids == dest_ref[j].astype(jnp.float32)
            mask = jnp.sum(jnp.where(hit, 1.0, 0.0), axis=0, keepdims=True)
            weights.append(jnp.sum(jnp.where(hit, route, 0.0), axis=0, keepdims=True))
            masks = jnp.where(rows == i * SIDE + j, mask, masks)
    before = lax.broadcasted_iota(jnp.int32, (128, 128), 0) < lax.broadcasted_iota(
        jnp.int32, (128, 128), 1
    )
    rank = jnp.dot(
        masks.astype(jnp.bfloat16),
        before.astype(jnp.float32).astype(jnp.bfloat16),
        preferred_element_type=jnp.float32,
    )
    rank = jnp.where(masks > 0.5, rank, -1.0)
    slot = lax.broadcasted_iota(jnp.int32, (SLOTS, 128), 0).astype(jnp.float32)
    for i in range(SIDE):
        for j in range(SIDE):
            n = i * SIDE + j
            pick = jnp.where(slot == rank[n : n + 1, :], 1.0, 0.0)
            pick_ref[i, j * SLOTS : (j + 1) * SLOTS, :] = pick.astype(jnp.bfloat16)
            put_ref[i, j, :, :] = pick.T.astype(jnp.bfloat16)
            column = jnp.sum(pick * weights[n], axis=1, keepdims=True)
            weight_ref[i, j * SLOTS : (j + 1) * SLOTS, :] = jnp.broadcast_to(column, (SLOTS, 128))


def route(dest, blocks):
    return pl.pallas_call(
        route_kernel,
        out_shape=(
            jax.ShapeDtypeStruct((SIDE, SIDE * SLOTS, 128), jnp.bfloat16),
            jax.ShapeDtypeStruct((SIDE, SIDE, 128, SLOTS), jnp.bfloat16),
            jax.ShapeDtypeStruct((SIDE, SIDE * SLOTS, 128), jnp.float32),
        ),
        grid=(1,),
        in_specs=[pl.BlockSpec(memory_space=pltpu.SMEM)]
        + [pl.BlockSpec((8, 512), lambda c: (16, 0))] * SIDE,
        out_specs=(
            pl.BlockSpec((SIDE, ROWS, 128), lambda c: (0, 0, 0)),
            pl.BlockSpec((SIDE, SIDE, 128, SLOTS), lambda c: (0, 0, 0, 0)),
            pl.BlockSpec((SIDE, ROWS, 128), lambda c: (0, 0, 0)),
        ),
        cost_estimate=LIGHT,
        name="route",
    )(dest, *blocks)


def select_kernel(scaled, pick_ref, weight_ref, b0, b1, b2, b3, o0, o1, o2, o3):
    outs = (o0, o1, o2, o3)
    for i, block in enumerate((b0, b1, b2, b3)):
        rows = jnp.dot(pick_ref[i], block[...], preferred_element_type=jnp.float32)
        if scaled:
            rows = rows * weight_ref[i][:, 0:1]
        rows = rows.astype(jnp.bfloat16)
        for j in range(SIDE):
            outs[j][i, :, :] = rows[j * SLOTS : (j + 1) * SLOTS, :]


def select(pick, weight, blocks, scaled):
    width = blocks[0].shape[1]
    tile = TILE
    return pl.pallas_call(
        functools.partial(select_kernel, scaled),
        out_shape=(jax.ShapeDtypeStruct((SIDE, SLOTS, width), jnp.bfloat16),) * SIDE,
        grid=(width // tile,),
        in_specs=[
            pl.BlockSpec((SIDE, SIDE * SLOTS, 128), lambda c: (0, 0, 0)),
            pl.BlockSpec((SIDE, SIDE * SLOTS, 128), lambda c: (0, 0, 0)),
        ]
        + [pl.BlockSpec((128, tile), lambda c: (0, c))] * SIDE,
        out_specs=(pl.BlockSpec((SIDE, SLOTS, tile), lambda c: (0, 0, c)),) * SIDE,
        compiler_params=PARAMS,
        cost_estimate=HEAVY,
        name="select_scaled" if scaled else "select",
    )(pick, weight, *blocks)


def combine_kernel(put_ref, r0, r1, r2, r3, o0, o1, o2, o3):
    returned = (r0, r1, r2, r3)
    for i, out in enumerate((o0, o1, o2, o3)):
        total = jnp.dot(put_ref[i, 0], r0[i], preferred_element_type=jnp.float32)
        for j in range(1, SIDE):
            total += jnp.dot(put_ref[i, j], returned[j][i], preferred_element_type=jnp.float32)
        out[...] = total.astype(jnp.bfloat16)


def combine(put, returned):
    width = returned[0].shape[2]
    tile = TILE
    return pl.pallas_call(
        combine_kernel,
        out_shape=(jax.ShapeDtypeStruct((128, width), jnp.bfloat16),) * SIDE,
        grid=(width // tile,),
        in_specs=[pl.BlockSpec((SIDE, SIDE, 128, SLOTS), lambda c: (0, 0, 0, 0))]
        + [pl.BlockSpec((SIDE, SLOTS, tile), lambda c: (0, 0, c))] * SIDE,
        out_specs=(pl.BlockSpec((128, tile), lambda c: (0, c)),) * SIDE,
        compiler_params=PARAMS,
        cost_estimate=LIGHT,
        name="combine",
    )(put, *returned)


def dot(a, b, dims=(((1,), (0,)), ((), ()))):
    return lax.dot_general(a, b, dims, preferred_element_type=jnp.float32)


def stacked(refs):
    return jnp.concatenate([r[...] for r in refs], axis=0)


def pre_kernel(*refs):
    xs, up, pre, act = refs[:SIDE], refs[SIDE], *refs[SIDE + 1 :]
    step = pl.program_id(0)
    part = dot(stacked(xs), up[...])

    @pl.when(step == 0)
    def _():
        pre[...] = part

    @pl.when(step > 0)
    def _():
        pre[...] += part

    @pl.when(step == pl.num_programs(0) - 1)
    def _():
        value = pre[...]
        act[...] = (value * jax.nn.sigmoid(value)).T.astype(jnp.bfloat16)


def expert_pre(xs, up):
    width, hidden = up.shape
    return pl.pallas_call(
        pre_kernel,
        out_shape=(
            jax.ShapeDtypeStruct((WIDE + ROWS, hidden), jnp.float32),
            jax.ShapeDtypeStruct((hidden, WIDE + ROWS), jnp.bfloat16),
        ),
        grid=(width // TILE,),
        in_specs=[pl.BlockSpec((ROWS, TILE), lambda c: (0, c))] * SIDE
        + [pl.BlockSpec((TILE, hidden), lambda c: (c, 0))],
        out_specs=(
            pl.BlockSpec((WIDE + ROWS, hidden), lambda c: (0, 0)),
            pl.BlockSpec((hidden, WIDE + ROWS), lambda c: (0, 0)),
        ),
        compiler_params=PARAMS,
        cost_estimate=cost(WIDE + ROWS, width, hidden),
        name="expert_pre",
    )(*xs, up)


def back_kernel(n, *refs):
    gs, pre, down, up, grad, rows, back = refs[:n], *refs[n : n + 4], refs[n + 4 : -1], refs[-1]
    step = pl.program_id(0)
    half = pl.num_programs(0) // 2

    @pl.when(step == 0)
    def _():
        back[...] = dot(stacked(gs), down[...], COLS_LAST)

    @pl.when(jnp.logical_and(step > 0, step < half))
    def _():
        back[...] += dot(stacked(gs), down[...], COLS_LAST)

    @pl.when(step == half - 1)
    def _():
        value = pre[...]
        sigma = jax.nn.sigmoid(value)
        grad[...] = (back[...] * sigma * (1.0 + value * (1.0 - sigma))).astype(jnp.bfloat16)

    @pl.when(step >= half)
    def _():
        out = dot(grad[...], up[...], COLS_LAST).astype(jnp.bfloat16)
        for i in range(n):
            rows[i][...] = out[i * ROWS : (i + 1) * ROWS, :]


def expert_back(gs, pre, place, down, up):
    n, (width, hidden) = len(gs), up.shape
    tile = 2 * TILE
    tiles = width // tile
    out = pl.pallas_call(
        functools.partial(back_kernel, n),
        out_shape=(jax.ShapeDtypeStruct((n * ROWS, hidden), jnp.bfloat16),)
        + (jax.ShapeDtypeStruct((ROWS, width), jnp.bfloat16),) * n,
        grid=(2 * tiles,),
        in_specs=[pl.BlockSpec((ROWS, tile), lambda c: (0, jnp.minimum(c, tiles - 1)))] * n
        + [
            pl.BlockSpec((n * ROWS, hidden), lambda c: (place, 0)),
            pl.BlockSpec((hidden, tile), lambda c: (0, jnp.minimum(c, tiles - 1))),
            pl.BlockSpec((tile, hidden), lambda c: (jnp.maximum(c - tiles, 0), 0)),
        ],
        out_specs=(pl.BlockSpec((n * ROWS, hidden), lambda c: (0, 0)),)
        + (pl.BlockSpec((ROWS, tile), lambda c: (0, jnp.maximum(c - tiles, 0))),) * n,
        scratch_shapes=[pltpu.VMEM((n * ROWS, hidden), jnp.float32)],
        compiler_params=PARAMS,
        cost_estimate=cost(2 * n * ROWS, width, hidden) if n > 1 else LIGHT,
        name="expert_back",
    )(*gs, pre, down, up)
    return out[0], list(out[1:])


def up_kernel(x0, x1, x2, x3, p0, p1, p2, out):
    total = dot(stacked((x0, x1, x2, x3)), stacked((p0, p1, p2)), ROWS_FIRST)
    out[...] = total.astype(jnp.bfloat16)


def up_partial(xs, grads):
    width, hidden = xs[0].shape[1], grads[0].shape[1]
    return pl.pallas_call(
        up_kernel,
        out_shape=jax.ShapeDtypeStruct((width, hidden), jnp.bfloat16),
        grid=(width // TILE,),
        in_specs=[pl.BlockSpec((ROWS, TILE), lambda c: (0, c))] * SIDE
        + [pl.BlockSpec(g.shape, lambda c: (0, 0)) for g in grads],
        out_specs=pl.BlockSpec((TILE, hidden), lambda c: (c, 0)),
        compiler_params=PARAMS,
        cost_estimate=LONGEST,
        name="up_partial",
    )(*xs, *grads)


def down_kernel(act, g0, g1, g2, g3, out):
    out[...] = dot(act[...], stacked((g0, g1, g2, g3))).astype(jnp.bfloat16)


def down_partial(act, gs):
    hidden, rows = act.shape
    width = gs[0].shape[1]
    return pl.pallas_call(
        down_kernel,
        out_shape=jax.ShapeDtypeStruct((hidden, width), jnp.bfloat16),
        grid=(width // TILE,),
        in_specs=[pl.BlockSpec((hidden, rows), lambda c: (0, 0))]
        + [pl.BlockSpec((ROWS, TILE), lambda c: (0, c))] * SIDE,
        out_specs=pl.BlockSpec((hidden, TILE), lambda c: (0, c)),
        compiler_params=PARAMS,
        cost_estimate=LIGHT,
        name="down_partial",
    )(act, *gs)


def after(value, *earlier):
    return lax.optimization_barrier((value, *earlier))[0]


def body(tokens, cotangent, expert_ids, route_weight, up_weight, down_weight):
    width = tokens.shape[1]
    up_matrix = up_weight[0]
    down_matrix = down_weight[0]
    dp = lax.axis_index("dp")
    core = dp & 1
    place = lax.axis_index("expert")
    y, x = place >> 2, place & 3
    shifts = jnp.array(OFFSETS, jnp.int32)
    dest = jnp.where(core == 1, y * SIDE + ((x + shifts) & 3), ((y + shifts) & 3) * SIDE + x)
    high = lax.reduce_precision(route_weight, 8, 7)
    middle = lax.reduce_precision(route_weight - high, 8, 7)
    low = route_weight - high - middle
    meta = jnp.concatenate(
        [m.astype(jnp.bfloat16).T for m in (expert_ids, high, middle, low)], axis=1
    )
    message = jnp.concatenate([tokens, jnp.pad(meta, ((0, 0), (0, width - 512)))], axis=0)

    with jax.named_scope("p1x"):
        token_blocks = [send(message, True, o) for o in OFFSETS]
    cotangent = after(cotangent, *token_blocks)
    with jax.named_scope("p1g"):
        cot_blocks = [send(cotangent, True, o) for o in OFFSETS]
    pick, put, weight = route(dest, token_blocks)

    out_x = select(pick, weight, token_blocks, False)
    with jax.named_scope("p2x"):
        rx = [send(r, False, o).reshape(ROWS, width) for r, o in zip(out_x, OFFSETS)]
    out_g = select(pick, weight, cot_blocks, True)
    with jax.named_scope("p2g"):
        rg = [send(r, False, o).reshape(ROWS, width) for r, o in zip(out_g[:3], OFFSETS)]
    rx = [rx[1], rx[2], rx[0], rx[3]]
    pre, act = expert_pre(rx, up_matrix)
    with jax.named_scope("p2g2"):
        last = send(after(out_g[3], pre, *rx), False, OFFSETS[3]).reshape(ROWS, width)

    grad_own, (rows_own,) = expert_back([rg[0]], pre, 2, down_matrix, up_matrix)
    rg = [after(rg[1], rows_own), rg[2], rg[0]]
    grad, rows = expert_back(rg[:2], pre, 0, down_matrix, up_matrix)
    rows = [rows_own, *rows]
    with jax.named_scope("r2"):
        returned = [send(r.reshape(SIDE, SLOTS, width), False, -o) for r, o in zip(rows, OFFSETS)]

    last = after(last, *rows)
    down_part = down_partial(act, [*rg, last])
    down_grad = lax.psum_scatter(down_part, "dp", scatter_dimension=0, tiled=True)
    last = after(last, down_part)
    grad_last, rows_last = expert_back([last], pre, 3, down_matrix, up_matrix)
    with jax.named_scope("r2"):
        rows_last = after(rows_last[0], *returned).reshape(SIDE, SLOTS, width)
        returned.append(send(rows_last, False, -OFFSETS[3]))
    grad_last = after(grad_last, *returned[:3])
    up_part = up_partial(rx, [grad, grad_own, grad_last])
    up_done, up_part = up_part, after(up_part, down_grad, returned[3])
    up_grad = lax.psum_scatter(up_part, "dp", scatter_dimension=0, tiled=True)

    parts = combine(after(put, up_done), returned)
    with jax.named_scope("r1"):
        parts = [send(p, True, -o) for p, o in zip(parts, OFFSETS)]
    token_grad = sum(p.astype(jnp.float32) for p in parts).astype(jnp.bfloat16)
    token_grad, up_grad = lax.optimization_barrier((token_grad, up_grad))
    return token_grad, up_grad.astype(jnp.float32)[None], down_grad.astype(jnp.float32)[None]


def solution(mesh):
    rows = P(("dp", "expert"), None)
    weights = P("expert", None, None)
    return jax.shard_map(
        body,
        mesh=mesh,
        in_specs=(rows, rows, rows, rows, weights, weights),
        out_specs=(rows, P("expert", "dp", None), P("expert", "dp", None)),
        check_vma=False,
    )
```
